256 devices in a mesh: seq: 64 (over y, z, core), head: 4 (over x).
Axes of the slice: x: 4, y: 4, z: 8, core: 2. Of those that a mesh axis runs over, the one named last changes fastest.
Arguments:
- queries: bfloat16 [32768, 3584], P(('seq', 'head')), may hold values from -256 to 256
- rotated_key_rows: bfloat16 [32768, 512], P(('seq', 'head')), may hold values from -5 to 5
- value_matrix: bfloat16 [32768, 512], P(('seq', 'head')), may hold values from -6 to 6
- cotangent: bfloat16 [32768, 3584], P(('seq', 'head')), may hold values from -6 to 6
- tree_mask: int32 [256, 4], P('seq'), may hold values from 0 to 1, as said below
Outputs:
- attention: bfloat16 [32768, 3584], P(('seq', 'head'))
- query_grad: bfloat16 [32768, 3584], P(('seq', 'head'))
- key_gradient: bfloat16 [32768, 512], P(('seq', 'head'))
- value_gradient: bfloat16 [32768, 512], P(('seq', 'head'))
The draws below stay inside these ranges and needn't reach their ends.
Inputs may be any that keep to these rules, and one draw needn't show every extreme that they name: `tree_mask`: rows of the prompt's 4 blocks are 0. All blocks of one response share one row: 1 on its first r columns and 0 after, with r from 1 to 4; the first response reads all 4 prompt blocks.
All inputs are finite; a program needn't handle non-finite values.
Results may differ from the reference program's by a relative error of at most 0.034.
Values may be sent and summed in bfloat16 or wider, within the bound.
A program may use at most 128 MiB of HBM per device.

```python
import jax
import jax.numpy as jnp
from jax import lax

QUERY_HEADS = 28
KEY_VALUE_HEADS = 4
HEAD_SIZE = 128
SEQUENCE_TOKENS = 512
MASK_BLOCK_SIZE = 128
TREE_TOKENS = 32768
NBLK = 256
PBLK = 4
QUERY_PER_KEY = 7
N_SEQ = 64


def drawn_pair(key):
    base = jax.random.fold_in(key, 17)
    query_key, random_key_seed = jax.random.split(base, 2)
    queries = jnp.clip(jax.random.normal(query_key, (TREE_TOKENS, QUERY_HEADS * HEAD_SIZE), jnp.float32), -4.0, 4.0)
    rotated_key_rows = jnp.clip(jax.random.normal(random_key_seed, (TREE_TOKENS, KEY_VALUE_HEADS * HEAD_SIZE), jnp.float32), -4.0, 4.0)
    return (queries, rotated_key_rows)


def draw_queries(key, part):
    return drawn_pair(key)[0].astype(jnp.bfloat16)


def draw_rotated_key_rows(key, part):
    return drawn_pair(key)[1].astype(jnp.bfloat16)


def draw_tree_mask(key, part):
    segments = NBLK // PBLK
    reach = jax.random.randint(jax.random.fold_in(key, 29), (segments,), 1, PBLK + 1)
    reach = jnp.where(jnp.arange(segments) == 1, PBLK, reach)
    block_segment = jnp.arange(NBLK) // PBLK
    columns = jnp.arange(PBLK)
    reads = (columns[None, :] < reach[block_segment][:, None]) & (block_segment[:, None] > 0)
    return reads.astype(jnp.int32)


def block_levels(stream_key, extent, shards, smallest, high):
    gain = 1.0
    for position, blocks in shards:
        draws = jax.random.uniform(jax.random.fold_in(jax.random.fold_in(stream_key, 6), position), (blocks,), jnp.float32, smallest / len(shards), high / len(shards))
        gain = gain * jnp.repeat(jnp.exp(draws), extent[position] // blocks).reshape((-1,) + (1,) * (len(extent) - 1 - position))
    return gain


def scatter_about(rng, shape, spread, most, pieces=(), held_as=jnp.bfloat16):
    gain = block_levels(rng, shape, pieces, -0.22, 0.18) if pieces else 1.0
    entries = jax.random.normal(rng, shape, jnp.float32) * spread * gain
    return jnp.minimum(jnp.maximum(entries, -most), most).astype(held_as)


def setup_inputs(seed: int = 0) -> dict:
    key_of = jax.random.split(jax.random.key(seed), 6)
    return {
        "queries": draw_queries(jax.random.fold_in(key_of[5], 71), 0),
        "rotated_key_rows": draw_rotated_key_rows(jax.random.fold_in(key_of[5], 71), 0),
        "value_matrix": scatter_about(key_of[2], (TREE_TOKENS, KEY_VALUE_HEADS * HEAD_SIZE), 1.0, 6.0, ((0, 256),)),
        "cotangent": scatter_about(key_of[3], (TREE_TOKENS, QUERY_HEADS * HEAD_SIZE), 1.0, 6.0, ((0, 256),)),
        "tree_mask": draw_tree_mask(jax.random.fold_in(key_of[5], 71), 0),
    }


def segment_terms(segment, queries, rotated_key_rows, value_matrix, cotangent, tree_mask):
    start_row = segment * SEQUENCE_TOKENS
    query_head_count = lax.dynamic_slice_in_dim(queries, start_row, SEQUENCE_TOKENS, 0).astype(jnp.float32).reshape(SEQUENCE_TOKENS, KEY_VALUE_HEADS, QUERY_PER_KEY, HEAD_SIZE)
    head_cotangents = lax.dynamic_slice_in_dim(cotangent, start_row, SEQUENCE_TOKENS, 0).astype(jnp.float32).reshape(SEQUENCE_TOKENS, KEY_VALUE_HEADS, QUERY_PER_KEY, HEAD_SIZE)
    response_keys = lax.dynamic_slice_in_dim(rotated_key_rows, start_row, SEQUENCE_TOKENS, 0)
    response_values = lax.dynamic_slice_in_dim(value_matrix, start_row, SEQUENCE_TOKENS, 0)
    block_keys = jnp.concatenate([rotated_key_rows[:SEQUENCE_TOKENS], response_keys], 0).astype(jnp.float32).reshape(2 * SEQUENCE_TOKENS, KEY_VALUE_HEADS, HEAD_SIZE)
    block_values = jnp.concatenate([value_matrix[:SEQUENCE_TOKENS], response_values], 0).astype(jnp.float32).reshape(2 * SEQUENCE_TOKENS, KEY_VALUE_HEADS, HEAD_SIZE)
    mask_rows = lax.dynamic_slice(tree_mask, (segment * PBLK, jnp.int32(0)), (PBLK, PBLK))
    token_mask = jnp.repeat(jnp.repeat(mask_rows, MASK_BLOCK_SIZE, axis=0), MASK_BLOCK_SIZE, axis=1)
    prompt_reads = (token_mask > 0) & (segment > 0)
    positions = jnp.arange(SEQUENCE_TOKENS, dtype=jnp.int32)
    causal = positions[None, :] <= positions[:, None]
    allowed = jnp.concatenate([prompt_reads, causal], 1)
    score_scale = HEAD_SIZE ** -0.5
    scores = jnp.einsum("tjgd,ujd->jgtu", query_head_count, block_keys) * score_scale
    scores = jnp.where(allowed, scores, jnp.float32(-1e30))
    row_max = jnp.max(scores, axis=-1, keepdims=True)
    weights = jnp.where(allowed, jnp.exp(scores - row_max), jnp.float32(0.0))
    softmax_probs = weights / jnp.sum(weights, axis=-1, keepdims=True)
    rounded_probs = softmax_probs.astype(jnp.bfloat16).astype(jnp.float32)
    attention = jnp.einsum("jgtu,ujd->tjgd", rounded_probs, block_values).astype(jnp.bfloat16)
    out_delta = jnp.sum(head_cotangents * attention.astype(jnp.float32), axis=-1)
    out_delta = jnp.transpose(out_delta, (1, 2, 0))[..., None]
    dprob = jnp.einsum("tjgd,ujd->jgtu", head_cotangents, block_values)
    dscore = (softmax_probs * (dprob - out_delta)).astype(jnp.bfloat16).astype(jnp.float32)
    query_grad = (jnp.einsum("jgtu,ujd->tjgd", dscore, block_keys) * score_scale).astype(jnp.bfloat16)
    key_terms = jnp.einsum("jgtu,tjgd->ujd", dscore, query_head_count) * score_scale
    value_terms = jnp.einsum("jgtu,tjgd->ujd", rounded_probs, head_cotangents)
    return (attention.reshape(SEQUENCE_TOKENS, QUERY_HEADS * HEAD_SIZE), query_grad.reshape(SEQUENCE_TOKENS, QUERY_HEADS * HEAD_SIZE),
            key_terms[:SEQUENCE_TOKENS], value_terms[:SEQUENCE_TOKENS], key_terms[SEQUENCE_TOKENS:], value_terms[SEQUENCE_TOKENS:])


def reference(queries, rotated_key_rows, value_matrix, cotangent, tree_mask):
    def one_segment(segment):
        return segment_terms(segment, queries, rotated_key_rows, value_matrix, cotangent, tree_mask)

    result_list = lax.map(one_segment, jnp.arange(N_SEQ, dtype=jnp.int32))
    attention = result_list[0].reshape(TREE_TOKENS, QUERY_HEADS * HEAD_SIZE)
    query_grad = result_list[1].reshape(TREE_TOKENS, QUERY_HEADS * HEAD_SIZE)
    prompt_key_rows = jnp.sum(result_list[2], axis=0)
    prompt_value_rows = jnp.sum(result_list[3], axis=0)
    key_gradient = result_list[4].at[0].add(prompt_key_rows).reshape(TREE_TOKENS, KEY_VALUE_HEADS * HEAD_SIZE).astype(jnp.bfloat16)
    value_gradient = result_list[5].at[0].add(prompt_value_rows).reshape(TREE_TOKENS, KEY_VALUE_HEADS * HEAD_SIZE).astype(jnp.bfloat16)
    return (attention, query_grad, key_gradient, value_gradient)
```

```python
import jax
import jax.numpy as jnp
from jax import lax
from jax.experimental import pallas as pl
from jax.experimental.pallas import tpu as pltpu
from jax.sharding import PartitionSpec as P

HEADS = 4
GROUP = 7
D = 128
QUARTERS = 4
NY, NZ = 4, 8
SCALE = D ** (-0.5)
LOG2E = 1.4426950408889634
MESH = pl.DeviceIdType.MESH
BF16 = jnp.bfloat16
F32 = jnp.float32


def place():
    seq = lax.axis_index("seq")
    x = lax.axis_index("head")
    return x, seq // (2 * NZ), (seq // 2) % NZ, seq % 2


def device(x, y, z, core):
    return ((y * NZ + z) * 2 + core, x)


def remote(src, dst, send_sem, recv_sem, target):
    return pltpu.make_async_remote_copy(
        src_ref=src,
        dst_ref=dst,
        send_sem=send_sem,
        recv_sem=recv_sem,
        device_id=target,
        device_id_type=MESH,
    )


def partners(x, j):
    flip, mirror = x + 1 - 2 * (x % 2), 3 - x
    return (flip, mirror) if j % 2 == 0 else (mirror, flip)


def signal(sem, targets):
    for target in targets:
        pl.semaphore_signal(sem, inc=1, device_id=target, device_id_type=MESH)


def greet(x, y, z, core, tree):
    sem = pltpu.get_barrier_semaphore()
    column, leaf, top = tree & (z == 0), tree & (z != 0), tree & (z == 0) & (y == 0)
    child = tree & (z == 0) & (y != 0)

    @pl.when(top)
    def _():
        signal(sem, [device(x, n, 0, core) for n in (2, 1, 3)])

    @pl.when(column)
    def _():
        signal(sem, [device(x, y, n, core) for n in (4, 3, 5, 2, 6, 1, 7)])

    @pl.when(child)
    def _():
        signal(sem, [device(x, 0, 0, core)])

    @pl.when(leaf)
    def _():
        signal(sem, [device(x, y, 0, core)])

    pa, pb = partners(x, 0)
    signal(sem, [device(pa, y, z, core), device(pb, y, z, core), device(x, y, z, 1 - core)])
    for role, peers in ((top, 2 + NZ + NY - 1), (child, 2 + NZ + 1), (leaf, 4), (~(column | leaf), 3)):
        @pl.when(role)
        def _():
            pl.semaphore_wait(sem, peers)


def gather_kernel(k_ref, v_ref, kv_ref, lsem, s_own, r_own, s_pr, r_pr, s_y, s_z, r_t, s_c, r_c):
    x, y, z, core = place()
    opp = (x + 2) % 4
    is_c0, is_c1 = core == 0, core == 1
    is_root = (core == 0) & (z == 0) & (y == 0)
    column = (core == 0) & (z == 0)
    leaf = (core == 0) & (z != 0)

    def local(j, block, base):
        return [
            pltpu.make_async_copy(
                ref.at[:, pl.ds(j * D, D)], kv_ref.at[j, block, t], lsem.at[base, j, t]
            )
            for t, ref in enumerate((k_ref, v_ref))
        ]

    for j in range(HEADS):
        for copy in local(j, 4 + x, 0):
            copy.start()

    @pl.when(is_root)
    def _():
        for j in range(HEADS):
            for copy in local(j, x, 1):
                copy.start()

    greet(x, y, z, core, core == 0)

    def y_send(j, n):
        blk = kv_ref.at[j, x]
        return remote(blk, blk, s_y.at[j, n - 1], r_t.at[j], device(x, n, 0, 0))

    def z_send(j, n):
        blk = kv_ref.at[j, x]
        return remote(blk, blk, s_z.at[j, n - 1], r_t.at[j], device(x, y, n, 0))

    def x_sends(j, base, ss, rs):
        pa, pb = partners(x, j)
        own, first = kv_ref.at[j, base + x], kv_ref.at[j, base + pa]
        to_a, to_b = device(pa, y, z, core), device(pb, y, z, core)
        return (
            remote(own, own, ss.at[j, 0], rs.at[j, 0], to_a),
            remote(own, own, ss.at[j, 1], rs.at[j, 1], to_b),
            remote(first, first, ss.at[j, 2], rs.at[j, 2], to_b),
        )

    def x_arrival(j, base, ss, rs, i):
        pa, pb = partners(x, j)
        blk = kv_ref.at[j, base + (pa, pb, opp)[i]]
        remote(blk, blk, ss.at[j, i], rs.at[j, i], device((pa, pb, pb)[i], y, z, core)).wait_recv()

    def core_send(j):
        blk = kv_ref.at[j, pl.ds(0, 4)]
        return remote(blk, blk, s_c.at[j], r_c.at[j], device(x, y, z, 1 - core))

    @pl.when(is_root)
    def _():
        for j in range(HEADS):
            for copy in local(j, x, 1):
                copy.wait()
            for n in (2, 1, 3):
                y_send(j, n).start()

    for j in range(HEADS):
        for copy in local(j, 4 + x, 0):
            copy.wait()
        sends = x_sends(j, 4, s_own, r_own)
        sends[0].start()
        sends[1].start()

    @pl.when(is_c0)
    def _():
        for j in range(HEADS):
            @pl.when(column & (y != 0))
            def _():
                y_send(j, y).wait_recv()

            @pl.when(column)
            def _():
                for n in (4, 5, 3, 6, 2, 7, 1):
                    z_send(j, n).start()

            @pl.when(leaf)
            def _():
                z_send(j, z).wait_recv()

            sends = x_sends(j, 0, s_pr, r_pr)
            sends[0].start()
            sends[1].start()
            x_arrival(j, 4, s_own, r_own, 0)
            x_sends(j, 4, s_own, r_own)[2].start()
        for j in range(HEADS):
            x_arrival(j, 0, s_pr, r_pr, 0)
            x_sends(j, 0, s_pr, r_pr)[2].start()
        for j in range(HEADS):
            x_arrival(j, 0, s_pr, r_pr, 1)
            x_arrival(j, 0, s_pr, r_pr, 2)
            core_send(j).start()
        for j in range(HEADS):
            for copy in x_sends(j, 0, s_pr, r_pr):
                copy.wait_send()
            core_send(j).wait_send()

    @pl.when(is_c1)
    def _():
        for j in range(HEADS):
            x_arrival(j, 4, s_own, r_own, 0)
            x_sends(j, 4, s_own, r_own)[2].start()
        for j in range(HEADS):
            core_send(j).wait_recv()

    for j in range(HEADS):
        x_arrival(j, 4, s_own, r_own, 1)
        x_arrival(j, 4, s_own, r_own, 2)
        for copy in x_sends(j, 4, s_own, r_own):
            copy.wait_send()

    @pl.when(column)
    def _():
        for j in range(HEADS):
            for n in range(1, NZ):
                z_send(j, n).wait_send()

    @pl.when(is_root)
    def _():
        for j in range(HEADS):
            for n in range(1, NY):
                y_send(j, n).wait_send()


def gather(k, v):
    dma = pltpu.SemaphoreType.DMA
    return pl.pallas_call(
        gather_kernel,
        out_shape=jax.ShapeDtypeStruct((HEADS, 8, 2, D, D), BF16),
        in_specs=[pl.BlockSpec(memory_space=pltpu.VMEM)] * 2,
        out_specs=pl.BlockSpec(memory_space=pltpu.VMEM),
        scratch_shapes=[
            dma((2, HEADS, 2)),
            dma((HEADS, 3)),
            dma((HEADS, 3)),
            dma((HEADS, 3)),
            dma((HEADS, 3)),
            dma((HEADS, NY - 1)),
            dma((HEADS, NZ - 1)),
            dma((HEADS,)),
            dma((HEADS,)),
            dma((HEADS,)),
        ],
        compiler_params=pltpu.CompilerParams(collective_id=0, has_side_effects=True),
        name="gather_keys_values",
    )(k, v)


def nt(a, b):
    return lax.dot_general(a, b, (((1,), (1,)), ((), ())), preferred_element_type=F32)


def nn(a, b):
    return lax.dot_general(a, b, (((1,), (0,)), ((), ())), preferred_element_type=F32)


def attend_kernel(mask_ref, q_ref, c_ref, kv_ref, att_ref, dq_ref, g_ref, bias, ps, dss, qs, cs):
    x = lax.axis_index("head")
    seq = lax.axis_index("seq")

    @pl.when(pl.program_id(0) == 0)
    def _():
        key = lax.broadcasted_iota(jnp.int32, (D, D), 0)
        query = lax.broadcasted_iota(jnp.int32, (D, D), 1)
        for b in range(QUARTERS):
            reads = jnp.where(seq > 0, mask_ref[x, b], 0)
            level = jnp.where(reads > 0, 0.0, -1e30).astype(F32)
            bias[pl.ds(b * D, D), :] = jnp.full((D, D), level, F32)
            seen = key + b * D <= query + x * D
            bias[pl.ds((4 + b) * D, D), :] = jnp.where(seen, 0.0, -1e30).astype(F32)

    keys = kv_ref[0, :, 0].reshape(8 * D, D)
    values = kv_ref[0, :, 1].reshape(8 * D, D)
    keys_t, values_t = keys.T, values.T
    for h in range(GROUP):
        cols = pl.ds(h * D, D)
        q, c = q_ref[:, cols], c_ref[:, cols]
        qs[cols, :] = q
        cs[cols, :] = c
        s = nt(keys, q) + bias[...]
        top = jnp.max(s, axis=0, keepdims=True)
        p = jnp.exp2((s - top) * (SCALE * LOG2E))
        p = p * (1.0 / jnp.sum(p, axis=0, keepdims=True))
        rounded = p.astype(BF16)
        ps[:, cols] = rounded
        out_t = nn(values_t, rounded)
        att = out_t.T.astype(BF16)
        att_ref[:, cols] = att
        delta = jnp.sum(c.astype(F32).T * out_t.astype(BF16).astype(F32), axis=0, keepdims=True)
        ds = (p * (nt(values, c) - delta)).astype(BF16)
        dss[:, cols] = ds
        dq_ref[:, cols] = (nn(keys_t, ds) * SCALE).T.astype(BF16)
    g_ref[0, :, 0] = (nn(dss[...], qs[...]) * SCALE).reshape(8, D, D)
    g_ref[0, :, 1] = nn(ps[...], cs[...]).reshape(8, D, D)


def attend(mask, q, c, kv):
    wide = pl.BlockSpec((D, GROUP * D), lambda j: (0, j))
    cubes = pl.BlockSpec((1, 8, 2, D, D), lambda j: (j, 0, 0, 0, 0))
    return pl.pallas_call(
        attend_kernel,
        grid=(HEADS,),
        out_shape=(
            jax.ShapeDtypeStruct(q.shape, BF16),
            jax.ShapeDtypeStruct(q.shape, BF16),
            jax.ShapeDtypeStruct((HEADS, 8, 2, D, D), F32),
        ),
        in_specs=[pl.BlockSpec(memory_space=pltpu.SMEM), wide, wide, cubes],
        out_specs=(wide, wide, cubes),
        scratch_shapes=[
            pltpu.VMEM((8 * D, D), F32),
            pltpu.VMEM((8 * D, GROUP * D), BF16),
            pltpu.VMEM((8 * D, GROUP * D), BF16),
            pltpu.VMEM((GROUP * D, D), BF16),
            pltpu.VMEM((GROUP * D, D), BF16),
        ],
        compiler_params=pltpu.CompilerParams(dimension_semantics=("arbitrary",)),
        name="attend",
    )(mask, q, c, kv)


def reduce_kernel(
    g_ref, dk_ref, dv_ref,
    so1, ro1, so2, ro2, sc, rc, gs, sp1, rp1, sp2, rp2, part, sz, rz, sy, ry, rv,
    ss, rs, s_y, r_y, s_z, r_z, s_v, r_v,
):
    x, y, z, core = place()
    opp = (x + 2) % 4
    is_root = (core == 0) & (z == 0) & (y == 0)
    root_pair = (core == 1) & (z == 0) & (y == 0)

    greet(x, y, z, core, z >= 0)

    def own1(j):
        return remote(so1.at[j], ro1.at[j], ss.at[0, j], rs.at[0, j], device(partners(x, j)[0], y, z, core))

    def own2(j):
        return remote(so2.at[j], ro2.at[j], ss.at[1, j], rs.at[1, j], device(partners(x, j)[1], y, z, core))

    def pair(j):
        return remote(sc.at[j], rc.at[j], ss.at[2, j], rs.at[2, j], device(x, y, z, 1 - core))

    def pr1(j):
        return remote(sp1.at[j], rp1.at[j], ss.at[3, j], rs.at[3, j], device(partners(x, j)[0], y, z, core))

    def pr2(j):
        return remote(sp2.at[j], rp2.at[j], ss.at[4, j], rs.at[4, j], device(partners(x, j)[1], y, z, core))

    def to_column(j, n):
        return remote(sz.at[j], rz.at[j, n - 1], s_z.at[j], r_z.at[j, n - 1], device(x, y, 0, core))

    def to_root(j, n):
        return remote(sy.at[j], ry.at[j, n - 1], s_y.at[j], r_y.at[j, n - 1], device(x, 0, 0, core))

    def hand_over(j):
        return remote(part.at[j], rv.at[j], s_v.at[j], r_v.at[j], device(x, y, z, 1 - core))

    for j in range(HEADS):
        for q in range(QUARTERS):
            sc[j, q] = g_ref[j, q, 1 - core].astype(BF16)
        pair(j).start()
    for j in range(HEADS):
        pa, pb = partners(x, j)
        so1[j, 0] = g_ref[j, 4 + pa].astype(BF16)
        so1[j, 1] = g_ref[j, 4 + opp].astype(BF16)
        own1(j).start()
    for j in range(HEADS):
        pa, pb = partners(x, j)
        pair(j).wait_recv()
        for q in range(QUARTERS):
            gs[j, q] = g_ref[j, q, core] + rc[j, q].astype(F32)
        sp1[j, 0] = gs[j, pa].astype(BF16)
        sp1[j, 1] = gs[j, opp].astype(BF16)
        pr1(j).start()
    for j in range(HEADS):
        pa, pb = partners(x, j)
        pr1(j).wait_recv()
        sp2[j] = (gs[j, pb] + rp1[j, 1].astype(F32)).astype(BF16)
        pr2(j).start()
    for j in range(HEADS):
        pa, pb = partners(x, j)
        own1(j).wait_recv()
        so2[j] = (g_ref[j, 4 + pb] + ro1[j, 1].astype(F32)).astype(BF16)
        own2(j).start()
    for j in range(HEADS):
        pr2(j).wait_recv()
        total = gs[j, x] + rp1[j, 0].astype(F32) + rp2[j].astype(F32)
        part[j] = total
        sz[j] = total.astype(BF16)

        @pl.when(z != 0)
        def _():
            to_column(j, z).start()

    @pl.when(z == 0)
    def _():
        for j in range(HEADS):
            total = part[j]
            for n in range(1, NZ):
                to_column(j, n).wait_recv()
                total = total + rz[j, n - 1].astype(F32)
            part[j] = total
            sy[j] = total.astype(BF16)

            @pl.when(y != 0)
            def _():
                to_root(j, y).start()

    @pl.when((z == 0) & (y == 0))
    def _():
        for j in range(HEADS):
            total = part[j]
            for n in range(1, NY):
                to_root(j, n).wait_recv()
                total = total + ry[j, n - 1].astype(F32)
            part[j] = total

            @pl.when(core == 1)
            def _():
                hand_over(j).start()

    for j in range(HEADS):
        own2(j).wait_recv()
        cols = pl.ds(j * D, D)
        total = g_ref[j, 4 + x] + ro1[j, 0].astype(F32) + ro2[j].astype(F32)
        dk_ref[:, cols] = total[0].astype(BF16)
        dv_ref[:, cols] = total[1].astype(BF16)

    @pl.when(is_root)
    def _():
        for j in range(HEADS):
            hand_over(j).wait_recv()
            cols = pl.ds(j * D, D)
            total = g_ref[j, 4 + x] + ro1[j, 0].astype(F32) + ro2[j].astype(F32)
            dk_ref[:, cols] = (total[0] + part[j]).astype(BF16)
            dv_ref[:, cols] = (total[1] + rv[j]).astype(BF16)

    for j in range(HEADS):
        for copy in (own1(j), own2(j), pair(j), pr1(j), pr2(j)):
            copy.wait_send()

        @pl.when(z != 0)
        def _():
            to_column(j, z).wait_send()

        @pl.when((z == 0) & (y != 0))
        def _():
            to_root(j, y).wait_send()

        @pl.when(root_pair)
        def _():
            hand_over(j).wait_send()


def reduce(g):
    dma = pltpu.SemaphoreType.DMA
    block = (D, D)
    vmem = pltpu.VMEM
    out = jax.ShapeDtypeStruct((D, HEADS * D), BF16)
    return pl.pallas_call(
        reduce_kernel,
        out_shape=(out, out),
        in_specs=[pl.BlockSpec(memory_space=pltpu.VMEM)],
        out_specs=(pl.BlockSpec(memory_space=pltpu.VMEM),) * 2,
        scratch_shapes=[
            vmem((HEADS, 2, 2) + block, BF16),
            vmem((HEADS, 2, 2) + block, BF16),
            vmem((HEADS, 2) + block, BF16),
            vmem((HEADS, 2) + block, BF16),
            vmem((HEADS, 4) + block, BF16),
            vmem((HEADS, 4) + block, BF16),
            vmem((HEADS, 4) + block, F32),
            vmem((HEADS, 2) + block, BF16),
            vmem((HEADS, 2) + block, BF16),
            vmem((HEADS,) + block, BF16),
            vmem((HEADS,) + block, BF16),
            vmem((HEADS,) + block, F32),
            vmem((HEADS,) + block, BF16),
            vmem((HEADS, NZ - 1) + block, BF16),
            vmem((HEADS,) + block, BF16),
            vmem((HEADS, NY - 1) + block, BF16),
            vmem((HEADS,) + block, F32),
            dma((5, HEADS)),
            dma((5, HEADS)),
            dma((HEADS,)),
            dma((HEADS, NY - 1)),
            dma((HEADS,)),
            dma((HEADS, NZ - 1)),
            dma((HEADS,)),
            dma((HEADS,)),
        ],
        compiler_params=pltpu.CompilerParams(collective_id=1, has_side_effects=True),
        name="reduce_gradients",
    )(g)


def on_device(queries, rotated_key_rows, value_matrix, cotangent, tree_mask):
    kv = gather(rotated_key_rows, value_matrix)
    attention, query_grad, terms = attend(tree_mask, queries, cotangent, kv)
    key_gradient, value_gradient = reduce(terms)
    return (attention, query_grad, key_gradient, value_gradient)


def solution(mesh):
    rows = P(("seq", "head"), None)
    return jax.shard_map(
        on_device,
        mesh=mesh,
        in_specs=(rows, rows, rows, rows, P("seq", None)),
        out_specs=(rows, rows, rows, rows),
        check_vma=False,
    )
```

```python
import jax
import jax.numpy as jnp
from jax import lax
from jax.experimental import pallas as pl
from jax.experimental.pallas import tpu as pltpu
from jax.sharding import PartitionSpec as P

HEADS = 4
GROUP = 7
D = 128
QUARTERS = 4
NY, NZ = 4, 8
SCALE = D ** (-0.5)
LOG2E = 1.4426950408889634
MESH = pl.DeviceIdType.MESH
BF16 = jnp.bfloat16
F32 = jnp.float32


def place():
    seq = lax.axis_index("seq")
    x = lax.axis_index("head")
    return x, seq // (2 * NZ), (seq // 2) % NZ, seq % 2


def device(x, y, z, core):
    return ((y * NZ + z) * 2 + core, x)


def remote(src, dst, send_sem, recv_sem, target):
    return pltpu.make_async_remote_copy(
        src_ref=src,
        dst_ref=dst,
        send_sem=send_sem,
        recv_sem=recv_sem,
        device_id=target,
        device_id_type=MESH,
    )


def partners(x, j):
    flip, mirror = x + 1 - 2 * (x % 2), 3 - x
    return (flip, mirror) if j % 2 == 0 else (mirror, flip)


def signal(sem, targets):
    for target in targets:
        pl.semaphore_signal(sem, inc=1, device_id=target, device_id_type=MESH)


def greet(x, y, z, core, tree):
    sem = pltpu.get_barrier_semaphore()
    column, leaf, top = tree & (z == 0), tree & (z != 0), tree & (z == 0) & (y == 0)
    child = tree & (z == 0) & (y != 0)

    @pl.when(top)
    def _():
        signal(sem, [device(x, n, 0, core) for n in (2, 1, 3)])

    @pl.when(column)
    def _():
        signal(sem, [device(x, y, n, core) for n in (4, 3, 5, 2, 6, 1, 7)])

    @pl.when(child)
    def _():
        signal(sem, [device(x, 0, 0, core)])

    @pl.when(leaf)
    def _():
        signal(sem, [device(x, y, 0, core)])

    pa, pb = partners(x, 0)
    signal(sem, [device(pa, y, z, core), device(pb, y, z, core), device(x, y, z, 1 - core)])
    for role, peers in ((top, 2 + NZ + NY - 1), (child, 2 + NZ + 1), (leaf, 4), (~(column | leaf), 3)):
        @pl.when(role)
        def _():
            pl.semaphore_wait(sem, peers)


TILES = ((0, 256), (256, 256), (512, 256), (768, 128))
WIDE = GROUP * D
EXP_SCALE = SCALE * LOG2E


def nt(a, b):
    return lax.dot_general(a, b, (((1,), (1,)), ((), ())), preferred_element_type=F32)


def nn(a, b):
    return lax.dot_general(a, b, (((1,), (0,)), ((), ())), preferred_element_type=F32)


def fold_max(a):
    return jnp.max(a.reshape(D // 8, 8, a.shape[1]), axis=0)


def fold_sum(a):
    return jnp.sum(a.reshape(D // 8, 8, a.shape[1]), axis=0)


def main_kernel(
    mask_ref, k_ref, v_ref, q_hbm, c_hbm,
    att_hbm, dq_hbm, dk_ref, dv_ref,
    kv, q_s, c_s, att_s, dq_s, bias, po, dpo, mo, lo, sp, dpp, ps, dss, vt,
    g, so1, ro1, so2, ro2, sc, rc, gs, sp1, rp1, sp2, rp2, part, sz, rz, sy, ry, rv,
    lsem, qsem, osem, s_own, r_own, s_pr, r_pr, s_by, s_bz, r_t, s_c, r_c,
    ss, rs, s_y, r_y, s_z, r_z, s_v, r_v,
):
    x, y, z, core = place()
    opp = (x + 2) % 4
    seq = lax.axis_index("seq")
    top_row = (z == 0) & (y == 0)
    is_root = top_row & (core == 0)
    root_pair = top_row & (core == 1)
    column = (core == 0) & (z == 0)
    leaf = (core == 0) & (z != 0)

    def local(j, block, base):
        return [
            pltpu.make_async_copy(ref.at[:, pl.ds(j * D, D)], kv.at[j, block, t], lsem.at[base, j, t])
            for t, ref in enumerate((k_ref, v_ref))
        ]

    for j in range(HEADS):
        for copy in local(j, 4 + x, 0):
            copy.start()

    @pl.when(is_root)
    def _():
        for j in range(HEADS):
            for copy in local(j, x, 1):
                copy.start()

    for j in range(HEADS):
        for h in range(GROUP):
            cols, rows = pl.ds((j * GROUP + h) * D, D), pl.ds(h * D, D)
            pltpu.make_async_copy(q_hbm.at[:, cols], q_s.at[j, rows], qsem.at[0, j]).start()
            pltpu.make_async_copy(c_hbm.at[:, cols], c_s.at[j, rows], qsem.at[1, j]).start()

    def take_out(buf, hbm, i, j):
        for h in range(GROUP):
            cols, rows = pl.ds((j * GROUP + h) * D, D), pl.ds(h * D, D)
            pltpu.make_async_copy(buf.at[j, rows], hbm.at[:, cols], osem.at[i, j]).start()

    greet(x, y, z, core, z >= 0)

    def y_send(j, n):
        blk = kv.at[j, x]
        return remote(blk, blk, s_by.at[j, n - 1], r_t.at[j], device(x, n, 0, 0))

    def z_send(j, n):
        blk = kv.at[j, x]
        return remote(blk, blk, s_bz.at[j, n - 1], r_t.at[j], device(x, y, n, 0))

    def x_send(j, base, ss, rs, i):
        pa, pb = partners(x, j)
        blk = kv.at[j, base + (x, x, pa)[i]]
        return remote(blk, blk, ss.at[j, i], rs.at[j, i], device((pa, pb, pb)[i], y, z, core))

    def x_arrival(j, base, ss, rs, i):
        pa, pb = partners(x, j)
        blk = kv.at[j, base + (pa, pb, opp)[i]]
        remote(blk, blk, ss.at[j, i], rs.at[j, i], device((pa, pb, pb)[i], y, z, core)).wait_recv()

    def core_send(j):
        blk = kv.at[j, pl.ds(0, 4)]
        return remote(blk, blk, s_c.at[j], r_c.at[j], device(x, y, z, 1 - core))

    @pl.when(is_root)
    def _():
        for j in range(HEADS):
            for copy in local(j, x, 1):
                copy.wait()
            for n in (2, 1, 3):
                y_send(j, n).start()

    for j in range(HEADS):
        for copy in local(j, 4 + x, 0):
            copy.wait()
        x_send(j, 4, s_own, r_own, 0).start()
        x_send(j, 4, s_own, r_own, 1).start()

    key = lax.broadcasted_iota(jnp.int32, (D, D), 0)
    query = lax.broadcasted_iota(jnp.int32, (D, D), 1)
    for b in range(QUARTERS):
        seen = key + b * D <= query + x * D
        tile = jnp.where(seen, 0.0, -1e30).astype(F32)
        bias[pl.ds(b * D, D), pl.ds(0, D)] = tile
        bias[pl.ds(b * D, D), pl.ds(D, D)] = tile
    levels = []
    for b in range(QUARTERS):
        reads = jnp.where(seq > 0, mask_ref[x, b], 0)
        levels.append(jnp.where(reads > 0, 0.0, -1e30).astype(F32))

    def relay(j):
        @pl.when(column)
        def _():
            @pl.when(y != 0)
            def _():
                y_send(j, y).wait_recv()

            for n in (4, 5, 3, 6, 2, 7, 1):
                z_send(j, n).start()

        x_arrival(j, 4, s_own, r_own, 0)
        x_send(j, 4, s_own, r_own, 2).start()

    def prompt1(j):
        @pl.when(core == 0)
        def _():
            @pl.when(leaf)
            def _():
                z_send(j, z).wait_recv()

            x_send(j, 0, s_pr, r_pr, 0).start()
            x_send(j, 0, s_pr, r_pr, 1).start()

    def prompt2(j):
        @pl.when(core == 0)
        def _():
            x_arrival(j, 0, s_pr, r_pr, 0)
            x_send(j, 0, s_pr, r_pr, 2).start()

    def prompt3(j):
        @pl.when(core == 0)
        def _():
            x_arrival(j, 0, s_pr, r_pr, 1)
            x_arrival(j, 0, s_pr, r_pr, 2)
            core_send(j).start()

    def prompt_here(j):
        @pl.when(core == 1)
        def _():
            core_send(j).wait_recv()

    def own_part(j):
        x_arrival(j, 4, s_own, r_own, 1)
        x_arrival(j, 4, s_own, r_own, 2)
        pltpu.make_async_copy(q_s.at[j], q_s.at[j], qsem.at[0, j]).wait()
        pltpu.make_async_copy(c_s.at[j], c_s.at[j], qsem.at[1, j]).wait()
        for at, width in TILES:
            cols = pl.ds(at, width)
            keys = kv[j, 4:8, 0].reshape(4 * D, D)
            values = kv[j, 4:8, 1].reshape(4 * D, D)
            po[j, :, cols] = nt(keys, q_s[j, cols, :]) + bias[:, pl.ds(0, width)]
            top = None
            for b in range(QUARTERS):
                part_top = fold_max(po[j, pl.ds(b * D, D), cols])
                top = part_top if top is None else jnp.maximum(top, part_top)
            top = jnp.max(top, axis=0, keepdims=True)
            total = None
            for b in range(QUARTERS):
                p = jnp.exp2((po[j, pl.ds(b * D, D), cols] - top) * EXP_SCALE)
                po[j, pl.ds(b * D, D), cols] = p
                part_sum = fold_sum(p)
                total = part_sum if total is None else total + part_sum
            mo[j, :, cols] = top
            lo[j, :, cols] = jnp.sum(total, axis=0, keepdims=True)
            dpo[j, :, cols] = nt(values, c_s[j, cols, :])

    def flip_values(j):
        for b in range(2 * QUARTERS):
            vt[:, pl.ds(b * D, D)] = kv[j, b, 1].T

    def prompt_part(j, at, width):
        cols, wide = pl.ds(at, width), pl.ds(0, width)
        c = c_s[j, cols, :]
        sp[:, wide] = nt(kv[j, 0:4, 0].reshape(4 * D, D), q_s[j, cols, :])
        dpp[:, wide] = nt(kv[j, 0:4, 1].reshape(4 * D, D), c)
        own_top = mo[j, :, cols]
        top = None
        for b in range(QUARTERS):
            part_top = fold_max(sp[pl.ds(b * D, D), wide]) + levels[b]
            top = part_top if top is None else jnp.maximum(top, part_top)
        top = jnp.maximum(own_top, jnp.max(top, axis=0, keepdims=True))
        shrink = jnp.exp2((own_top - top) * EXP_SCALE)
        total = None
        for b in range(QUARTERS):
            rows = pl.ds(b * D, D)
            p = jnp.exp2((sp[rows, wide] - (top - levels[b])) * EXP_SCALE)
            sp[rows, wide] = p
            part_sum = fold_sum(p)
            total = part_sum if total is None else total + part_sum
        total = jnp.sum(total, axis=0, keepdims=True) + lo[j, :, cols] * shrink
        inverse = 1.0 / total
        shrink = shrink * inverse
        for b in range(QUARTERS):
            rows = pl.ds(b * D, D)
            ps[rows, cols] = (sp[rows, wide] * inverse).astype(BF16)
            ps[pl.ds((4 + b) * D, D), cols] = (po[j, rows, cols] * shrink).astype(BF16)
        out_t = nn(vt[...], ps[:, cols]).astype(BF16)
        deltas = []
        for i in range(width // D):
            lanes, rows = slice(i * D, i * D + D), pl.ds(at + i * D, D)
            att_s[j, rows, :] = out_t[:, lanes].T
            prod = c_s[j, rows, :].T.astype(F32) * out_t[:, lanes].astype(F32)
            deltas.append(jnp.sum(prod, axis=0, keepdims=True))
        delta = jnp.concatenate(deltas, axis=1)
        for b in range(QUARTERS):
            rows = pl.ds(b * D, D)
            dss[j, rows, cols] = ((sp[rows, wide] * inverse) * (dpp[rows, wide] - delta)).astype(BF16)
            dss[j, pl.ds((4 + b) * D, D), cols] = (
                (po[j, rows, cols] * shrink) * (dpo[j, rows, cols] - delta)
            ).astype(BF16)

    def key_terms(j, first):
        rows = pl.ds(first * D, 4 * D)
        g[j, first : first + 4, 0] = (nn(dss[j, rows, :], q_s[j]) * SCALE).reshape(4, D, D)
        g[j, first : first + 4, 1] = nn(ps[rows, :], c_s[j]).reshape(4, D, D)

    def query_part(j):
        for b in range(2 * QUARTERS):
            vt[:, pl.ds(b * D, D)] = kv[j, b, 0].T
        for at, width in TILES:
            grad_t = (nn(vt[...], dss[j, :, pl.ds(at, width)]) * SCALE).astype(BF16)
            for i in range(width // D):
                dq_s[j, pl.ds(at + i * D, D), :] = grad_t[:, i * D : i * D + D].T
        take_out(dq_s, dq_hbm, 1, j)

    def hop(send, arrive, i, j, target):
        return remote(send.at[j], arrive.at[j], ss.at[i, j], rs.at[i, j], target)

    def own1(j):
        return hop(so1, ro1, 0, j, device(partners(x, j)[0], y, z, core))

    def own2(j):
        return hop(so2, ro2, 1, j, device(partners(x, j)[1], y, z, core))

    def pair(j):
        return hop(sc, rc, 2, j, device(x, y, z, 1 - core))

    def pr1(j):
        return hop(sp1, rp1, 3, j, device(partners(x, j)[0], y, z, core))

    def pr2(j):
        return hop(sp2, rp2, 4, j, device(partners(x, j)[1], y, z, core))

    def to_column(j, n):
        return remote(sz.at[j], rz.at[j, n - 1], s_z.at[j], r_z.at[j, n - 1], device(x, y, 0, core))

    def to_root(j, n):
        return remote(sy.at[j], ry.at[j, n - 1], s_y.at[j], r_y.at[j, n - 1], device(x, 0, 0, core))

    def hand_over(j):
        return remote(part.at[j], rv.at[j], s_v.at[j], r_v.at[j], device(x, y, z, 1 - core))

    def reduce0(j):
        for b in range(QUARTERS):
            sc[j, b] = g[j, b, 1 - core].astype(BF16)
        pair(j).start()

    def own_reduce1(j):
        pa, pb = partners(x, j)
        so1[j, 0] = g[j, 4 + pa].astype(BF16)
        so1[j, 1] = g[j, 4 + opp].astype(BF16)
        own1(j).start()

    def reduce1(j):
        pa, pb = partners(x, j)
        pair(j).wait_recv()
        for b in range(QUARTERS):
            gs[j, b] = g[j, b, core] + rc[j, b].astype(F32)
        sp1[j, 0] = gs[j, pa].astype(BF16)
        sp1[j, 1] = gs[j, opp].astype(BF16)
        pr1(j).start()

    def reduce2(j):
        pa, pb = partners(x, j)
        pr1(j).wait_recv()
        sp2[j] = (gs[j, pb] + rp1[j, 1].astype(F32)).astype(BF16)
        pr2(j).start()

    def own_reduce2(j):
        pa, pb = partners(x, j)
        own1(j).wait_recv()
        so2[j] = (g[j, 4 + pb] + ro1[j, 1].astype(F32)).astype(BF16)
        own2(j).start()

    def reduce3(j):
        pr2(j).wait_recv()
        total = gs[j, x] + rp1[j, 0].astype(F32) + rp2[j].astype(F32)
        part[j] = total
        sz[j] = total.astype(BF16)

        @pl.when(z != 0)
        def _():
            to_column(j, z).start()

    def reduce4(j):
        @pl.when(z == 0)
        def _():
            total = part[j]
            for n in range(1, NZ):
                to_column(j, n).wait_recv()
                total = total + rz[j, n - 1].astype(F32)
            part[j] = total
            sy[j] = total.astype(BF16)

            @pl.when(y != 0)
            def _():
                to_root(j, y).start()

    def reduce5(j):
        @pl.when(top_row)
        def _():
            total = part[j]
            for n in range(1, NY):
                to_root(j, n).wait_recv()
                total = total + ry[j, n - 1].astype(F32)
            part[j] = total

            @pl.when(core == 1)
            def _():
                hand_over(j).start()

    def own_result(j):
        own2(j).wait_recv()
        cols = pl.ds(j * D, D)
        total = g[j, 4 + x] + ro1[j, 0].astype(F32) + ro2[j].astype(F32)
        g[j, 4 + x] = total
        dk_ref[:, cols] = total[0].astype(BF16)
        dv_ref[:, cols] = total[1].astype(BF16)

    def root_result(j):
        @pl.when(is_root)
        def _():
            hand_over(j).wait_recv()
            cols = pl.ds(j * D, D)
            dk_ref[:, cols] = (g[j, 4 + x, 0] + part[j]).astype(BF16)
            dv_ref[:, cols] = (g[j, 4 + x, 1] + rv[j]).astype(BF16)

    for j in range(HEADS):
        relay(j)
    own_part(0)
    prompt1(0)
    prompt1(1)
    own_part(1)
    prompt2(0)
    prompt1(2)
    own_part(2)
    prompt3(0)
    prompt2(1)
    prompt1(3)
    own_part(3)
    prompt3(1)
    prompt2(2)
    prompt2(3)
    between = {
        (0, 1): lambda: prompt3(2),
        (0, 3): lambda: prompt3(3),
    }
    for j in range(1, HEADS):
        between[j, 0] = lambda j=j: reduce1(j - 1)
        between[j, 2] = lambda j=j: (reduce2(j - 1), own_reduce2(j - 1))
        between[j, 4] = lambda j=j: reduce3(j - 1)
    for j in range(2, HEADS):
        between[j, 3] = lambda j=j: (reduce4(j - 2), own_result(j - 2))
    for j in range(HEADS):
        prompt_here(j)
        flip_values(j)
        for i, (at, width) in enumerate(TILES):
            prompt_part(j, at, width)
            between.get((j, i), lambda: None)()
        key_terms(j, 0)
        reduce0(j)
        key_terms(j, 4)
        own_reduce1(j)
        take_out(att_s, att_hbm, 0, j)
        between.get((j, 4), lambda: None)()
    last = HEADS - 1
    reduce1(last)
    query_part(0)
    reduce2(last)
    own_reduce2(last)
    query_part(1)
    reduce4(last - 1)
    reduce3(last)
    query_part(2)
    own_result(last - 1)
    query_part(3)
    own_result(last)
    reduce4(last)
    for j in range(HEADS):
        reduce5(j)
        root_result(j)

    for j in range(HEADS):
        for i in range(3):
            x_send(j, 4, s_own, r_own, i).wait_send()

        @pl.when(core == 0)
        def _():
            for i in range(3):
                x_send(j, 0, s_pr, r_pr, i).wait_send()
            core_send(j).wait_send()

        @pl.when(column)
        def _():
            for n in range(1, NZ):
                z_send(j, n).wait_send()

        @pl.when(is_root)
        def _():
            for n in range(1, NY):
                y_send(j, n).wait_send()

        for copy in (own1(j), own2(j), pair(j), pr1(j), pr2(j)):
            copy.wait_send()

        @pl.when(z != 0)
        def _():
            to_column(j, z).wait_send()

        @pl.when((z == 0) & (y != 0))
        def _():
            to_root(j, y).wait_send()

        @pl.when(root_pair)
        def _():
            hand_over(j).wait_send()

        pltpu.make_async_copy(att_s.at[j], att_s.at[j], osem.at[0, j]).wait()
        pltpu.make_async_copy(dq_s.at[j], dq_s.at[j], osem.at[1, j]).wait()


def main(mask, k, v, q, c):
    dma, vmem = pltpu.SemaphoreType.DMA, pltpu.VMEM
    block = (D, D)
    wide = jax.ShapeDtypeStruct(q.shape, BF16)
    narrow = jax.ShapeDtypeStruct(k.shape, BF16)
    here = pl.BlockSpec(memory_space=pltpu.VMEM)
    there = pl.BlockSpec(memory_space=pl.ANY)
    return pl.pallas_call(
        main_kernel,
        out_shape=(wide, wide, narrow, narrow),
        in_specs=[pl.BlockSpec(memory_space=pltpu.SMEM), here, here, there, there],
        out_specs=(there, there, here, here),
        scratch_shapes=[
            vmem((HEADS, 8, 2) + block, BF16),
            vmem((HEADS, WIDE, D), BF16),
            vmem((HEADS, WIDE, D), BF16),
            vmem((HEADS, WIDE, D), BF16),
            vmem((HEADS, WIDE, D), BF16),
            vmem((4 * D, 2 * D), F32),
            vmem((HEADS, 4 * D, WIDE), F32),
            vmem((HEADS, 4 * D, WIDE), F32),
            vmem((HEADS, 1, WIDE), F32),
            vmem((HEADS, 1, WIDE), F32),
            vmem((4 * D, 2 * D), F32),
            vmem((4 * D, 2 * D), F32),
            vmem((8 * D, WIDE), BF16),
            vmem((HEADS, 8 * D, WIDE), BF16),
            vmem((D, 8 * D), BF16),
            vmem((HEADS, 8, 2) + block, F32),
            vmem((HEADS, 2, 2) + block, BF16),
            vmem((HEADS, 2, 2) + block, BF16),
            vmem((HEADS, 2) + block, BF16),
            vmem((HEADS, 2) + block, BF16),
            vmem((HEADS, 4) + block, BF16),
            vmem((HEADS, 4) + block, BF16),
            vmem((HEADS, 4) + block, F32),
            vmem((HEADS, 2) + block, BF16),
            vmem((HEADS, 2) + block, BF16),
            vmem((HEADS,) + block, BF16),
            vmem((HEADS,) + block, BF16),
            vmem((HEADS,) + block, F32),
            vmem((HEADS,) + block, BF16),
            vmem((HEADS, NZ - 1) + block, BF16),
            vmem((HEADS,) + block, BF16),
            vmem((HEADS, NY - 1) + block, BF16),
            vmem((HEADS,) + block, F32),
            dma((2, HEADS, 2)),
            dma((2, HEADS)),
            dma((2, HEADS)),
            dma((HEADS, 3)),
            dma((HEADS, 3)),
            dma((HEADS, 3)),
            dma((HEADS, 3)),
            dma((HEADS, NY - 1)),
            dma((HEADS, NZ - 1)),
            dma((HEADS,)),
            dma((HEADS,)),
            dma((HEADS,)),
            dma((5, HEADS)),
            dma((5, HEADS)),
            dma((HEADS,)),
            dma((HEADS, NY - 1)),
            dma((HEADS,)),
            dma((HEADS, NZ - 1)),
            dma((HEADS,)),
            dma((HEADS,)),
        ],
        compiler_params=pltpu.CompilerParams(
            collective_id=0, has_side_effects=True, vmem_limit_bytes=60 * 2**20
        ),
        name="tree_attention",
    )(mask, k, v, q, c)


def hand_on_kernel(*refs):
    for src, dst in zip(refs[:4], refs[4:]):
        dst[...] = src[...]


def hand_on(arrays):
    specs = [pl.BlockSpec((D // 4, a.shape[1]), lambda i: (i, 0)) for a in arrays]
    return pl.pallas_call(
        hand_on_kernel,
        grid=(4,),
        out_shape=[jax.ShapeDtypeStruct(a.shape, a.dtype) for a in arrays],
        in_specs=specs,
        out_specs=specs,
        name="hand_on",
    )(*arrays)


def on_device(queries, rotated_key_rows, value_matrix, cotangent, tree_mask):
    return tuple(hand_on(main(tree_mask, rotated_key_rows, value_matrix, queries, cotangent)))


def solution(mesh):
    rows = P(("seq", "head"), None)
    return jax.shard_map(
        on_device,
        mesh=mesh,
        in_specs=(rows, rows, rows, rows, P("seq", None)),
        out_specs=(rows, rows, rows, rows),
        check_vma=False,
    )
```

```python
import jax
import jax.numpy as jnp
from jax import lax
from jax.experimental import pallas as pl
from jax.experimental.pallas import tpu as pltpu
from jax.sharding import PartitionSpec as P

HEADS = 4
GROUP = 7
D = 128
QUARTERS = 4
NY, NZ = 4, 8
SCALE = D ** (-0.5)
LOG2E = 1.4426950408889634
MESH = pl.DeviceIdType.MESH
BF16 = jnp.bfloat16
F32 = jnp.float32


def place():
    seq = lax.axis_index("seq")
    x = lax.axis_index("head")
    return x, seq // (2 * NZ), (seq // 2) % NZ, seq % 2


def device(x, y, z, core):
    return ((y * NZ + z) * 2 + core, x)


def remote(src, dst, send_sem, recv_sem, target):
    return pltpu.make_async_remote_copy(
        src_ref=src,
        dst_ref=dst,
        send_sem=send_sem,
        recv_sem=recv_sem,
        device_id=target,
        device_id_type=MESH,
    )


def partners(x, j):
    flip, mirror = x + 1 - 2 * (x % 2), 3 - x
    return (flip, mirror) if j % 2 == 0 else (mirror, flip)


def others(x):
    return (x + 1 - 2 * (x % 2), 3 - x, (x + 2) % 4)


def say_hello(x, y, z, core):
    sem = pltpu.get_barrier_semaphore()

    def signal(condition, targets):
        @pl.when(condition)
        def _():
            for target in targets:
                pl.semaphore_signal(sem, inc=1, device_id=target, device_id_type=MESH)

    first = core == 0
    signal((z == 0) & (y == 0) & first, [device(x, n, 0, c) for n in (2, 1, 3) for c in (0, 1)])
    signal(z == 0, [device(x, y, n, core) for n in (4, 3, 5, 2, 6, 1, 7)])
    signal((z == 0) & (y != 0), [device(x, 0, 0, 0)])
    signal(z != 0, [device(x, y, 0, core)])
    signal((z == 2) & first, [device(x, y, 3, 0), device(x, y, 4, 0)])
    signal((z == 6) & first, [device(x, y, 5, 0)])
    signal(((z == 3) | (z == 4)) & first, [device(x, y, 2, 0)])
    signal((z == 5) & first, [device(x, y, 6, 0)])
    signal(z >= 0, [device(n, y, z, core) for n in others(x)] + [device(x, y, z, 1 - core)])


def hear_all(x, y, z, core):
    sem = pltpu.get_barrier_semaphore()
    first = core == 0
    end = (z == 1) | (z == 7)
    for role, peers in (
        ((z == 0) & (y == 0) & first, 17),
        ((z == 0) & (y == 0) & ~first, 11),
        ((z == 0) & (y != 0), 12),
        ((z != 0) & (~first | end), 5),
        ((z == 2) & first, 7),
        ((z != 0) & (z != 2) & ~end & first, 6),
    ):
        @pl.when(role)
        def _():
            pl.semaphore_wait(sem, peers)


TILES = ((0, 256), (256, 256), (512, 256), (768, 128))
WIDE = GROUP * D
EXP_SCALE = SCALE * LOG2E


def nt(a, b):
    return lax.dot_general(a, b, (((1,), (1,)), ((), ())), preferred_element_type=F32)


def nn(a, b):
    return lax.dot_general(a, b, (((1,), (0,)), ((), ())), preferred_element_type=F32)


def fold_max(a):
    return jnp.max(a.reshape(D // 8, 8, a.shape[1]), axis=0)


def fold_sum(a):
    return jnp.sum(a.reshape(D // 8, 8, a.shape[1]), axis=0)


def main_kernel(
    mask_ref, k_ref, v_ref, q_hbm, c_hbm,
    att_hbm, dq_hbm, dk_ref, dv_ref,
    kv, q_s, c_s, att_s, dq_s, bias, po, dpo, mo, lo, fo, de, sp, dpp, ps, dss, vt,
    g, so1, ro1, so2, ro2, sc, rc, gs, sp1, rp1, part, sz, rz, sy, ry,
    lsem, qsem, osem, s_own, r_own, s_pr, r_pr, s_by, s_bz, r_t, s_c, r_c,
    ss, rs, s_a, r_a, s_y, r_y, s_z, r_z,
):
    x, y, z, core = place()
    opp = (x + 2) % 4
    seq = lax.axis_index("seq")
    top_row = (z == 0) & (y == 0)
    is_root = top_row & (core == 0)
    column = (core == 0) & (z == 0)
    leaf = (core == 0) & (z != 0)

    say_hello(x, y, z, core)

    def local(j, block, base):
        return [
            pltpu.make_async_copy(ref.at[:, pl.ds(j * D, D)], kv.at[j, block, t], lsem.at[base, j, t])
            for t, ref in enumerate((k_ref, v_ref))
        ]

    @pl.when(is_root)
    def _():
        for j in range(HEADS):
            for copy in local(j, x, 1):
                copy.start()

    for j in range(HEADS):
        for copy in local(j, 4 + x, 0):
            copy.start()

    for j in range(HEADS):
        for h in range(GROUP):
            cols, rows = pl.ds((j * GROUP + h) * D, D), pl.ds(h * D, D)
            pltpu.make_async_copy(q_hbm.at[:, cols], q_s.at[j, rows], qsem.at[0, j]).start()
            pltpu.make_async_copy(c_hbm.at[:, cols], c_s.at[j, rows], qsem.at[1, j]).start()

    def take_out(buf, hbm, i, j):
        for h in range(GROUP):
            cols, rows = pl.ds((j * GROUP + h) * D, D), pl.ds(h * D, D)
            pltpu.make_async_copy(buf.at[j, rows], hbm.at[:, cols], osem.at[i, j]).start()

    hear_all(x, y, z, core)

    def y_send(j, n):
        blk = kv.at[j, x]
        return remote(blk, blk, s_by.at[j, n - 1], r_t.at[j], device(x, n, 0, 0))

    def z_send(j, n):
        blk = kv.at[j, x]
        return remote(blk, blk, s_bz.at[j, n - 1], r_t.at[j], device(x, y, n, 0))

    def pass_on(j):
        for n in (2, 6, 1, 7):
            z_send(j, n).start()

    def x_send(j, base, ss, rs, i):
        pa, pb = partners(x, j)
        blk = kv.at[j, base + (x, x, pa)[i]]
        return remote(blk, blk, ss.at[j, i], rs.at[j, i], device((pa, pb, pb)[i], y, z, core))

    def x_arrival(j, base, ss, rs, i):
        pa, pb = partners(x, j)
        blk = kv.at[j, base + (pa, pb, opp)[i]]
        remote(blk, blk, ss.at[j, i], rs.at[j, i], device((pa, pb, pb)[i], y, z, core)).wait_recv()

    def p_send(j, i):
        blk = kv.at[j, x]
        return remote(blk, blk, s_pr.at[j, i], r_pr.at[j, i], device(others(x)[i], y, z, core))

    def core_send(j):
        blk = kv.at[j, pl.ds(0, 4)]
        return remote(blk, blk, s_c.at[j], r_c.at[j], device(x, y, z, 1 - core))

    @pl.when(is_root)
    def _():
        for j in range(HEADS):
            for copy in local(j, x, 1):
                copy.wait()
            for n in (2, 1, 3):
                y_send(j, n).start()
            pass_on(j)

    for j in range(HEADS):
        for copy in local(j, 4 + x, 0):
            copy.wait()
        x_send(j, 4, s_own, r_own, 0).start()
        x_send(j, 4, s_own, r_own, 1).start()

    key = lax.broadcasted_iota(jnp.int32, (D, D), 0)
    query = lax.broadcasted_iota(jnp.int32, (D, D), 1)
    for b in range(QUARTERS):
        seen = key + b * D <= query + x * D
        tile = jnp.where(seen, 0.0, -1e30).astype(F32)
        bias[pl.ds(b * D, D), pl.ds(0, D)] = tile
        bias[pl.ds(b * D, D), pl.ds(D, D)] = tile
    levels = []
    for b in range(QUARTERS):
        reads = jnp.where(seq > 0, mask_ref[x, b], 0)
        levels.append(jnp.where(reads > 0, 0.0, -1e30).astype(F32))

    def relay(j):
        @pl.when(column & (y != 0))
        def _():
            y_send(j, y).wait_recv()
            pass_on(j)

        x_arrival(j, 4, s_own, r_own, 0)
        x_send(j, 4, s_own, r_own, 2).start()

    def prompt1(j):
        @pl.when(leaf)
        def _():
            z_send(j, z).wait_recv()

            @pl.when(z == 2)
            def _():
                z_send(j, 4).start()
                z_send(j, 3).start()

            @pl.when(z == 6)
            def _():
                z_send(j, 5).start()

        @pl.when(core == 0)
        def _():
            for i in (2, 0, 1):
                p_send(j, i).start()

    def prompt3(j):
        @pl.when(core == 0)
        def _():
            for i, n in enumerate(others(x)):
                blk = kv.at[j, n]
                remote(blk, blk, s_pr.at[j, i], r_pr.at[j, i], device(n, y, z, core)).wait_recv()
            core_send(j).start()

    def prompt_here(j):
        @pl.when(core == 1)
        def _():
            core_send(j).wait_recv()

    def own_part(j):
        x_arrival(j, 4, s_own, r_own, 1)
        x_arrival(j, 4, s_own, r_own, 2)
        pltpu.make_async_copy(q_s.at[j], q_s.at[j], qsem.at[0, j]).wait()
        pltpu.make_async_copy(c_s.at[j], c_s.at[j], qsem.at[1, j]).wait()
        for at, width in TILES:
            cols = pl.ds(at, width)
            keys = kv[j, 4:8, 0].reshape(4 * D, D)
            values = kv[j, 4:8, 1].reshape(4 * D, D)
            po[j, :, cols] = nt(keys, q_s[j, cols, :]) + bias[:, pl.ds(0, width)]
            top = None
            for b in range(QUARTERS):
                part_top = fold_max(po[j, pl.ds(b * D, D), cols])
                top = part_top if top is None else jnp.maximum(top, part_top)
            top = jnp.max(top, axis=0, keepdims=True)
            total = None
            for b in range(QUARTERS):
                p = jnp.exp2((po[j, pl.ds(b * D, D), cols] - top) * EXP_SCALE)
                po[j, pl.ds(b * D, D), cols] = p
                part_sum = fold_sum(p)
                total = part_sum if total is None else total + part_sum
            mo[j, :, cols] = top
            lo[j, :, cols] = jnp.sum(total, axis=0, keepdims=True)
            dpo[j, :, cols] = nt(values, c_s[j, cols, :])

    def flip_values(j):
        for b in range(2 * QUARTERS):
            vt[:, pl.ds(b * D, D)] = kv[j, b, 1].T

    def prompt_part(j, at, width):
        cols, wide = pl.ds(at, width), pl.ds(0, width)
        c = c_s[j, cols, :]
        sp[:, wide] = nt(kv[j, 0:4, 0].reshape(4 * D, D), q_s[j, cols, :])
        dpp[:, wide] = nt(kv[j, 0:4, 1].reshape(4 * D, D), c)
        own_top = mo[j, :, cols]
        top = None
        for b in range(QUARTERS):
            part_top = fold_max(sp[pl.ds(b * D, D), wide]) + levels[b]
            top = part_top if top is None else jnp.maximum(top, part_top)
        top = jnp.maximum(own_top, jnp.max(top, axis=0, keepdims=True))
        shrink = jnp.exp2((own_top - top) * EXP_SCALE)
        total = None
        for b in range(QUARTERS):
            rows = pl.ds(b * D, D)
            p = jnp.exp2((sp[rows, wide] - (top - levels[b])) * EXP_SCALE)
            sp[rows, wide] = p
            part_sum = fold_sum(p)
            total = part_sum if total is None else total + part_sum
        total = jnp.sum(total, axis=0, keepdims=True) + lo[j, :, cols] * shrink
        inverse = 1.0 / total
        shrink = shrink * inverse
        fo[j, :, cols] = shrink
        for b in range(QUARTERS):
            rows = pl.ds(b * D, D)
            ps[j, rows, cols] = (sp[rows, wide] * inverse).astype(BF16)
            ps[j, pl.ds((4 + b) * D, D), cols] = (po[j, rows, cols] * shrink).astype(BF16)
        out_t = nn(vt[...], ps[j, :, cols]).astype(BF16)
        deltas = []
        for i in range(width // D):
            lanes, rows = slice(i * D, i * D + D), pl.ds(at + i * D, D)
            att_s[j, rows, :] = out_t[:, lanes].T
            prod = c_s[j, rows, :].T.astype(F32) * out_t[:, lanes].astype(F32)
            deltas.append(jnp.sum(prod, axis=0, keepdims=True))
        delta = jnp.concatenate(deltas, axis=1)
        de[j, :, cols] = delta
        for b in range(QUARTERS):
            rows = pl.ds(b * D, D)
            dss[j, rows, cols] = ((sp[rows, wide] * inverse) * (dpp[rows, wide] - delta)).astype(BF16)

    def own_terms(j):
        for at, width in TILES:
            cols = pl.ds(at, width)
            for b in range(QUARTERS):
                rows = pl.ds(b * D, D)
                dss[j, pl.ds((4 + b) * D, D), cols] = (
                    (po[j, rows, cols] * fo[j, :, cols]) * (dpo[j, rows, cols] - de[j, :, cols])
                ).astype(BF16)
        key_terms(j, 4)
        own_reduce1(j)

    def key_terms(j, first):
        rows = pl.ds(first * D, 4 * D)
        g[j, first : first + 4, 0] = (nn(dss[j, rows, :], q_s[j]) * SCALE).reshape(4, D, D)
        g[j, first : first + 4, 1] = nn(ps[j, rows, :], c_s[j]).reshape(4, D, D)

    def query_part(j):
        for b in range(2 * QUARTERS):
            vt[:, pl.ds(b * D, D)] = kv[j, b, 0].T
        for at, width in TILES:
            grad_t = (nn(vt[...], dss[j, :, pl.ds(at, width)]) * SCALE).astype(BF16)
            for i in range(width // D):
                dq_s[j, pl.ds(at + i * D, D), :] = grad_t[:, i * D : i * D + D].T
        take_out(dq_s, dq_hbm, 1, j)

    def hop(send, arrive, i, j, target):
        return remote(send.at[j], arrive.at[j], ss.at[i, j], rs.at[i, j], target)

    def own1(j):
        return hop(so1, ro1, 0, j, device(partners(x, j)[0], y, z, core))

    def own2(j):
        return hop(so2, ro2, 1, j, device(partners(x, j)[1], y, z, core))

    def pair(j):
        return hop(sc, rc, 2, j, device(x, y, z, 1 - core))

    def across(j, i):
        return remote(sp1.at[j, i], rp1.at[j, i], s_a.at[j, i], r_a.at[j, i], device(others(x)[i], y, z, core))

    def to_column(j, n):
        return remote(sz.at[j], rz.at[j, n - 1], s_z.at[j], r_z.at[j, n - 1], device(x, y, 0, core))

    def to_root(j, t, n):
        return remote(sy.at[j], ry.at[j, t, n], s_y.at[j], r_y.at[j, t, n], device(x, 0, 0, 0))

    def reduce0(j):
        for b in range(QUARTERS):
            sc[j, b] = g[j, b, 1 - core].astype(BF16)
        pair(j).start()

    def own_reduce1(j):
        pa, pb = partners(x, j)
        so1[j, 0] = g[j, 4 + pa].astype(BF16)
        so1[j, 1] = g[j, 4 + opp].astype(BF16)
        own1(j).start()

    def reduce1(j):
        pair(j).wait_recv()
        for b in range(QUARTERS):
            gs[j, b] = g[j, b, core] + rc[j, b].astype(F32)
        for i in (2, 0, 1):
            sp1[j, i] = gs[j, others(x)[i]].astype(BF16)
            across(j, i).start()

    def own_reduce2(j):
        pa, pb = partners(x, j)
        own1(j).wait_recv()
        so2[j] = (g[j, 4 + pb] + ro1[j, 1].astype(F32)).astype(BF16)
        own2(j).start()

    def reduce3(j):
        total = gs[j, x]
        for i in range(3):
            across(j, i).wait_recv()
            total = total + rp1[j, i].astype(F32)
        part[j] = total
        sz[j] = total.astype(BF16)

        @pl.when(z != 0)
        def _():
            to_column(j, z).start()

    def reduce4(j):
        @pl.when(z == 0)
        def _():
            total = part[j]
            for n in range(1, NZ):
                to_column(j, n).wait_recv()
                total = total + rz[j, n - 1].astype(F32)
            part[j] = total
            sy[j] = total.astype(BF16)

            @pl.when((y != 0) | (core == 1))
            def _():
                to_root(j, core, y).start()

    def own_result(j):
        own2(j).wait_recv()
        cols = pl.ds(j * D, D)
        total = g[j, 4 + x] + ro1[j, 0].astype(F32) + ro2[j].astype(F32)
        g[j, 4 + x] = total
        dk_ref[:, cols] = total[0].astype(BF16)
        dv_ref[:, cols] = total[1].astype(BF16)

    def root_result(j):
        @pl.when(is_root)
        def _():
            cols = pl.ds(j * D, D)
            total = g[j, 4 + x, 0] + part[j]
            for n in range(1, NY):
                to_root(j, 0, n).wait_recv()
                total = total + ry[j, 0, n].astype(F32)
            dk_ref[:, cols] = total.astype(BF16)
            total = g[j, 4 + x, 1]
            for n in range(NY):
                to_root(j, 1, n).wait_recv()
                total = total + ry[j, 1, n].astype(F32)
            dv_ref[:, cols] = total.astype(BF16)

    for j in range(HEADS):
        relay(j)
    prompt1(0)
    own_part(0)
    prompt1(1)
    own_part(1)
    prompt1(2)
    own_part(2)
    prompt3(0)
    own_part(3)
    prompt1(3)
    between = {
        (0, 0): lambda: prompt3(1),
        (0, 2): lambda: prompt3(2),
        (1, 0): lambda: prompt3(3),
        (1, 2): lambda: reduce1(0),
        (2, 1): lambda: reduce1(1),
        (2, 3): lambda: reduce3(0),
        (3, 1): lambda: reduce1(2),
        (3, 3): lambda: reduce3(1),
    }
    for j in range(HEADS):
        prompt_here(j)
        flip_values(j)
        for i, (at, width) in enumerate(TILES):
            prompt_part(j, at, width)
            between.get((j, i), lambda: None)()
        key_terms(j, 0)
        reduce0(j)
        take_out(att_s, att_hbm, 0, j)
    own_terms(0)
    reduce1(3)
    own_terms(1)
    reduce3(2)
    own_terms(2)
    own_terms(3)
    reduce3(3)
    reduce4(0)
    own_reduce2(0)
    query_part(0)
    reduce4(1)
    own_reduce2(1)
    query_part(1)
    reduce4(2)
    own_reduce2(2)
    query_part(2)
    own_reduce2(3)
    query_part(3)
    own_result(0)
    own_result(1)
    reduce4(3)
    own_result(2)
    own_result(3)
    for j in range(HEADS):
        root_result(j)

    for j in range(HEADS):
        for i in range(3):
            x_send(j, 4, s_own, r_own, i).wait_send()

        @pl.when(core == 0)
        def _():
            for i in range(3):
                p_send(j, i).wait_send()
            core_send(j).wait_send()

        @pl.when(column)
        def _():
            for n in (2, 6, 1, 7):
                z_send(j, n).wait_send()

        @pl.when(leaf & (z == 2))
        def _():
            z_send(j, 4).wait_send()
            z_send(j, 3).wait_send()

        @pl.when(leaf & (z == 6))
        def _():
            z_send(j, 5).wait_send()

        @pl.when(is_root)
        def _():
            for n in range(1, NY):
                y_send(j, n).wait_send()

        for copy in (own1(j), own2(j), pair(j), across(j, 0), across(j, 1), across(j, 2)):
            copy.wait_send()

        @pl.when(z != 0)
        def _():
            to_column(j, z).wait_send()

        @pl.when((z == 0) & ((y != 0) | (core == 1)))
        def _():
            to_root(j, core, y).wait_send()

        pltpu.make_async_copy(att_s.at[j], att_s.at[j], osem.at[0, j]).wait()
        pltpu.make_async_copy(dq_s.at[j], dq_s.at[j], osem.at[1, j]).wait()


def main(mask, k, v, q, c):
    dma, vmem = pltpu.SemaphoreType.DMA, pltpu.VMEM
    block = (D, D)
    wide = jax.ShapeDtypeStruct(q.shape, BF16)
    narrow = jax.ShapeDtypeStruct(k.shape, BF16)
    here = pl.BlockSpec(memory_space=pltpu.VMEM)
    there = pl.BlockSpec(memory_space=pl.ANY)
    return pl.pallas_call(
        main_kernel,
        out_shape=(wide, wide, narrow, narrow),
        in_specs=[pl.BlockSpec(memory_space=pltpu.SMEM), there, there, there, there],
        out_specs=(there, there, here, here),
        scratch_shapes=[
            vmem((HEADS, 8, 2) + block, BF16),
            vmem((HEADS, WIDE, D), BF16),
            vmem((HEADS, WIDE, D), BF16),
            vmem((HEADS, WIDE, D), BF16),
            vmem((HEADS, WIDE, D), BF16),
            vmem((4 * D, 2 * D), F32),
            vmem((HEADS, 4 * D, WIDE), F32),
            vmem((HEADS, 4 * D, WIDE), F32),
            vmem((HEADS, 1, WIDE), F32),
            vmem((HEADS, 1, WIDE), F32),
            vmem((HEADS, 1, WIDE), F32),
            vmem((HEADS, 1, WIDE), F32),
            vmem((4 * D, 2 * D), F32),
            vmem((4 * D, 2 * D), F32),
            vmem((HEADS, 8 * D, WIDE), BF16),
            vmem((HEADS, 8 * D, WIDE), BF16),
            vmem((D, 8 * D), BF16),
            vmem((HEADS, 8, 2) + block, F32),
            vmem((HEADS, 2, 2) + block, BF16),
            vmem((HEADS, 2, 2) + block, BF16),
            vmem((HEADS, 2) + block, BF16),
            vmem((HEADS, 2) + block, BF16),
            vmem((HEADS, 4) + block, BF16),
            vmem((HEADS, 4) + block, BF16),
            vmem((HEADS, 4) + block, F32),
            vmem((HEADS, 3) + block, BF16),
            vmem((HEADS, 3) + block, BF16),
            vmem((HEADS,) + block, F32),
            vmem((HEADS,) + block, BF16),
            vmem((HEADS, NZ - 1) + block, BF16),
            vmem((HEADS,) + block, BF16),
            vmem((HEADS, 2, NY) + block, BF16),
            dma((2, HEADS, 2)),
            dma((2, HEADS)),
            dma((2, HEADS)),
            dma((HEADS, 3)),
            dma((HEADS, 3)),
            dma((HEADS, 3)),
            dma((HEADS, 3)),
            dma((HEADS, NY - 1)),
            dma((HEADS, NZ - 1)),
            dma((HEADS,)),
            dma((HEADS,)),
            dma((HEADS,)),
            dma((3, HEADS)),
            dma((3, HEADS)),
            dma((HEADS, 3)),
            dma((HEADS, 3)),
            dma((HEADS,)),
            dma((HEADS, 2, NY)),
            dma((HEADS,)),
            dma((HEADS, NZ - 1)),
        ],
        compiler_params=pltpu.CompilerParams(
            collective_id=0, has_side_effects=True, vmem_limit_bytes=60 * 2**20
        ),
        name="tree_attention",
    )(mask, k, v, q, c)


PIECES = 2


def hand_on_kernel(*refs):
    arrays, outs, held, (came, went) = refs[:4], refs[4:8], refs[8:12], refs[12:]

    def copies(i, p):
        rows = pl.ds(p * (D // PIECES), D // PIECES)
        inner = held[i].at[rows]
        return (
            pltpu.make_async_copy(arrays[i].at[rows], inner, came.at[i, p]),
            pltpu.make_async_copy(inner, outs[i].at[rows], went.at[i, p]),
        )

    order = [(i, p) for i in (2, 3, 0, 1) for p in range(PIECES)]
    for at in order:
        copies(*at)[0].start()
    for at in order:
        copies(*at)[0].wait()
        copies(*at)[1].start()
    for at in order:
        copies(*at)[1].wait()


def hand_on(arrays):
    there = pl.BlockSpec(memory_space=pl.ANY)
    return pl.pallas_call(
        hand_on_kernel,
        out_shape=[jax.ShapeDtypeStruct(a.shape, a.dtype) for a in arrays],
        in_specs=[there] * 4,
        out_specs=[there] * 4,
        scratch_shapes=[pltpu.VMEM(a.shape, a.dtype) for a in arrays]
        + [pltpu.SemaphoreType.DMA((4, PIECES))] * 2,
        name="hand_on",
    )(*arrays)


def on_device(queries, rotated_key_rows, value_matrix, cotangent, tree_mask):
    return tuple(hand_on(main(tree_mask, rotated_key_rows, value_matrix, queries, cotangent)))


def solution(mesh):
    rows = P(("seq", "head"), None)
    return jax.shard_map(
        on_device,
        mesh=mesh,
        in_specs=(rows, rows, rows, rows, P("seq", None)),
        out_specs=(rows, rows, rows, rows),
        check_vma=False,
    )
```

```python
import jax
import jax.numpy as jnp
from jax import lax
from jax.experimental import pallas as pl
from jax.experimental.pallas import tpu as pltpu
from jax.sharding import PartitionSpec as P

HEADS = 4
GROUP = 7
D = 128
QUARTERS = 4
NY, NZ = 4, 8
SCALE = D ** (-0.5)
LOG2E = 1.4426950408889634
MESH = pl.DeviceIdType.MESH
BF16 = jnp.bfloat16
F32 = jnp.float32


def place():
    seq = lax.axis_index("seq")
    x = lax.axis_index("head")
    return x, seq // (2 * NZ), (seq // 2) % NZ, seq % 2


def device(x, y, z, core):
    return ((y * NZ + z) * 2 + core, x)


def remote(src, dst, send_sem, recv_sem, target):
    return pltpu.make_async_remote_copy(
        src_ref=src,
        dst_ref=dst,
        send_sem=send_sem,
        recv_sem=recv_sem,
        device_id=target,
        device_id_type=MESH,
    )


def partners(x, j):
    flip, mirror = x + 1 - 2 * (x % 2), 3 - x
    return (flip, mirror) if j % 2 == 0 else (mirror, flip)


def others(x):
    return (x + 1 - 2 * (x % 2), 3 - x, (x + 2) % 4)


def say_hello(x, y, z, core):
    sem = pltpu.get_barrier_semaphore()

    def signal(condition, targets):
        @pl.when(condition)
        def _():
            for target in targets:
                pl.semaphore_signal(sem, inc=1, device_id=target, device_id_type=MESH)

    first = core == 0
    signal((z == 0) & (y == 0) & first, [device(x, n, 0, c) for n in (2, 1, 3) for c in (0, 1)])
    signal(z == 0, [device(x, y, n, core) for n in (4, 3, 5, 2, 6, 1, 7)])
    signal((z == 0) & (y != 0), [device(x, 0, 0, 0)])
    signal(z != 0, [device(x, y, 0, core)])
    signal((z == 2) & first, [device(x, y, 3, 0), device(x, y, 4, 0)])
    signal((z == 6) & first, [device(x, y, 5, 0)])
    signal(((z == 3) | (z == 4)) & first, [device(x, y, 2, 0)])
    signal((z == 5) & first, [device(x, y, 6, 0)])
    signal(z >= 0, [device(n, y, z, core) for n in others(x)] + [device(x, y, z, 1 - core)])


def hear_all(x, y, z, core):
    sem = pltpu.get_barrier_semaphore()
    first = core == 0
    end = (z == 1) | (z == 7)
    for role, peers in (
        ((z == 0) & (y == 0) & first, 17),
        ((z == 0) & (y == 0) & ~first, 11),
        ((z == 0) & (y != 0), 12),
        ((z != 0) & (~first | end), 5),
        ((z == 2) & first, 7),
        ((z != 0) & (z != 2) & ~end & first, 6),
    ):
        @pl.when(role)
        def _():
            pl.semaphore_wait(sem, peers)


TILES = ((0, 256), (256, 256), (512, 256), (768, 128))
WIDE = GROUP * D
EXP_SCALE = SCALE * LOG2E


def nt(a, b):
    return lax.dot_general(a, b, (((1,), (1,)), ((), ())), preferred_element_type=F32)


def nn(a, b):
    return lax.dot_general(a, b, (((1,), (0,)), ((), ())), preferred_element_type=F32)


def fold_max(a):
    return jnp.max(a.reshape(D // 8, 8, a.shape[1]), axis=0)


def fold_sum(a):
    return jnp.sum(a.reshape(D // 8, 8, a.shape[1]), axis=0)


def main_kernel(
    mask_ref, k_ref, v_ref, q_hbm, c_hbm,
    att_hbm, dq_hbm, dk_ref, dv_ref,
    kv, q_s, c_s, att_s, dq_s, bias, po, dpo, mo, lo, fo, de, sp, dpp, ps, dss, vt,
    g, so1, ro1, so2, ro2, sc, rc, gs, sp1, rp1, part, sz, rz, sy, ry,
    lsem, qsem, osem, s_own, r_own, s_pr, r_pr, s_by, s_bz, r_t, s_c, r_c,
    ss, rs, s_a, r_a, s_y, r_y, s_z, r_z,
):
    x, y, z, core = place()
    opp = (x + 2) % 4
    seq = lax.axis_index("seq")
    top_row = (z == 0) & (y == 0)
    is_root = top_row & (core == 0)
    column = (core == 0) & (z == 0)
    leaf = (core == 0) & (z != 0)

    say_hello(x, y, z, core)

    def local(j, block, base):
        return [
            pltpu.make_async_copy(ref.at[:, pl.ds(j * D, D)], kv.at[j, block, t], lsem.at[base, j, t])
            for t, ref in enumerate((k_ref, v_ref))
        ]

    @pl.when(is_root)
    def _():
        for j in range(HEADS):
            for copy in local(j, x, 1):
                copy.start()

    for j in range(HEADS):
        for copy in local(j, 4 + x, 0):
            copy.start()

    def take_out(buf, hbm, i, j):
        for h in range(GROUP):
            cols, rows = pl.ds((j * GROUP + h) * D, D), pl.ds(h * D, D)
            pltpu.make_async_copy(buf.at[j, rows], hbm.at[:, cols], osem.at[i, j]).start()

    hear_all(x, y, z, core)

    def y_send(j, n):
        blk = kv.at[j, x]
        return remote(blk, blk, s_by.at[j, n - 1], r_t.at[j], device(x, n, 0, 0))

    def z_send(j, n):
        blk = kv.at[j, x]
        return remote(blk, blk, s_bz.at[j, n - 1], r_t.at[j], device(x, y, n, 0))

    def children(j):
        return (4, 5, 3, 6, 2, 7, 1) if j == 0 else (2, 6, 1, 7)

    def pass_on(j):
        for n in children(j):
            z_send(j, n).start()

    def x_send(j, base, ss, rs, i):
        pa, pb = partners(x, j)
        blk = kv.at[j, base + (x, x, pa)[i]]
        return remote(blk, blk, ss.at[j, i], rs.at[j, i], device((pa, pb, pb)[i], y, z, core))

    def x_arrival(j, base, ss, rs, i):
        pa, pb = partners(x, j)
        blk = kv.at[j, base + (pa, pb, opp)[i]]
        remote(blk, blk, ss.at[j, i], rs.at[j, i], device((pa, pb, pb)[i], y, z, core)).wait_recv()

    def p_send(j, i):
        blk = kv.at[j, x]
        return remote(blk, blk, s_pr.at[j, i], r_pr.at[j, i], device(others(x)[i], y, z, core))

    def core_send(j, i):
        blk = kv.at[j, x if i == 3 else others(x)[i]]
        return remote(blk, blk, s_c.at[j, i], r_c.at[j, i], device(x, y, z, 1 - core))

    def spread(j):
        for i in (2, 0, 1):
            p_send(j, i).start()
        core_send(j, 3).start()

    @pl.when(is_root)
    def _():
        for j in range(HEADS):
            for copy in local(j, x, 1):
                copy.wait()
            for n in (2, 1, 3):
                y_send(j, n).start()
            pass_on(j)
            spread(j)

    for j in range(HEADS):
        for copy in local(j, 4 + x, 0):
            copy.wait()
        x_send(j, 4, s_own, r_own, 0).start()
        x_send(j, 4, s_own, r_own, 1).start()

    for j in range(HEADS):
        for h in range(GROUP):
            cols, rows = pl.ds((j * GROUP + h) * D, D), pl.ds(h * D, D)
            pltpu.make_async_copy(q_hbm.at[:, cols], q_s.at[j, rows], qsem.at[0, j]).start()
            pltpu.make_async_copy(c_hbm.at[:, cols], c_s.at[j, rows], qsem.at[1, j]).start()

    key = lax.broadcasted_iota(jnp.int32, (D, D), 0)
    query = lax.broadcasted_iota(jnp.int32, (D, D), 1)
    for b in range(QUARTERS):
        seen = key + b * D <= query + x * D
        tile = jnp.where(seen, 0.0, -1e30).astype(F32)
        bias[pl.ds(b * D, D), pl.ds(0, D)] = tile
        bias[pl.ds(b * D, D), pl.ds(D, D)] = tile
    levels = []
    for b in range(QUARTERS):
        reads = jnp.where(seq > 0, mask_ref[x, b], 0)
        levels.append(jnp.where(reads > 0, 0.0, -1e30).astype(F32))

    def relay(j):
        @pl.when(column & (y != 0))
        def _():
            y_send(j, y).wait_recv()
            pass_on(j)
            spread(j)

        x_arrival(j, 4, s_own, r_own, 0)
        x_send(j, 4, s_own, r_own, 2).start()

    def prompt1(j, here):
        @pl.when(here)
        def _():
            z_send(j, z).wait_recv()
            if j > 0:
                @pl.when(z == 2)
                def _():
                    z_send(j, 4).start()
                    z_send(j, 3).start()

                @pl.when(z == 6)
                def _():
                    z_send(j, 5).start()

            spread(j)

    def prompt3(j):
        @pl.when(core == 0)
        def _():
            for i in (0, 1, 2):
                blk = kv.at[j, others(x)[i]]
                remote(blk, blk, s_pr.at[j, i], r_pr.at[j, i], device(others(x)[i], y, z, core)).wait_recv()
                core_send(j, i).start()

    def prompt_here(j):
        @pl.when(core == 1)
        def _():
            for i in range(4):
                core_send(j, i).wait_recv()

    def own_part(j):
        x_arrival(j, 4, s_own, r_own, 1)
        x_arrival(j, 4, s_own, r_own, 2)
        pltpu.make_async_copy(q_s.at[j], q_s.at[j], qsem.at[0, j]).wait()
        pltpu.make_async_copy(c_s.at[j], c_s.at[j], qsem.at[1, j]).wait()
        for at, width in TILES:
            cols = pl.ds(at, width)
            keys = kv[j, 4:8, 0].reshape(4 * D, D)
            values = kv[j, 4:8, 1].reshape(4 * D, D)
            po[j, :, cols] = nt(keys, q_s[j, cols, :]) + bias[:, pl.ds(0, width)]
            top = None
            for b in range(QUARTERS):
                part_top = fold_max(po[j, pl.ds(b * D, D), cols])
                top = part_top if top is None else jnp.maximum(top, part_top)
            top = jnp.max(top, axis=0, keepdims=True)
            total = None
            for b in range(QUARTERS):
                p = jnp.exp2((po[j, pl.ds(b * D, D), cols] - top) * EXP_SCALE)
                po[j, pl.ds(b * D, D), cols] = p
                part_sum = fold_sum(p)
                total = part_sum if total is None else total + part_sum
            mo[j, :, cols] = top
            lo[j, :, cols] = jnp.sum(total, axis=0, keepdims=True)
            dpo[j, :, cols] = nt(values, c_s[j, cols, :])

    def flip_values(j):
        for b in range(2 * QUARTERS):
            vt[:, pl.ds(b * D, D)] = kv[j, b, 1].T

    def prompt_part(j, at, width):
        cols, wide = pl.ds(at, width), pl.ds(0, width)
        c = c_s[j, cols, :]
        sp[:, wide] = nt(kv[j, 0:4, 0].reshape(4 * D, D), q_s[j, cols, :])
        dpp[:, wide] = nt(kv[j, 0:4, 1].reshape(4 * D, D), c)
        own_top = mo[j, :, cols]
        top = None
        for b in range(QUARTERS):
            part_top = fold_max(sp[pl.ds(b * D, D), wide]) + levels[b]
            top = part_top if top is None else jnp.maximum(top, part_top)
        top = jnp.maximum(own_top, jnp.max(top, axis=0, keepdims=True))
        shrink = jnp.exp2((own_top - top) * EXP_SCALE)
        total = None
        for b in range(QUARTERS):
            rows = pl.ds(b * D, D)
            p = jnp.exp2((sp[rows, wide] - (top - levels[b])) * EXP_SCALE)
            sp[rows, wide] = p
            part_sum = fold_sum(p)
            total = part_sum if total is None else total + part_sum
        total = jnp.sum(total, axis=0, keepdims=True) + lo[j, :, cols] * shrink
        inverse = 1.0 / total
        shrink = shrink * inverse
        fo[j, :, cols] = shrink
        for b in range(QUARTERS):
            rows = pl.ds(b * D, D)
            ps[j, rows, cols] = (sp[rows, wide] * inverse).astype(BF16)
            ps[j, pl.ds((4 + b) * D, D), cols] = (po[j, rows, cols] * shrink).astype(BF16)
        out_t = nn(vt[...], ps[j, :, cols]).astype(BF16)
        deltas = []
        for i in range(width // D):
            lanes, rows = slice(i * D, i * D + D), pl.ds(at + i * D, D)
            att_s[j, rows, :] = out_t[:, lanes].T
            prod = c_s[j, rows, :].T.astype(F32) * out_t[:, lanes].astype(F32)
            deltas.append(jnp.sum(prod, axis=0, keepdims=True))
        delta = jnp.concatenate(deltas, axis=1)
        de[j, :, cols] = delta
        for b in range(QUARTERS):
            rows = pl.ds(b * D, D)
            dss[j, rows, cols] = ((sp[rows, wide] * inverse) * (dpp[rows, wide] - delta)).astype(BF16)

    def own_terms(j):
        for at, width in TILES:
            cols = pl.ds(at, width)
            for b in range(QUARTERS):
                rows = pl.ds(b * D, D)
                dss[j, pl.ds((4 + b) * D, D), cols] = (
                    (po[j, rows, cols] * fo[j, :, cols]) * (dpo[j, rows, cols] - de[j, :, cols])
                ).astype(BF16)
        key_terms(j, 4)

    def key_terms(j, first):
        rows = pl.ds(first * D, 4 * D)
        g[j, first : first + 4, 0] = (nn(dss[j, rows, :], q_s[j]) * SCALE).reshape(4, D, D)
        g[j, first : first + 4, 1] = nn(ps[j, rows, :], c_s[j]).reshape(4, D, D)

    def query_part(j):
        for b in range(2 * QUARTERS):
            vt[:, pl.ds(b * D, D)] = kv[j, b, 0].T
        for at, width in TILES:
            grad_t = (nn(vt[...], dss[j, :, pl.ds(at, width)]) * SCALE).astype(BF16)
            for i in range(width // D):
                dq_s[j, pl.ds(at + i * D, D), :] = grad_t[:, i * D : i * D + D].T
        take_out(dq_s, dq_hbm, 1, j)

    def hop(send, arrive, i, j, target):
        return remote(send.at[j], arrive.at[j], ss.at[i, j], rs.at[i, j], target)

    def own1(j):
        return hop(so1, ro1, 0, j, device(partners(x, j)[0], y, z, core))

    def own2(j):
        return hop(so2, ro2, 1, j, device(partners(x, j)[1], y, z, core))

    def pair(j):
        return hop(sc, rc, 2, j, device(x, y, z, 1 - core))

    def across(j, i):
        return remote(sp1.at[j, i], rp1.at[j, i], s_a.at[j, i], r_a.at[j, i], device(others(x)[i], y, z, core))

    def to_column(j, n):
        return remote(sz.at[j], rz.at[j, n - 1], s_z.at[j], r_z.at[j, n - 1], device(x, y, 0, core))

    def to_root(j, t, n):
        return remote(sy.at[j], ry.at[j, t, n], s_y.at[j], r_y.at[j, t, n], device(x, 0, 0, 0))

    def reduce0(j):
        for b in range(QUARTERS):
            sc[j, b] = g[j, b, 1 - core].astype(BF16)
        pair(j).start()

    def own_reduce1(j):
        pa, pb = partners(x, j)
        so1[j, 0] = g[j, 4 + pa].astype(BF16)
        so1[j, 1] = g[j, 4 + opp].astype(BF16)
        own1(j).start()

    def reduce1(j):
        pair(j).wait_recv()
        for b in range(QUARTERS):
            gs[j, b] = g[j, b, core] + rc[j, b].astype(F32)
        for i in (2, 0, 1):
            sp1[j, i] = gs[j, others(x)[i]].astype(BF16)
            across(j, i).start()

    def own_reduce2(j):
        pa, pb = partners(x, j)
        own1(j).wait_recv()
        so2[j] = (g[j, 4 + pb] + ro1[j, 1].astype(F32)).astype(BF16)
        own2(j).start()

    def reduce3(j):
        total = gs[j, x]
        for i in range(3):
            across(j, i).wait_recv()
            total = total + rp1[j, i].astype(F32)
        part[j] = total
        sz[j] = total.astype(BF16)

        @pl.when(z != 0)
        def _():
            to_column(j, z).start()

    def reduce4(j):
        @pl.when(z == 0)
        def _():
            total = part[j]
            for n in range(1, NZ):
                to_column(j, n).wait_recv()
                total = total + rz[j, n - 1].astype(F32)
            part[j] = total
            sy[j] = total.astype(BF16)

            @pl.when((y != 0) | (core == 1))
            def _():
                to_root(j, core, y).start()

    def own_result(j):
        own2(j).wait_recv()
        cols = pl.ds(j * D, D)
        total = g[j, 4 + x] + ro1[j, 0].astype(F32) + ro2[j].astype(F32)
        g[j, 4 + x] = total
        dk_ref[:, cols] = total[0].astype(BF16)
        dv_ref[:, cols] = total[1].astype(BF16)

    def root_result(j):
        @pl.when(is_root)
        def _():
            cols = pl.ds(j * D, D)
            total = g[j, 4 + x, 0] + part[j]
            for n in range(1, NY):
                to_root(j, 0, n).wait_recv()
                total = total + ry[j, 0, n].astype(F32)
            dk_ref[:, cols] = total.astype(BF16)
            total = g[j, 4 + x, 1]
            for n in range(NY):
                to_root(j, 1, n).wait_recv()
                total = total + ry[j, 1, n].astype(F32)
            dv_ref[:, cols] = total.astype(BF16)

    near = leaf & ((z < 3) | (z > 5))
    far = leaf & (z > 2) & (z < 6)
    relay(0)
    relay(1)
    prompt1(0, near)
    relay(2)
    relay(3)
    prompt1(0, far)
    prompt1(1, near)
    own_part(0)
    prompt1(1, far)
    prompt1(2, near)
    own_part(1)
    prompt1(2, far)
    prompt1(3, near)
    own_part(2)
    prompt3(0)
    own_part(3)
    prompt1(3, far)
    between = {
        (0, 0): lambda: prompt3(1),
        (0, 2): lambda: prompt3(2),
        (1, 0): lambda: prompt3(3),
        (1, 2): lambda: reduce1(0),
        (2, 1): lambda: reduce1(1),
        (2, 3): lambda: reduce3(0),
        (3, 1): lambda: reduce1(2),
        (3, 3): lambda: reduce3(1),
    }
    for j in range(HEADS):
        prompt_here(j)
        flip_values(j)
        for i, (at, width) in enumerate(TILES):
            prompt_part(j, at, width)
            between.get((j, i), lambda: None)()
        key_terms(j, 0)
        reduce0(j)
        take_out(att_s, att_hbm, 0, j)
    own_terms(0)
    reduce1(3)
    own_reduce1(0)
    reduce3(2)
    own_terms(1)
    own_reduce1(1)
    own_terms(2)
    own_reduce1(2)
    reduce4(0)
    own_terms(3)
    reduce3(3)
    own_reduce1(3)
    own_reduce2(0)
    reduce4(1)
    query_part(0)
    own_reduce2(1)
    reduce4(2)
    query_part(1)
    own_reduce2(2)
    query_part(2)
    query_part(3)
    reduce4(3)
    own_reduce2(3)
    own_result(0)
    own_result(1)
    own_result(2)
    own_result(3)
    for j in range(HEADS):
        root_result(j)

    for j in range(HEADS):
        for i in range(3):
            x_send(j, 4, s_own, r_own, i).wait_send()

        @pl.when(core == 0)
        def _():
            for i in range(3):
                p_send(j, i).wait_send()
            for i in range(4):
                core_send(j, i).wait_send()

        @pl.when(column)
        def _():
            for n in children(j):
                z_send(j, n).wait_send()

        if j > 0:
            @pl.when(leaf & (z == 2))
            def _():
                z_send(j, 4).wait_send()
                z_send(j, 3).wait_send()

            @pl.when(leaf & (z == 6))
            def _():
                z_send(j, 5).wait_send()

        @pl.when(is_root)
        def _():
            for n in range(1, NY):
                y_send(j, n).wait_send()

        for copy in (own1(j), own2(j), pair(j), across(j, 0), across(j, 1), across(j, 2)):
            copy.wait_send()

        @pl.when(z != 0)
        def _():
            to_column(j, z).wait_send()

        @pl.when((z == 0) & ((y != 0) | (core == 1)))
        def _():
            to_root(j, core, y).wait_send()

        pltpu.make_async_copy(att_s.at[j], att_s.at[j], osem.at[0, j]).wait()
        pltpu.make_async_copy(dq_s.at[j], dq_s.at[j], osem.at[1, j]).wait()


def main(mask, k, v, q, c):
    dma, vmem = pltpu.SemaphoreType.DMA, pltpu.VMEM
    block = (D, D)
    wide = jax.ShapeDtypeStruct(q.shape, BF16)
    narrow = jax.ShapeDtypeStruct(k.shape, BF16)
    here = pl.BlockSpec(memory_space=pltpu.VMEM)
    there = pl.BlockSpec(memory_space=pl.ANY)
    return pl.pallas_call(
        main_kernel,
        out_shape=(wide, wide, narrow, narrow),
        in_specs=[pl.BlockSpec(memory_space=pltpu.SMEM), there, there, there, there],
        out_specs=(there, there, here, here),
        scratch_shapes=[
            vmem((HEADS, 8, 2) + block, BF16),
            vmem((HEADS, WIDE, D), BF16),
            vmem((HEADS, WIDE, D), BF16),
            vmem((HEADS, WIDE, D), BF16),
            vmem((HEADS, WIDE, D), BF16),
            vmem((4 * D, 2 * D), F32),
            vmem((HEADS, 4 * D, WIDE), F32),
            vmem((HEADS, 4 * D, WIDE), F32),
            vmem((HEADS, 1, WIDE), F32),
            vmem((HEADS, 1, WIDE), F32),
            vmem((HEADS, 1, WIDE), F32),
            vmem((HEADS, 1, WIDE), F32),
            vmem((4 * D, 2 * D), F32),
            vmem((4 * D, 2 * D), F32),
            vmem((HEADS, 8 * D, WIDE), BF16),
            vmem((HEADS, 8 * D, WIDE), BF16),
            vmem((D, 8 * D), BF16),
            vmem((HEADS, 8, 2) + block, F32),
            vmem((HEADS, 2, 2) + block, BF16),
            vmem((HEADS, 2, 2) + block, BF16),
            vmem((HEADS, 2) + block, BF16),
            vmem((HEADS, 2) + block, BF16),
            vmem((HEADS, 4) + block, BF16),
            vmem((HEADS, 4) + block, BF16),
            vmem((HEADS, 4) + block, F32),
            vmem((HEADS, 3) + block, BF16),
            vmem((HEADS, 3) + block, BF16),
            vmem((HEADS,) + block, F32),
            vmem((HEADS,) + block, BF16),
            vmem((HEADS, NZ - 1) + block, BF16),
            vmem((HEADS,) + block, BF16),
            vmem((HEADS, 2, NY) + block, BF16),
            dma((2, HEADS, 2)),
            dma((2, HEADS)),
            dma((2, HEADS)),
            dma((HEADS, 3)),
            dma((HEADS, 3)),
            dma((HEADS, 3)),
            dma((HEADS, 3)),
            dma((HEADS, NY - 1)),
            dma((HEADS, NZ - 1)),
            dma((HEADS,)),
            dma((HEADS, 4)),
            dma((HEADS, 4)),
            dma((3, HEADS)),
            dma((3, HEADS)),
            dma((HEADS, 3)),
            dma((HEADS, 3)),
            dma((HEADS,)),
            dma((HEADS, 2, NY)),
            dma((HEADS,)),
            dma((HEADS, NZ - 1)),
        ],
        compiler_params=pltpu.CompilerParams(
            collective_id=0, has_side_effects=True, vmem_limit_bytes=60 * 2**20
        ),
        name="tree_attention",
    )(mask, k, v, q, c)


PIECES = 2


def hand_on_kernel(*refs):
    arrays, outs, held, (came, went) = refs[:4], refs[4:8], refs[8:12], refs[12:]

    def copies(i, p):
        rows = pl.ds(p * (D // PIECES), D // PIECES)
        inner = held[i].at[rows]
        return (
            pltpu.make_async_copy(arrays[i].at[rows], inner, came.at[i, p]),
            pltpu.make_async_copy(inner, outs[i].at[rows], went.at[i, p]),
        )

    order = [(i, p) for i in (2, 3, 0, 1) for p in range(PIECES)]
    for at in order:
        copies(*at)[0].start()
    for at in order:
        copies(*at)[0].wait()
        copies(*at)[1].start()
    for at in order:
        copies(*at)[1].wait()


def hand_on(arrays):
    there = pl.BlockSpec(memory_space=pl.ANY)
    return pl.pallas_call(
        hand_on_kernel,
        out_shape=[jax.ShapeDtypeStruct(a.shape, a.dtype) for a in arrays],
        in_specs=[there] * 4,
        out_specs=[there] * 4,
        scratch_shapes=[pltpu.VMEM(a.shape, a.dtype) for a in arrays]
        + [pltpu.SemaphoreType.DMA((4, PIECES))] * 2,
        name="hand_on",
    )(*arrays)


def on_device(queries, rotated_key_rows, value_matrix, cotangent, tree_mask):
    return tuple(hand_on(main(tree_mask, rotated_key_rows, value_matrix, queries, cotangent)))


def solution(mesh):
    rows = P(("seq", "head"), None)
    return jax.shard_map(
        on_device,
        mesh=mesh,
        in_specs=(rows, rows, rows, rows, P("seq", None)),
        out_specs=(rows, rows, rows, rows),
        check_vma=False,
    )
```

```python
import jax
import jax.numpy as jnp
from jax import lax
from jax.experimental import pallas as pl
from jax.experimental.pallas import tpu as pltpu
from jax.sharding import PartitionSpec as P

HEADS = 4
GROUP = 7
D = 128
QUARTERS = 4
NY, NZ = 4, 8
SCALE = D ** (-0.5)
LOG2E = 1.4426950408889634
MESH = pl.DeviceIdType.MESH
BF16 = jnp.bfloat16
F32 = jnp.float32


def place():
    seq = lax.axis_index("seq")
    x = lax.axis_index("head")
    return x, seq // (2 * NZ), (seq // 2) % NZ, seq % 2


def device(x, y, z, core):
    return ((y * NZ + z) * 2 + core, x)


def remote(src, dst, send_sem, recv_sem, target):
    return pltpu.make_async_remote_copy(
        src_ref=src,
        dst_ref=dst,
        send_sem=send_sem,
        recv_sem=recv_sem,
        device_id=target,
        device_id_type=MESH,
    )


def partners(x, j):
    flip, mirror = x + 1 - 2 * (x % 2), 3 - x
    return (flip, mirror) if j % 2 == 0 else (mirror, flip)


def others(x):
    return (x + 1 - 2 * (x % 2), 3 - x, (x + 2) % 4)


def say_hello(x, y, z, core):
    sem = pltpu.get_barrier_semaphore()

    def signal(condition, targets):
        @pl.when(condition)
        def _():
            for target in targets:
                pl.semaphore_signal(sem, inc=1, device_id=target, device_id_type=MESH)

    first = core == 0
    signal((z == 0) & (y == 0) & first, [device(x, n, 0, c) for n in (2, 1, 3) for c in (0, 1)])
    signal(z == 0, [device(x, y, n, core) for n in (4, 3, 5, 2, 6, 1, 7)])
    signal((z == 0) & (y != 0), [device(x, 0, 0, 0)])
    signal(z != 0, [device(x, y, 0, core)])
    signal((z == 2) & first, [device(x, y, 3, 0), device(x, y, 4, 0)])
    signal((z == 6) & first, [device(x, y, 5, 0)])
    signal(((z == 3) | (z == 4)) & first, [device(x, y, 2, 0)])
    signal((z == 5) & first, [device(x, y, 6, 0)])
    signal(z >= 0, [device(n, y, z, core) for n in others(x)] + [device(x, y, z, 1 - core)])


def hear_all(x, y, z, core):
    sem = pltpu.get_barrier_semaphore()
    first = core == 0
    end = (z == 1) | (z == 7)
    for role, peers in (
        ((z == 0) & (y == 0) & first, 17),
        ((z == 0) & (y == 0) & ~first, 11),
        ((z == 0) & (y != 0), 12),
        ((z != 0) & (~first | end), 5),
        ((z == 2) & first, 7),
        ((z != 0) & (z != 2) & ~end & first, 6),
    ):
        @pl.when(role)
        def _():
            pl.semaphore_wait(sem, peers)


TILES = ((0, 256), (256, 256), (512, 256), (768, 128))
WIDE = GROUP * D
EXP_SCALE = SCALE * LOG2E


def nt(a, b):
    return lax.dot_general(a, b, (((1,), (1,)), ((), ())), preferred_element_type=F32)


def nn(a, b):
    return lax.dot_general(a, b, (((1,), (0,)), ((), ())), preferred_element_type=F32)


def fold_max(a):
    return jnp.max(a.reshape(D // 8, 8, a.shape[1]), axis=0)


def fold_sum(a):
    return jnp.sum(a.reshape(D // 8, 8, a.shape[1]), axis=0)


def main_kernel(
    mask_ref, k_ref, v_ref, q_hbm, c_hbm,
    att_hbm, dq_hbm, dk_ref, dv_ref,
    kv, q_s, c_s, att_s, dq_s, bias, po, dpo, mo, lo, fo, de, sp, dpp, ps, dss, vt,
    g, so1, ro1, so2, ro2, sc, rc, gs, sp1, rp1, part, sz, rz, sy, ry,
    lsem, qsem, osem, s_own, r_own, s_pr, r_pr, s_by, s_bz, r_t, s_c, r_c,
    ss, rs, s_a, r_a, s_y, r_y, s_z, r_z,
):
    x, y, z, core = place()
    opp = (x + 2) % 4
    seq = lax.axis_index("seq")
    top_row = (z == 0) & (y == 0)
    is_root = top_row & (core == 0)
    column = (core == 0) & (z == 0)
    leaf = (core == 0) & (z != 0)
    mesh_c0 = (core == 0) & ~top_row

    say_hello(x, y, z, core)

    def local(j, block, base):
        return [
            pltpu.make_async_copy(ref.at[:, pl.ds(j * D, D)], kv.at[j, block, t], lsem.at[base, j, t])
            for t, ref in enumerate((k_ref, v_ref))
        ]

    @pl.when(is_root)
    def _():
        for j in range(HEADS):
            for b in range(QUARTERS):
                for copy in local(j, b, 1 + b):
                    copy.start()

    for j in range(HEADS):
        for copy in local(j, 4 + x, 0):
            copy.start()

    def take_out(buf, hbm, i, j):
        for h in range(GROUP):
            cols, rows = pl.ds((j * GROUP + h) * D, D), pl.ds(h * D, D)
            pltpu.make_async_copy(buf.at[j, rows], hbm.at[:, cols], osem.at[i, j]).start()

    hear_all(x, y, z, core)

    def y_send(j, n):
        blk = kv.at[j, x]
        return remote(blk, blk, s_by.at[j, n - 1], r_t.at[j], device(x, n, 0, 0))

    def z_send(j, n):
        blk = kv.at[j, x]
        return remote(blk, blk, s_bz.at[j, n - 1], r_t.at[j], device(x, y, n, 0))

    def children(j):
        return (4, 5, 3, 6, 2, 7, 1) if j < 2 else (2, 6, 1, 7)

    def pass_on(j):
        for n in children(j):
            z_send(j, n).start()

    def x_send(j, base, ss, rs, i):
        pa, pb = partners(x, j)
        blk = kv.at[j, base + (x, x, pa)[i]]
        return remote(blk, blk, ss.at[j, i], rs.at[j, i], device((pa, pb, pb)[i], y, z, core))

    def x_arrival(j, base, ss, rs, i):
        pa, pb = partners(x, j)
        blk = kv.at[j, base + (pa, pb, opp)[i]]
        remote(blk, blk, ss.at[j, i], rs.at[j, i], device((pa, pb, pb)[i], y, z, core)).wait_recv()

    def p_send(j, i):
        blk = kv.at[j, x]
        return remote(blk, blk, s_pr.at[j, i], r_pr.at[j, i], device(others(x)[i], y, z, core))

    def core_send(j, i, base=0):
        n = x if i == 3 else others(x)[i]
        src, dst = kv.at[j, base + n], kv.at[j, n]
        return remote(src, dst, s_c.at[j, i], r_c.at[j, i], device(x, y, z, 1 - core))

    def spread(j):
        for i in (2, 0, 1):
            p_send(j, i).start()
        core_send(j, 3).start()

    @pl.when(is_root)
    def _():
        for j in range(HEADS):
            for b in range(QUARTERS):
                for copy in local(j, b, 1 + b):
                    copy.wait()
            for n in (2, 1, 3):
                y_send(j, n).start()
            pass_on(j)
            core_send(j, 3).start()

    for j in range(HEADS):
        for copy in local(j, 4 + x, 0):
            copy.wait()
        x_send(j, 4, s_own, r_own, 0).start()
        x_send(j, 4, s_own, r_own, 1).start()

    for j in range(HEADS):
        for h in range(GROUP):
            cols, rows = pl.ds((j * GROUP + h) * D, D), pl.ds(h * D, D)
            pltpu.make_async_copy(q_hbm.at[:, cols], q_s.at[j, rows], qsem.at[0, j]).start()
            pltpu.make_async_copy(c_hbm.at[:, cols], c_s.at[j, rows], qsem.at[1, j]).start()

    key = lax.broadcasted_iota(jnp.int32, (D, D), 0)
    query = lax.broadcasted_iota(jnp.int32, (D, D), 1)
    for b in range(QUARTERS):
        seen = key + b * D <= query + x * D
        tile = jnp.where(seen, 0.0, -1e30).astype(F32)
        bias[pl.ds(b * D, D), pl.ds(0, D)] = tile
        bias[pl.ds(b * D, D), pl.ds(D, D)] = tile
    levels = []
    for b in range(QUARTERS):
        reads = jnp.where(seq > 0, mask_ref[x, b], 0)
        levels.append(jnp.where(reads > 0, 0.0, -1e30).astype(F32))

    def relay(j):
        @pl.when(column & (y != 0))
        def _():
            y_send(j, y).wait_recv()
            pass_on(j)
            spread(j)

        x_arrival(j, 4, s_own, r_own, 0)
        x_send(j, 4, s_own, r_own, 2).start()

    def prompt1(j, here):
        @pl.when(here)
        def _():
            z_send(j, z).wait_recv()
            if j > 1:
                @pl.when(z == 2)
                def _():
                    z_send(j, 4).start()
                    z_send(j, 3).start()

                @pl.when(z == 6)
                def _():
                    z_send(j, 5).start()

            spread(j)

    def prompt3(j):
        @pl.when(is_root)
        def _():
            for i in (0, 1, 2):
                core_send(j, i, 4).start()

        @pl.when(mesh_c0)
        def _():
            for i in (0, 1, 2):
                blk = kv.at[j, others(x)[i]]
                remote(blk, blk, s_pr.at[j, i], r_pr.at[j, i], device(others(x)[i], y, z, core)).wait_recv()
                core_send(j, i).start()

    def prompt_here(j):
        @pl.when(core == 1)
        def _():
            for i in range(4):
                core_send(j, i).wait_recv()

    def own_part(j):
        x_arrival(j, 4, s_own, r_own, 1)
        x_arrival(j, 4, s_own, r_own, 2)
        pltpu.make_async_copy(q_s.at[j], q_s.at[j], qsem.at[0, j]).wait()
        pltpu.make_async_copy(c_s.at[j], c_s.at[j], qsem.at[1, j]).wait()
        for at, width in TILES:
            cols = pl.ds(at, width)
            keys = kv[j, 4:8, 0].reshape(4 * D, D)
            values = kv[j, 4:8, 1].reshape(4 * D, D)
            po[j, :, cols] = nt(keys, q_s[j, cols, :]) + bias[:, pl.ds(0, width)]
            top = None
            for b in range(QUARTERS):
                part_top = fold_max(po[j, pl.ds(b * D, D), cols])
                top = part_top if top is None else jnp.maximum(top, part_top)
            top = jnp.max(top, axis=0, keepdims=True)
            total = None
            for b in range(QUARTERS):
                p = jnp.exp2((po[j, pl.ds(b * D, D), cols] - top) * EXP_SCALE)
                po[j, pl.ds(b * D, D), cols] = p
                part_sum = fold_sum(p)
                total = part_sum if total is None else total + part_sum
            mo[j, :, cols] = top
            lo[j, :, cols] = jnp.sum(total, axis=0, keepdims=True)
            dpo[j, :, cols] = nt(values, c_s[j, cols, :])

    def flip_values(j):
        for b in range(2 * QUARTERS):
            vt[:, pl.ds(b * D, D)] = kv[j, b, 1].T

    def prompt_part(j, at, width):
        cols, wide = pl.ds(at, width), pl.ds(0, width)
        c = c_s[j, cols, :]
        sp[:, wide] = nt(kv[j, 0:4, 0].reshape(4 * D, D), q_s[j, cols, :])
        dpp[:, wide] = nt(kv[j, 0:4, 1].reshape(4 * D, D), c)
        own_top = mo[j, :, cols]
        top = None
        for b in range(QUARTERS):
            part_top = fold_max(sp[pl.ds(b * D, D), wide]) + levels[b]
            top = part_top if top is None else jnp.maximum(top, part_top)
        top = jnp.maximum(own_top, jnp.max(top, axis=0, keepdims=True))
        shrink = jnp.exp2((own_top - top) * EXP_SCALE)
        total = None
        for b in range(QUARTERS):
            rows = pl.ds(b * D, D)
            p = jnp.exp2((sp[rows, wide] - (top - levels[b])) * EXP_SCALE)
            sp[rows, wide] = p
            part_sum = fold_sum(p)
            total = part_sum if total is None else total + part_sum
        total = jnp.sum(total, axis=0, keepdims=True) + lo[j, :, cols] * shrink
        inverse = 1.0 / total
        shrink = shrink * inverse
        fo[j, :, cols] = shrink
        for b in range(QUARTERS):
            rows = pl.ds(b * D, D)
            ps[j, rows, cols] = (sp[rows, wide] * inverse).astype(BF16)
            ps[j, pl.ds((4 + b) * D, D), cols] = (po[j, rows, cols] * shrink).astype(BF16)
        out_t = nn(vt[...], ps[j, :, cols]).astype(BF16)
        deltas = []
        for i in range(width // D):
            lanes, rows = slice(i * D, i * D + D), pl.ds(at + i * D, D)
            att_s[j, rows, :] = out_t[:, lanes].T
            prod = c_s[j, rows, :].T.astype(F32) * out_t[:, lanes].astype(F32)
            deltas.append(jnp.sum(prod, axis=0, keepdims=True))
        delta = jnp.concatenate(deltas, axis=1)
        de[j, :, cols] = delta
        for b in range(QUARTERS):
            rows = pl.ds(b * D, D)
            dss[j, rows, cols] = ((sp[rows, wide] * inverse) * (dpp[rows, wide] - delta)).astype(BF16)

    def own_terms(j):
        for at, width in TILES:
            cols = pl.ds(at, width)
            for b in range(QUARTERS):
                rows = pl.ds(b * D, D)
                dss[j, pl.ds((4 + b) * D, D), cols] = (
                    (po[j, rows, cols] * fo[j, :, cols]) * (dpo[j, rows, cols] - de[j, :, cols])
                ).astype(BF16)
        key_terms(j, 4)

    def key_terms(j, first):
        rows = pl.ds(first * D, 4 * D)
        g[j, first : first + 4, 0] = (nn(dss[j, rows, :], q_s[j]) * SCALE).reshape(4, D, D)
        g[j, first : first + 4, 1] = nn(ps[j, rows, :], c_s[j]).reshape(4, D, D)

    def query_part(j):
        for b in range(2 * QUARTERS):
            vt[:, pl.ds(b * D, D)] = kv[j, b, 0].T
        for at, width in TILES:
            grad_t = (nn(vt[...], dss[j, :, pl.ds(at, width)]) * SCALE).astype(BF16)
            for i in range(width // D):
                dq_s[j, pl.ds(at + i * D, D), :] = grad_t[:, i * D : i * D + D].T
        take_out(dq_s, dq_hbm, 1, j)

    def hop(send, arrive, i, j, target):
        return remote(send.at[j], arrive.at[j], ss.at[i, j], rs.at[i, j], target)

    def own1(j):
        return hop(so1, ro1, 0, j, device(partners(x, j)[0], y, z, core))

    def own2(j):
        return hop(so2, ro2, 1, j, device(partners(x, j)[1], y, z, core))

    def pair(j):
        return hop(sc, rc, 2, j, device(x, y, z, 1 - core))

    def across(j, i):
        return remote(sp1.at[j, i], rp1.at[j, i], s_a.at[j, i], r_a.at[j, i], device(others(x)[i], y, z, core))

    def to_column(j, n):
        return remote(sz.at[j], rz.at[j, n - 1], s_z.at[j], r_z.at[j, n - 1], device(x, y, 0, core))

    def to_root(j, t, n):
        return remote(sy.at[j], ry.at[j, t, n], s_y.at[j], r_y.at[j, t, n], device(x, 0, 0, 0))

    def reduce0(j):
        for b in range(QUARTERS):
            sc[j, b] = g[j, b, 1 - core].astype(BF16)
        pair(j).start()

    def own_reduce1(j):
        pa, pb = partners(x, j)
        so1[j, 0] = g[j, 4 + pa].astype(BF16)
        so1[j, 1] = g[j, 4 + opp].astype(BF16)
        own1(j).start()

    def reduce1(j):
        pair(j).wait_recv()
        for b in range(QUARTERS):
            gs[j, b] = g[j, b, core] + rc[j, b].astype(F32)
        for i in (2, 0, 1):
            sp1[j, i] = gs[j, others(x)[i]].astype(BF16)
            across(j, i).start()

    def own_reduce2(j):
        pa, pb = partners(x, j)
        own1(j).wait_recv()
        so2[j] = (g[j, 4 + pb] + ro1[j, 1].astype(F32)).astype(BF16)
        own2(j).start()

    def reduce3(j):
        total = gs[j, x]
        for i in range(3):
            across(j, i).wait_recv()
            total = total + rp1[j, i].astype(F32)
        part[j] = total
        sz[j] = total.astype(BF16)

        @pl.when(z != 0)
        def _():
            to_column(j, z).start()

    def reduce4(j):
        @pl.when(z == 0)
        def _():
            total = part[j]
            for n in range(1, NZ):
                to_column(j, n).wait_recv()
                total = total + rz[j, n - 1].astype(F32)
            part[j] = total
            sy[j] = total.astype(BF16)

            @pl.when((y != 0) | (core == 1))
            def _():
                to_root(j, core, y).start()

    def own_result(j):
        own2(j).wait_recv()
        cols = pl.ds(j * D, D)
        total = g[j, 4 + x] + ro1[j, 0].astype(F32) + ro2[j].astype(F32)
        g[j, 4 + x] = total
        dk_ref[:, cols] = total[0].astype(BF16)
        dv_ref[:, cols] = total[1].astype(BF16)

    def root_result(j):
        @pl.when(is_root)
        def _():
            cols = pl.ds(j * D, D)
            total = g[j, 4 + x, 0] + part[j]
            for n in range(1, NY):
                to_root(j, 0, n).wait_recv()
                total = total + ry[j, 0, n].astype(F32)
            dk_ref[:, cols] = total.astype(BF16)
            total = g[j, 4 + x, 1]
            for n in range(NY):
                to_root(j, 1, n).wait_recv()
                total = total + ry[j, 1, n].astype(F32)
            dv_ref[:, cols] = total.astype(BF16)

    near = leaf & ((z < 3) | (z > 5))
    far = leaf & (z > 2) & (z < 6)
    relay(0)
    relay(1)
    prompt1(0, near)
    relay(2)
    relay(3)
    prompt1(0, far)
    prompt1(1, near)
    own_part(0)
    own_part(1)
    prompt1(1, far)
    own_part(2)
    prompt1(2, near)
    prompt3(0)
    own_part(3)
    prompt1(2, far)
    prompt1(3, near)
    between = {
        (0, 0): lambda: (prompt3(1), prompt1(3, far)),
        (0, 2): lambda: prompt3(2),
        (1, 0): lambda: prompt3(3),
        (1, 2): lambda: reduce1(0),
        (2, 1): lambda: reduce1(1),
        (2, 3): lambda: reduce3(0),
        (3, 1): lambda: reduce1(2),
        (3, 3): lambda: reduce3(1),
    }
    for j in range(HEADS):
        prompt_here(j)
        flip_values(j)
        for i, (at, width) in enumerate(TILES):
            prompt_part(j, at, width)
            between.get((j, i), lambda: None)()
        key_terms(j, 0)
        reduce0(j)
        take_out(att_s, att_hbm, 0, j)
    own_terms(0)
    reduce1(3)
    own_reduce1(0)
    reduce3(2)
    own_terms(1)
    own_reduce1(1)
    own_terms(2)
    own_reduce1(2)
    reduce4(0)
    own_terms(3)
    reduce3(3)
    own_reduce1(3)
    own_reduce2(0)
    reduce4(1)
    query_part(0)
    own_reduce2(1)
    reduce4(2)
    query_part(1)
    own_reduce2(2)
    query_part(2)
    query_part(3)
    reduce4(3)
    own_reduce2(3)
    own_result(0)
    own_result(1)
    own_result(2)
    own_result(3)

    for j in range(HEADS):
        for i in range(3):
            x_send(j, 4, s_own, r_own, i).wait_send()

        @pl.when(core == 0)
        def _():
            for i in range(4):
                core_send(j, i).wait_send()

        @pl.when(mesh_c0)
        def _():
            for i in range(3):
                p_send(j, i).wait_send()

        @pl.when(column)
        def _():
            for n in children(j):
                z_send(j, n).wait_send()

        if j > 1:
            @pl.when(leaf & (z == 2))
            def _():
                z_send(j, 4).wait_send()
                z_send(j, 3).wait_send()

            @pl.when(leaf & (z == 6))
            def _():
                z_send(j, 5).wait_send()

        @pl.when(is_root)
        def _():
            for n in range(1, NY):
                y_send(j, n).wait_send()

        for copy in (own1(j), own2(j), pair(j), across(j, 0), across(j, 1), across(j, 2)):
            copy.wait_send()

        @pl.when(z != 0)
        def _():
            to_column(j, z).wait_send()

        @pl.when((z == 0) & ((y != 0) | (core == 1)))
        def _():
            to_root(j, core, y).wait_send()

        pltpu.make_async_copy(att_s.at[j], att_s.at[j], osem.at[0, j]).wait()
        pltpu.make_async_copy(dq_s.at[j], dq_s.at[j], osem.at[1, j]).wait()

    for j in range(HEADS):
        root_result(j)


def main(mask, k, v, q, c):
    dma, vmem = pltpu.SemaphoreType.DMA, pltpu.VMEM
    block = (D, D)
    wide = jax.ShapeDtypeStruct(q.shape, BF16)
    narrow = jax.ShapeDtypeStruct(k.shape, BF16)
    here = pl.BlockSpec(memory_space=pltpu.VMEM)
    there = pl.BlockSpec(memory_space=pl.ANY)
    return pl.pallas_call(
        main_kernel,
        out_shape=(wide, wide, narrow, narrow),
        in_specs=[pl.BlockSpec(memory_space=pltpu.SMEM), there, there, there, there],
        out_specs=(there, there, here, here),
        scratch_shapes=[
            vmem((HEADS, 8, 2) + block, BF16),
            vmem((HEADS, WIDE, D), BF16),
            vmem((HEADS, WIDE, D), BF16),
            vmem((HEADS, WIDE, D), BF16),
            vmem((HEADS, WIDE, D), BF16),
            vmem((4 * D, 2 * D), F32),
            vmem((HEADS, 4 * D, WIDE), F32),
            vmem((HEADS, 4 * D, WIDE), F32),
            vmem((HEADS, 1, WIDE), F32),
            vmem((HEADS, 1, WIDE), F32),
            vmem((HEADS, 1, WIDE), F32),
            vmem((HEADS, 1, WIDE), F32),
            vmem((4 * D, 2 * D), F32),
            vmem((4 * D, 2 * D), F32),
            vmem((HEADS, 8 * D, WIDE), BF16),
            vmem((HEADS, 8 * D, WIDE), BF16),
            vmem((D, 8 * D), BF16),
            vmem((HEADS, 8, 2) + block, F32),
            vmem((HEADS, 2, 2) + block, BF16),
            vmem((HEADS, 2, 2) + block, BF16),
            vmem((HEADS, 2) + block, BF16),
            vmem((HEADS, 2) + block, BF16),
            vmem((HEADS, 4) + block, BF16),
            vmem((HEADS, 4) + block, BF16),
            vmem((HEADS, 4) + block, F32),
            vmem((HEADS, 3) + block, BF16),
            vmem((HEADS, 3) + block, BF16),
            vmem((HEADS,) + block, F32),
            vmem((HEADS,) + block, BF16),
            vmem((HEADS, NZ - 1) + block, BF16),
            vmem((HEADS,) + block, BF16),
            vmem((HEADS, 2, NY) + block, BF16),
            dma((5, HEADS, 2)),
            dma((2, HEADS)),
            dma((2, HEADS)),
            dma((HEADS, 3)),
            dma((HEADS, 3)),
            dma((HEADS, 3)),
            dma((HEADS, 3)),
            dma((HEADS, NY - 1)),
            dma((HEADS, NZ - 1)),
            dma((HEADS,)),
            dma((HEADS, 4)),
            dma((HEADS, 4)),
            dma((3, HEADS)),
            dma((3, HEADS)),
            dma((HEADS, 3)),
            dma((HEADS, 3)),
            dma((HEADS,)),
            dma((HEADS, 2, NY)),
            dma((HEADS,)),
            dma((HEADS, NZ - 1)),
        ],
        compiler_params=pltpu.CompilerParams(
            collective_id=0, has_side_effects=True, vmem_limit_bytes=60 * 2**20
        ),
        name="tree_attention",
    )(mask, k, v, q, c)


PIECES = 2


def hand_on_kernel(*refs):
    arrays, outs, held, (came, went) = refs[:4], refs[4:8], refs[8:12], refs[12:]

    def copies(i, p):
        rows = pl.ds(p * (D // PIECES), D // PIECES)
        inner = held[i].at[rows]
        return (
            pltpu.make_async_copy(arrays[i].at[rows], inner, came.at[i, p]),
            pltpu.make_async_copy(inner, outs[i].at[rows], went.at[i, p]),
        )

    order = [(i, p) for i in (2, 3, 0, 1) for p in range(PIECES)]
    for at in order:
        copies(*at)[0].start()
    for at in order:
        copies(*at)[0].wait()
        copies(*at)[1].start()
    for at in order:
        copies(*at)[1].wait()


def hand_on(arrays):
    there = pl.BlockSpec(memory_space=pl.ANY)
    return pl.pallas_call(
        hand_on_kernel,
        out_shape=[jax.ShapeDtypeStruct(a.shape, a.dtype) for a in arrays],
        in_specs=[there] * 4,
        out_specs=[there] * 4,
        scratch_shapes=[pltpu.VMEM(a.shape, a.dtype) for a in arrays]
        + [pltpu.SemaphoreType.DMA((4, PIECES))] * 2,
        name="hand_on",
    )(*arrays)


def on_device(queries, rotated_key_rows, value_matrix, cotangent, tree_mask):
    return tuple(hand_on(main(tree_mask, rotated_key_rows, value_matrix, queries, cotangent)))


def solution(mesh):
    rows = P(("seq", "head"), None)
    return jax.shard_map(
        on_device,
        mesh=mesh,
        in_specs=(rows, rows, rows, rows, P("seq", None)),
        out_specs=(rows, rows, rows, rows),
        check_vma=False,
    )
```

```python
import jax
import jax.numpy as jnp
from jax import lax
from jax.experimental import pallas as pl
from jax.experimental.pallas import tpu as pltpu
from jax.sharding import PartitionSpec as P

HEADS = 4
GROUP = 7
D = 128
QUARTERS = 4
NY, NZ = 4, 8
SCALE = D ** (-0.5)
LOG2E = 1.4426950408889634
MESH = pl.DeviceIdType.MESH
BF16 = jnp.bfloat16
F32 = jnp.float32


def place():
    seq = lax.axis_index("seq")
    x = lax.axis_index("head")
    return x, seq // (2 * NZ), (seq // 2) % NZ, seq % 2


def device(x, y, z, core):
    return ((y * NZ + z) * 2 + core, x)


def remote(src, dst, send_sem, recv_sem, target):
    return pltpu.make_async_remote_copy(
        src_ref=src,
        dst_ref=dst,
        send_sem=send_sem,
        recv_sem=recv_sem,
        device_id=target,
        device_id_type=MESH,
    )


def partners(x, j):
    flip, mirror = x + 1 - 2 * (x % 2), 3 - x
    return (flip, mirror) if j % 2 == 0 else (mirror, flip)


def drain(view, sem):
    pltpu.make_async_copy(view, view, sem).wait()


def others(x):
    return (x + 1 - 2 * (x % 2), 3 - x, (x + 2) % 4)


def say_hello(x, y, z, core):
    sem = pltpu.get_barrier_semaphore()

    def signal(condition, targets):
        @pl.when(condition)
        def _():
            for target in targets:
                pl.semaphore_signal(sem, inc=1, device_id=target, device_id_type=MESH)

    first = core == 0
    signal((z == 0) & (y == 0) & first, [device(x, n, 0, c) for n in (2, 1, 3) for c in (0, 1)])
    signal(z == 0, [device(x, y, n, core) for n in (4, 3, 5, 2, 6, 1, 7)])
    signal((z == 0) & (y != 0), [device(x, 0, 0, 0)])
    signal(z != 0, [device(x, y, 0, core)])
    signal((z == 2) & first, [device(x, y, 3, 0), device(x, y, 4, 0)])
    signal((z == 6) & first, [device(x, y, 5, 0)])
    signal(((z == 3) | (z == 4)) & first, [device(x, y, 2, 0)])
    signal((z == 5) & first, [device(x, y, 6, 0)])
    signal(z >= 0, [device(n, y, z, core) for n in others(x)] + [device(x, y, z, 1 - core)])


def hear_all(x, y, z, core):
    sem = pltpu.get_barrier_semaphore()
    first = core == 0
    end = (z == 1) | (z == 7)
    for role, peers in (
        ((z == 0) & (y == 0) & first, 17),
        ((z == 0) & (y == 0) & ~first, 11),
        ((z == 0) & (y != 0), 12),
        ((z != 0) & (~first | end), 5),
        ((z == 2) & first, 7),
        ((z != 0) & (z != 2) & ~end & first, 6),
    ):
        @pl.when(role)
        def _():
            pl.semaphore_wait(sem, peers)


TILES = ((0, 256), (256, 256), (512, 256), (768, 128))
WIDE = GROUP * D
EXP_SCALE = SCALE * LOG2E


def nt(a, b):
    return lax.dot_general(a, b, (((1,), (1,)), ((), ())), preferred_element_type=F32)


def nn(a, b):
    return lax.dot_general(a, b, (((1,), (0,)), ((), ())), preferred_element_type=F32)


def fold_max(a):
    return jnp.max(a.reshape(D // 8, 8, a.shape[1]), axis=0)


def fold_sum(a):
    return jnp.sum(a.reshape(D // 8, 8, a.shape[1]), axis=0)


def main_kernel(
    mask_ref, k_ref, v_ref, q_hbm, c_hbm,
    att_hbm, dq_hbm, dk_ref, dv_ref,
    kv, q_s, c_s, att_s, dq_s, bias, po, dpo, mo, lo, fo, de, sp, dpp, ps, dss, vt,
    g, so1, ro1, so2, ro2, sc, rc, gs, sp1, rp1, part, sz, rz, sy, ry,
    lsem, qsem, osem, s_own, r_own, s_pr, r_pr, s_by, s_bz, r_t, s_c, r_c,
    ss, rs, s_a, r_a, s_y, r_y, s_z, r_z,
):
    x, y, z, core = place()
    opp = (x + 2) % 4
    seq = lax.axis_index("seq")
    top_row = (z == 0) & (y == 0)
    is_root = top_row & (core == 0)
    column = (core == 0) & (z == 0)
    leaf = (core == 0) & (z != 0)
    mesh_c0 = (core == 0) & ~top_row

    say_hello(x, y, z, core)

    def local(j, block, base):
        return [
            pltpu.make_async_copy(ref.at[:, pl.ds(j * D, D)], kv.at[j, block, t], lsem.at[base])
            for t, ref in enumerate((k_ref, v_ref))
        ]

    @pl.when(is_root)
    def _():
        for j in range(HEADS):
            for b in range(QUARTERS):
                for copy in local(j, b, 1):
                    copy.start()

    for j in range(HEADS):
        for copy in local(j, 4 + x, 0):
            copy.start()

    def take_out(buf, hbm, i, j):
        for h in range(GROUP):
            cols, rows = pl.ds((j * GROUP + h) * D, D), pl.ds(h * D, D)
            pltpu.make_async_copy(buf.at[j, rows], hbm.at[:, cols], osem.at[i]).start()

    hear_all(x, y, z, core)

    def y_send(j, n):
        blk = kv.at[j, x]
        return remote(blk, blk, s_by.at[0], r_t.at[j], device(x, n, 0, 0))

    def z_send(j, n):
        blk = kv.at[j, x]
        return remote(blk, blk, s_bz.at[0], r_t.at[j], device(x, y, n, 0))

    def pass_on(j):
        for n in (2, 6, 1, 7):
            z_send(j, n).start()

    def x_send(j, base, ss, rs, i):
        pa, pb = partners(x, j)
        blk = kv.at[j, base + (x, x, pa)[i]]
        return remote(blk, blk, ss.at[0], rs.at[j, (0, 1, 1)[i]], device((pa, pb, pb)[i], y, z, core))

    def p_send(j, i):
        blk = kv.at[j, x]
        return remote(blk, blk, s_pr.at[0], r_pr.at[j], device(others(x)[i], y, z, core))

    def core_send(j, i, base=0):
        n = x if i == 3 else others(x)[i]
        src, dst = kv.at[j, base + n], kv.at[j, n]
        return remote(src, dst, s_c.at[0], r_c.at[j], device(x, y, z, 1 - core))

    def spread(j):
        for i in (2, 0, 1):
            p_send(j, i).start()
        core_send(j, 3).start()

    @pl.when(is_root)
    def _():
        drain(kv.at[:, pl.ds(0, 4)], lsem.at[1])
        for j in range(HEADS):
            for n in (2, 1, 3):
                y_send(j, n).start()
            pass_on(j)
            core_send(j, 3).start()

    drain(kv.at[:, pl.ds(4, 1)], lsem.at[0])
    for j in range(HEADS):
        x_send(j, 4, s_own, r_own, 0).start()
        x_send(j, 4, s_own, r_own, 1).start()

    for j in range(HEADS):
        for h in range(GROUP):
            cols, rows = pl.ds((j * GROUP + h) * D, D), pl.ds(h * D, D)
            pltpu.make_async_copy(q_hbm.at[:, cols], q_s.at[j, rows], qsem.at[0]).start()
            pltpu.make_async_copy(c_hbm.at[:, cols], c_s.at[j, rows], qsem.at[1]).start()

    key = lax.broadcasted_iota(jnp.int32, (D, D), 0)
    query = lax.broadcasted_iota(jnp.int32, (D, D), 1)
    for b in range(QUARTERS):
        seen = key + b * D <= query + x * D
        tile = jnp.where(seen, 0.0, -1e30).astype(F32)
        bias[pl.ds(b * D, D), pl.ds(0, D)] = tile
        bias[pl.ds(b * D, D), pl.ds(D, D)] = tile
    levels = []
    for b in range(QUARTERS):
        reads = jnp.where(seq > 0, mask_ref[x, b], 0)
        levels.append(jnp.where(reads > 0, 0.0, -1e30).astype(F32))

    def relay(j):
        @pl.when(column & (y != 0))
        def _():
            y_send(j, y).wait_recv()
            pass_on(j)
            spread(j)

        drain(kv.at[j, pl.ds(4, 1)], r_own.at[j, 0])
        x_send(j, 4, s_own, r_own, 2).start()

    def prompt1(j, here):
        @pl.when(here)
        def _():
            z_send(j, z).wait_recv()

            @pl.when(z == 2)
            def _():
                z_send(j, 4).start()
                z_send(j, 3).start()

            @pl.when(z == 6)
            def _():
                z_send(j, 5).start()

            spread(j)

    def prompt3(j):
        @pl.when(is_root)
        def _():
            for i in (0, 1, 2):
                core_send(j, i, 4).start()

        @pl.when(mesh_c0)
        def _():
            drain(kv.at[j, pl.ds(0, 3)], r_pr.at[j])
            for i in (0, 1, 2):
                core_send(j, i).start()

    def prompt_here(j):
        @pl.when(core == 1)
        def _():
            drain(kv.at[j, pl.ds(0, 4)], r_c.at[j])

    def own_part(j):
        drain(kv.at[j, pl.ds(4, 2)], r_own.at[j, 1])
        if j == 0:
            drain(q_s, qsem.at[0])
            drain(c_s, qsem.at[1])
        for at, width in TILES:
            cols = pl.ds(at, width)
            keys = kv[j, 4:8, 0].reshape(4 * D, D)
            values = kv[j, 4:8, 1].reshape(4 * D, D)
            po[j, :, cols] = nt(keys, q_s[j, cols, :]) + bias[:, pl.ds(0, width)]
            top = None
            for b in range(QUARTERS):
                part_top = fold_max(po[j, pl.ds(b * D, D), cols])
                top = part_top if top is None else jnp.maximum(top, part_top)
            top = jnp.max(top, axis=0, keepdims=True)
            total = None
            for b in range(QUARTERS):
                p = jnp.exp2((po[j, pl.ds(b * D, D), cols] - top) * EXP_SCALE)
                po[j, pl.ds(b * D, D), cols] = p
                part_sum = fold_sum(p)
                total = part_sum if total is None else total + part_sum
            mo[j, :, cols] = top
            lo[j, :, cols] = jnp.sum(total, axis=0, keepdims=True)
            dpo[j, :, cols] = nt(values, c_s[j, cols, :])

    def flip_values(j):
        for b in range(2 * QUARTERS):
            vt[:, pl.ds(b * D, D)] = kv[j, b, 1].T

    def prompt_part(j, at, width):
        cols, wide = pl.ds(at, width), pl.ds(0, width)
        c = c_s[j, cols, :]
        sp[:, wide] = nt(kv[j, 0:4, 0].reshape(4 * D, D), q_s[j, cols, :])
        dpp[:, wide] = nt(kv[j, 0:4, 1].reshape(4 * D, D), c)
        own_top = mo[j, :, cols]
        top = None
        for b in range(QUARTERS):
            part_top = fold_max(sp[pl.ds(b * D, D), wide]) + levels[b]
            top = part_top if top is None else jnp.maximum(top, part_top)
        top = jnp.maximum(own_top, jnp.max(top, axis=0, keepdims=True))
        shrink = jnp.exp2((own_top - top) * EXP_SCALE)
        total = None
        for b in range(QUARTERS):
            rows = pl.ds(b * D, D)
            p = jnp.exp2((sp[rows, wide] - (top - levels[b])) * EXP_SCALE)
            sp[rows, wide] = p
            part_sum = fold_sum(p)
            total = part_sum if total is None else total + part_sum
        total = jnp.sum(total, axis=0, keepdims=True) + lo[j, :, cols] * shrink
        inverse = 1.0 / total
        shrink = shrink * inverse
        fo[j, :, cols] = shrink
        for b in range(QUARTERS):
            rows = pl.ds(b * D, D)
            ps[j, rows, cols] = (sp[rows, wide] * inverse).astype(BF16)
            ps[j, pl.ds((4 + b) * D, D), cols] = (po[j, rows, cols] * shrink).astype(BF16)
        out_t = nn(vt[...], ps[j, :, cols]).astype(BF16)
        deltas = []
        for i in range(width // D):
            lanes, rows = slice(i * D, i * D + D), pl.ds(at + i * D, D)
            att_s[j, rows, :] = out_t[:, lanes].T
            prod = c_s[j, rows, :].T.astype(F32) * out_t[:, lanes].astype(F32)
            deltas.append(jnp.sum(prod, axis=0, keepdims=True))
        delta = jnp.concatenate(deltas, axis=1)
        de[j, :, cols] = delta
        for b in range(QUARTERS):
            rows = pl.ds(b * D, D)
            dss[j, rows, cols] = ((sp[rows, wide] * inverse) * (dpp[rows, wide] - delta)).astype(BF16)

    def own_terms(j):
        for at, width in TILES:
            cols = pl.ds(at, width)
            for b in range(QUARTERS):
                rows = pl.ds(b * D, D)
                dss[j, pl.ds((4 + b) * D, D), cols] = (
                    (po[j, rows, cols] * fo[j, :, cols]) * (dpo[j, rows, cols] - de[j, :, cols])
                ).astype(BF16)
        key_terms(j, 4)

    def key_terms(j, first):
        rows = pl.ds(first * D, 4 * D)
        g[j, first : first + 4, 0] = (nn(dss[j, rows, :], q_s[j]) * SCALE).reshape(4, D, D)
        g[j, first : first + 4, 1] = nn(ps[j, rows, :], c_s[j]).reshape(4, D, D)

    def query_part(j):
        for b in range(2 * QUARTERS):
            vt[:, pl.ds(b * D, D)] = kv[j, b, 0].T
        for at, width in TILES:
            grad_t = (nn(vt[...], dss[j, :, pl.ds(at, width)]) * SCALE).astype(BF16)
            for i in range(width // D):
                dq_s[j, pl.ds(at + i * D, D), :] = grad_t[:, i * D : i * D + D].T
        take_out(dq_s, dq_hbm, 1, j)

    def hop(send, arrive, i, j, target):
        return remote(send.at[j], arrive.at[j], ss.at[i], rs.at[i, j], target)

    def own1(j):
        return hop(so1, ro1, 0, j, device(partners(x, j)[0], y, z, core))

    def own2(j):
        return hop(so2, ro2, 1, j, device(partners(x, j)[1], y, z, core))

    def pair(j):
        return hop(sc, rc, 2, j, device(x, y, z, 1 - core))

    def across(j, i):
        return remote(sp1.at[j, i], rp1.at[j, i], s_a.at[0], r_a.at[j], device(others(x)[i], y, z, core))

    def to_column(j, n):
        return remote(sz.at[j], rz.at[j, n - 1], s_z.at[0], r_z.at[j], device(x, y, 0, core))

    def to_root(j, t, n):
        return remote(sy.at[j], ry.at[j, 4 * t + n - 1], s_y.at[0], r_y.at[j], device(x, 0, 0, 0))

    def reduce0(j):
        for b in range(QUARTERS):
            sc[j, b] = g[j, b, 1 - core].astype(BF16)
        pair(j).start()

    def own_reduce1(j):
        pa, pb = partners(x, j)
        so1[j, 0] = g[j, 4 + pa].astype(BF16)
        so1[j, 1] = g[j, 4 + opp].astype(BF16)
        own1(j).start()

    def reduce1(j):
        pair(j).wait_recv()
        for b in range(QUARTERS):
            gs[j, b] = g[j, b, core] + rc[j, b].astype(F32)
        for i in (2, 0, 1):
            sp1[j, i] = gs[j, others(x)[i]].astype(BF16)
            across(j, i).start()

    def own_reduce2(j):
        pa, pb = partners(x, j)
        own1(j).wait_recv()
        so2[j] = (g[j, 4 + pb] + ro1[j, 1].astype(F32)).astype(BF16)
        own2(j).start()

    def reduce3(j):
        total = gs[j, x]
        drain(rp1.at[j], r_a.at[j])
        for i in range(3):
            total = total + rp1[j, i].astype(F32)
        part[j] = total
        sz[j] = total.astype(BF16)

        @pl.when(z != 0)
        def _():
            to_column(j, z).start()

    def reduce4(j):
        @pl.when(z == 0)
        def _():
            total = part[j]
            drain(rz.at[j], r_z.at[j])
            for n in range(1, NZ):
                total = total + rz[j, n - 1].astype(F32)
            part[j] = total
            sy[j] = total.astype(BF16)

            @pl.when((y != 0) | (core == 1))
            def _():
                to_root(j, core, y).start()

    def own_result(j):
        own2(j).wait_recv()
        cols = pl.ds(j * D, D)
        total = g[j, 4 + x] + ro1[j, 0].astype(F32) + ro2[j].astype(F32)
        g[j, 4 + x] = total
        dk_ref[:, cols] = total[0].astype(BF16)
        dv_ref[:, cols] = total[1].astype(BF16)

    def root_result(j):
        @pl.when(is_root)
        def _():
            cols = pl.ds(j * D, D)
            drain(ry.at[j], r_y.at[j])
            total = g[j, 4 + x, 0] + part[j]
            for n in range(1, NY):
                total = total + ry[j, n - 1].astype(F32)
            dk_ref[:, cols] = total.astype(BF16)
            total = g[j, 4 + x, 1]
            for n in range(NY):
                total = total + ry[j, 3 + n].astype(F32)
            dv_ref[:, cols] = total.astype(BF16)

    near = leaf & ((z < 3) | (z > 5))
    far = leaf & (z > 2) & (z < 6)
    relay(0)
    relay(1)
    prompt1(0, near)
    relay(2)
    prompt1(1, near)
    relay(3)
    prompt1(2, near)
    own_part(0)
    prompt1(3, near)
    prompt1(0, far)
    own_part(1)
    prompt1(1, far)
    own_part(2)
    prompt1(2, far)
    own_part(3)
    prompt3(0)
    prompt1(3, far)
    between = {
        (0, 0): lambda: prompt3(1),
        (0, 2): lambda: prompt3(2),
        (1, 0): lambda: prompt3(3),
        (1, 2): lambda: reduce1(0),
        (2, 1): lambda: reduce1(1),
        (2, 3): lambda: reduce3(0),
        (3, 1): lambda: reduce1(2),
        (3, 3): lambda: reduce3(1),
    }
    for j in range(HEADS):
        prompt_here(j)
        flip_values(j)
        for i, (at, width) in enumerate(TILES):
            prompt_part(j, at, width)
            between.get((j, i), lambda: None)()
        key_terms(j, 0)
        reduce0(j)
        take_out(att_s, att_hbm, 0, j)
    own_terms(0)
    reduce1(3)
    own_reduce1(0)
    reduce3(2)
    own_terms(1)
    own_reduce1(1)
    own_terms(2)
    own_reduce1(2)
    reduce4(0)
    own_terms(3)
    reduce3(3)
    own_reduce1(3)
    own_reduce2(0)
    reduce4(1)
    query_part(0)
    own_reduce2(1)
    reduce4(2)
    query_part(1)
    own_reduce2(2)
    query_part(2)
    query_part(3)
    reduce4(3)
    own_reduce2(3)
    own_result(0)
    own_result(1)
    own_result(2)
    own_result(3)

    twelve = kv.at[pl.ds(0, 2), pl.ds(0, 6)]
    sixteen = kv.at[pl.ds(0, 2)]
    drain(twelve, s_own.at[0])

    @pl.when(core == 0)
    def _():
        drain(sixteen, s_c.at[0])

    @pl.when(mesh_c0)
    def _():
        drain(twelve, s_pr.at[0])

    @pl.when(column)
    def _():
        drain(sixteen, s_bz.at[0])

    @pl.when(leaf & (z == 2))
    def _():
        drain(kv.at[0], s_bz.at[0])

    @pl.when(leaf & (z == 6))
    def _():
        drain(kv.at[0, pl.ds(0, 4)], s_bz.at[0])

    @pl.when(is_root)
    def _():
        drain(twelve, s_by.at[0])

    drain(so1, ss.at[0])
    drain(so2, ss.at[1])
    drain(sc, ss.at[2])
    drain(sp1, s_a.at[0])

    @pl.when(z != 0)
    def _():
        drain(sz, s_z.at[0])

    @pl.when((z == 0) & ((y != 0) | (core == 1)))
    def _():
        drain(sy, s_y.at[0])

    drain(att_s, osem.at[0])
    drain(dq_s, osem.at[1])

    for j in range(HEADS):
        root_result(j)


def main(mask, k, v, q, c):
    dma, vmem = pltpu.SemaphoreType.DMA, pltpu.VMEM
    block = (D, D)
    wide = jax.ShapeDtypeStruct(q.shape, BF16)
    narrow = jax.ShapeDtypeStruct(k.shape, BF16)
    here = pl.BlockSpec(memory_space=pltpu.VMEM)
    there = pl.BlockSpec(memory_space=pl.ANY)
    return pl.pallas_call(
        main_kernel,
        out_shape=(wide, wide, narrow, narrow),
        in_specs=[pl.BlockSpec(memory_space=pltpu.SMEM), there, there, there, there],
        out_specs=(there, there, here, here),
        scratch_shapes=[
            vmem((HEADS, 8, 2) + block, BF16),
            vmem((HEADS, WIDE, D), BF16),
            vmem((HEADS, WIDE, D), BF16),
            vmem((HEADS, WIDE, D), BF16),
            vmem((HEADS, WIDE, D), BF16),
            vmem((4 * D, 2 * D), F32),
            vmem((HEADS, 4 * D, WIDE), F32),
            vmem((HEADS, 4 * D, WIDE), F32),
            vmem((HEADS, 1, WIDE), F32),
            vmem((HEADS, 1, WIDE), F32),
            vmem((HEADS, 1, WIDE), F32),
            vmem((HEADS, 1, WIDE), F32),
            vmem((4 * D, 2 * D), F32),
            vmem((4 * D, 2 * D), F32),
            vmem((HEADS, 8 * D, WIDE), BF16),
            vmem((HEADS, 8 * D, WIDE), BF16),
            vmem((D, 8 * D), BF16),
            vmem((HEADS, 8, 2) + block, F32),
            vmem((HEADS, 2, 2) + block, BF16),
            vmem((HEADS, 2, 2) + block, BF16),
            vmem((HEADS, 2) + block, BF16),
            vmem((HEADS, 2) + block, BF16),
            vmem((HEADS, 4) + block, BF16),
            vmem((HEADS, 4) + block, BF16),
            vmem((HEADS, 4) + block, F32),
            vmem((HEADS, 3) + block, BF16),
            vmem((HEADS, 3) + block, BF16),
            vmem((HEADS,) + block, F32),
            vmem((HEADS,) + block, BF16),
            vmem((HEADS, NZ - 1) + block, BF16),
            vmem((HEADS,) + block, BF16),
            vmem((HEADS, 2 * NY - 1) + block, BF16),
            dma((2,)),
            dma((2,)),
            dma((2,)),
            dma((1,)),
            dma((HEADS, 2)),
            dma((1,)),
            dma((HEADS,)),
            dma((1,)),
            dma((1,)),
            dma((HEADS,)),
            dma((1,)),
            dma((HEADS,)),
            dma((3,)),
            dma((3, HEADS)),
            dma((1,)),
            dma((HEADS,)),
            dma((1,)),
            dma((HEADS,)),
            dma((1,)),
            dma((HEADS,)),
        ],
        compiler_params=pltpu.CompilerParams(
            collective_id=0, has_side_effects=True, vmem_limit_bytes=60 * 2**20
        ),
        name="tree_attention",
    )(mask, k, v, q, c)


PIECES = 2


def hand_on_kernel(*refs):
    arrays, outs, held, (came, went) = refs[:4], refs[4:8], refs[8:12], refs[12:]

    def copies(i, p):
        rows = pl.ds(p * (D // PIECES), D // PIECES)
        inner = held[i].at[rows]
        return (
            pltpu.make_async_copy(arrays[i].at[rows], inner, came.at[i, p]),
            pltpu.make_async_copy(inner, outs[i].at[rows], went.at[i, p]),
        )

    order = [(i, p) for i in (2, 3, 0, 1) for p in range(PIECES)]
    for at in order:
        copies(*at)[0].start()
    for at in order:
        copies(*at)[0].wait()
        copies(*at)[1].start()
    for at in order:
        copies(*at)[1].wait()


def hand_on(arrays):
    there = pl.BlockSpec(memory_space=pl.ANY)
    return pl.pallas_call(
        hand_on_kernel,
        out_shape=[jax.ShapeDtypeStruct(a.shape, a.dtype) for a in arrays],
        in_specs=[there] * 4,
        out_specs=[there] * 4,
        scratch_shapes=[pltpu.VMEM(a.shape, a.dtype) for a in arrays]
        + [pltpu.SemaphoreType.DMA((4, PIECES))] * 2,
        name="hand_on",
    )(*arrays)


def on_device(queries, rotated_key_rows, value_matrix, cotangent, tree_mask):
    return tuple(hand_on(main(tree_mask, rotated_key_rows, value_matrix, queries, cotangent)))


def solution(mesh):
    rows = P(("seq", "head"), None)
    return jax.shard_map(
        on_device,
        mesh=mesh,
        in_specs=(rows, rows, rows, rows, P("seq", None)),
        out_specs=(rows, rows, rows, rows),
        check_vma=False,
    )
```

```python
import jax
import jax.numpy as jnp
from jax import lax
from jax.experimental import pallas as pl
from jax.experimental.pallas import tpu as pltpu
from jax.sharding import PartitionSpec as P

HEADS = 4
GROUP = 7
D = 128
QUARTERS = 4
NY, NZ = 4, 8
SCALE = D ** (-0.5)
LOG2E = 1.4426950408889634
MESH = pl.DeviceIdType.MESH
BF16 = jnp.bfloat16
F32 = jnp.float32


def place():
    seq = lax.axis_index("seq")
    x = lax.axis_index("head")
    return x, seq // (2 * NZ), (seq // 2) % NZ, seq % 2


def device(x, y, z, core):
    return ((y * NZ + z) * 2 + core, x)


def remote(src, dst, send_sem, recv_sem, target):
    return pltpu.make_async_remote_copy(
        src_ref=src,
        dst_ref=dst,
        send_sem=send_sem,
        recv_sem=recv_sem,
        device_id=target,
        device_id_type=MESH,
    )


def partners(x, j):
    flip, mirror = x + 1 - 2 * (x % 2), 3 - x
    return (flip, mirror) if j % 2 == 0 else (mirror, flip)


def drain(view, sem):
    pltpu.make_async_copy(view, view, sem).wait()


def others(x):
    return (x + 1 - 2 * (x % 2), 3 - x, (x + 2) % 4)


def say_hello(x, y, z, core):
    sem = pltpu.get_barrier_semaphore()

    def signal(condition, targets):
        @pl.when(condition)
        def _():
            for target in targets:
                pl.semaphore_signal(sem, inc=1, device_id=target, device_id_type=MESH)

    first = core == 0
    signal((z == 0) & (y == 0) & first, [device(x, n, 0, c) for n in (2, 1, 3) for c in (0, 1)])
    signal(z == 0, [device(x, y, n, core) for n in (4, 3, 5, 2, 6, 1, 7)])
    signal((z == 0) & (y != 0), [device(x, 0, 0, 0)])
    signal(z != 0, [device(x, y, 0, core)])
    signal((z == 2) & first, [device(x, y, 3, 0), device(x, y, 4, 0)])
    signal((z == 6) & first, [device(x, y, 5, 0)])
    signal(((z == 3) | (z == 4)) & first, [device(x, y, 2, 0)])
    signal((z == 5) & first, [device(x, y, 6, 0)])
    signal(z >= 0, [device(n, y, z, core) for n in others(x)] + [device(x, y, z, 1 - core)])


def hear_all(x, y, z, core):
    sem = pltpu.get_barrier_semaphore()
    first = core == 0
    end = (z == 1) | (z == 7)
    for role, peers in (
        ((z == 0) & (y == 0) & first, 17),
        ((z == 0) & (y == 0) & ~first, 11),
        ((z == 0) & (y != 0), 12),
        ((z != 0) & (~first | end), 5),
        ((z == 2) & first, 7),
        ((z != 0) & (z != 2) & ~end & first, 6),
    ):
        @pl.when(role)
        def _():
            pl.semaphore_wait(sem, peers)


TILES = ((0, 256), (256, 256), (512, 256), (768, 128))
WIDE = GROUP * D
EXP_SCALE = SCALE * LOG2E


def nt(a, b):
    return lax.dot_general(a, b, (((1,), (1,)), ((), ())), preferred_element_type=F32)


def nn(a, b):
    return lax.dot_general(a, b, (((1,), (0,)), ((), ())), preferred_element_type=F32)


def fold_max(a):
    return jnp.max(a.reshape(D // 8, 8, a.shape[1]), axis=0)


def fold_sum(a):
    return jnp.sum(a.reshape(D // 8, 8, a.shape[1]), axis=0)


def main_kernel(
    mask_ref, k_ref, v_ref, q_hbm, c_hbm,
    att_hbm, dq_hbm, dk_ref, dv_ref,
    kv, q_s, c_s, att_s, dq_s, bias, po, dpo, mo, lo, fo, de, sp, dpp, pb, oo, ps, dss, vt,
    g, so1, ro1, so2, ro2, sc, rc, gs, sp1, rp1, part, sz, rz, sy, ry,
    lsem, qsem, osem, s_own, r_own, s_pr, r_pr, s_by, s_bz, r_t, s_c, r_c,
    ss, rs, s_a, r_a, s_y, r_y, s_z, r_z,
):
    x, y, z, core = place()
    opp = (x + 2) % 4
    seq = lax.axis_index("seq")
    top_row = (z == 0) & (y == 0)
    is_root = top_row & (core == 0)
    column = (core == 0) & (z == 0)
    leaf = (core == 0) & (z != 0)
    mesh_c0 = (core == 0) & ~top_row

    say_hello(x, y, z, core)

    def local(j, block, base):
        return [
            pltpu.make_async_copy(ref.at[:, pl.ds(j * D, D)], kv.at[j, block, t], lsem.at[base])
            for t, ref in enumerate((k_ref, v_ref))
        ]

    @pl.when(is_root)
    def _():
        for j in range(HEADS):
            for b in range(QUARTERS):
                for copy in local(j, b, 1):
                    copy.start()

    for j in range(HEADS):
        for copy in local(j, 4 + x, 0):
            copy.start()

    def take_out(buf, hbm, i, j):
        for h in range(GROUP):
            cols, rows = pl.ds((j * GROUP + h) * D, D), pl.ds(h * D, D)
            pltpu.make_async_copy(buf.at[j, rows], hbm.at[:, cols], osem.at[i]).start()

    hear_all(x, y, z, core)

    def y_send(j, n):
        blk = kv.at[j, x]
        return remote(blk, blk, s_by.at[0], r_t.at[j], device(x, n, 0, 0))

    def z_send(j, n):
        blk = kv.at[j, x]
        return remote(blk, blk, s_bz.at[0], r_t.at[j], device(x, y, n, 0))

    def pass_on(j):
        for n in (2, 6, 1, 7):
            z_send(j, n).start()

    def x_send(j, base, ss, rs, i):
        pa, pb = partners(x, j)
        blk = kv.at[j, base + (x, x, pa)[i]]
        return remote(blk, blk, ss.at[0], rs.at[j, (0, 1, 1)[i]], device((pa, pb, pb)[i], y, z, core))

    def p_send(j, i):
        blk = kv.at[j, x]
        return remote(blk, blk, s_pr.at[0], r_pr.at[j], device(others(x)[i], y, z, core))

    def core_send(j, i, base=0):
        n = x if i == 3 else others(x)[i]
        src, dst = kv.at[j, base + n], kv.at[j, n]
        return remote(src, dst, s_c.at[0], r_c.at[j], device(x, y, z, 1 - core))

    def spread(j):
        for i in (2, 0, 1):
            p_send(j, i).start()
        core_send(j, 3).start()

    @pl.when(is_root)
    def _():
        drain(kv.at[:, pl.ds(0, 4)], lsem.at[1])
        for j in range(HEADS):
            for n in (2, 1, 3):
                y_send(j, n).start()
            pass_on(j)
            core_send(j, 3).start()

    drain(kv.at[:, pl.ds(4, 1)], lsem.at[0])
    for j in range(HEADS):
        x_send(j, 4, s_own, r_own, 0).start()
        x_send(j, 4, s_own, r_own, 1).start()

    for j in range(HEADS):
        for h in range(GROUP):
            cols, rows = pl.ds((j * GROUP + h) * D, D), pl.ds(h * D, D)
            pltpu.make_async_copy(q_hbm.at[:, cols], q_s.at[j, rows], qsem.at[0]).start()
            pltpu.make_async_copy(c_hbm.at[:, cols], c_s.at[j, rows], qsem.at[1]).start()

    key = lax.broadcasted_iota(jnp.int32, (D, D), 0)
    query = lax.broadcasted_iota(jnp.int32, (D, D), 1)
    for b in range(QUARTERS):
        seen = key + b * D <= query + x * D
        tile = jnp.where(seen, 0.0, -1e30).astype(F32)
        bias[pl.ds(b * D, D), pl.ds(0, D)] = tile
        bias[pl.ds(b * D, D), pl.ds(D, D)] = tile
    levels = []
    for b in range(QUARTERS):
        reads = jnp.where(seq > 0, mask_ref[x, b], 0)
        levels.append(jnp.where(reads > 0, 0.0, -1e30).astype(F32))

    def relay(j):
        @pl.when(column & (y != 0))
        def _():
            y_send(j, y).wait_recv()
            pass_on(j)

        drain(kv.at[j, pl.ds(4, 1)], r_own.at[j, 0])
        x_send(j, 4, s_own, r_own, 2).start()

    relaying = leaf & ((z == 2) | (z == 6))
    quiet = leaf & (z != 2) & (z != 6)

    def forward(j):
        @pl.when(relaying)
        def _():
            z_send(j, z).wait_recv()

            @pl.when(z == 2)
            def _():
                z_send(j, 4).start()
                z_send(j, 3).start()

            @pl.when(z == 6)
            def _():
                z_send(j, 5).start()

    def prompt1(j):
        @pl.when(quiet)
        def _():
            z_send(j, z).wait_recv()

        @pl.when(mesh_c0)
        def _():
            spread(j)

    def prompt3(j):
        @pl.when(is_root)
        def _():
            for i in (0, 1, 2):
                core_send(j, i, 4).start()

        @pl.when(mesh_c0)
        def _():
            drain(kv.at[j, pl.ds(0, 3)], r_pr.at[j])
            for i in (0, 1, 2):
                core_send(j, i).start()

    def prompt_here(j):
        @pl.when(core == 1)
        def _():
            drain(kv.at[j, pl.ds(0, 4)], r_c.at[j])

    def own_part(j):
        drain(kv.at[j, pl.ds(4, 2)], r_own.at[j, 1])
        if j == 0:
            drain(q_s, qsem.at[0])
            drain(c_s, qsem.at[1])
        for b in range(QUARTERS):
            vt[:, pl.ds(b * D, D)] = kv[j, 4 + b, 1].T
        for at, width in TILES:
            cols, wide = pl.ds(at, width), pl.ds(0, width)
            keys = kv[j, 4:8, 0].reshape(4 * D, D)
            values = kv[j, 4:8, 1].reshape(4 * D, D)
            po[j, :, cols] = nt(keys, q_s[j, cols, :]) + bias[:, pl.ds(0, width)]
            top = None
            for b in range(QUARTERS):
                part_top = fold_max(po[j, pl.ds(b * D, D), cols])
                top = part_top if top is None else jnp.maximum(top, part_top)
            top = jnp.max(top, axis=0, keepdims=True)
            total = None
            for b in range(QUARTERS):
                p = jnp.exp2((po[j, pl.ds(b * D, D), cols] - top) * EXP_SCALE)
                po[j, pl.ds(b * D, D), cols] = p
                pb[pl.ds(b * D, D), wide] = p.astype(BF16)
                part_sum = fold_sum(p)
                total = part_sum if total is None else total + part_sum
            mo[j, :, cols] = top
            lo[j, :, cols] = jnp.sum(total, axis=0, keepdims=True)
            oo[j, :, cols] = nn(vt[:, pl.ds(0, 4 * D)], pb[:, wide])
            dpo[j, :, cols] = nt(values, c_s[j, cols, :])

    def flip_values(j):
        for b in range(QUARTERS):
            vt[:, pl.ds(b * D, D)] = kv[j, b, 1].T

    def prompt_part(j, at, width):
        cols, wide = pl.ds(at, width), pl.ds(0, width)
        c = c_s[j, cols, :]
        sp[:, wide] = nt(kv[j, 0:4, 0].reshape(4 * D, D), q_s[j, cols, :])
        dpp[:, wide] = nt(kv[j, 0:4, 1].reshape(4 * D, D), c)
        own_top = mo[j, :, cols]
        top = None
        for b in range(QUARTERS):
            part_top = fold_max(sp[pl.ds(b * D, D), wide]) + levels[b]
            top = part_top if top is None else jnp.maximum(top, part_top)
        top = jnp.maximum(own_top, jnp.max(top, axis=0, keepdims=True))
        shrink = jnp.exp2((own_top - top) * EXP_SCALE)
        total = None
        for b in range(QUARTERS):
            rows = pl.ds(b * D, D)
            p = jnp.exp2((sp[rows, wide] - (top - levels[b])) * EXP_SCALE)
            sp[rows, wide] = p
            part_sum = fold_sum(p)
            total = part_sum if total is None else total + part_sum
        total = jnp.sum(total, axis=0, keepdims=True) + lo[j, :, cols] * shrink
        inverse = 1.0 / total
        shrink = shrink * inverse
        fo[j, :, cols] = shrink
        for b in range(QUARTERS):
            rows = pl.ds(b * D, D)
            ps[j, rows, cols] = (sp[rows, wide] * inverse).astype(BF16)
        out_t = nn(vt[:, pl.ds(0, 4 * D)], ps[j, pl.ds(0, 4 * D), cols])
        out_t = (out_t + oo[j, :, cols] * shrink).astype(BF16)
        deltas = []
        for i in range(width // D):
            lanes, rows = slice(i * D, i * D + D), pl.ds(at + i * D, D)
            att_s[j, rows, :] = out_t[:, lanes].T
            prod = c_s[j, rows, :].T.astype(F32) * out_t[:, lanes].astype(F32)
            deltas.append(jnp.sum(prod, axis=0, keepdims=True))
        delta = jnp.concatenate(deltas, axis=1)
        de[j, :, cols] = delta
        for b in range(QUARTERS):
            rows = pl.ds(b * D, D)
            dss[j, rows, cols] = ((sp[rows, wide] * inverse) * (dpp[rows, wide] - delta)).astype(BF16)

    def own_terms(j):
        for at, width in TILES:
            cols = pl.ds(at, width)
            for b in range(QUARTERS):
                rows = pl.ds(b * D, D)
                p = po[j, rows, cols] * fo[j, :, cols]
                ps[j, pl.ds((4 + b) * D, D), cols] = p.astype(BF16)
                dss[j, pl.ds((4 + b) * D, D), cols] = (
                    p * (dpo[j, rows, cols] - de[j, :, cols])
                ).astype(BF16)
        key_terms(j, 4)

    def key_terms(j, first):
        rows = pl.ds(first * D, 4 * D)
        g[j, first : first + 4, 0] = (nn(dss[j, rows, :], q_s[j]) * SCALE).reshape(4, D, D)
        g[j, first : first + 4, 1] = nn(ps[j, rows, :], c_s[j]).reshape(4, D, D)

    def query_part(j):
        for b in range(2 * QUARTERS):
            vt[:, pl.ds(b * D, D)] = kv[j, b, 0].T
        for at, width in TILES:
            grad_t = (nn(vt[...], dss[j, :, pl.ds(at, width)]) * SCALE).astype(BF16)
            for i in range(width // D):
                dq_s[j, pl.ds(at + i * D, D), :] = grad_t[:, i * D : i * D + D].T
        take_out(dq_s, dq_hbm, 1, j)

    def hop(send, arrive, i, j, target):
        return remote(send.at[j], arrive.at[j], ss.at[i], rs.at[i, j], target)

    def own1(j):
        return hop(so1, ro1, 0, j, device(partners(x, j)[0], y, z, core))

    def own2(j):
        return hop(so2, ro2, 1, j, device(partners(x, j)[1], y, z, core))

    def pair(j):
        return hop(sc, rc, 2, j, device(x, y, z, 1 - core))

    def across(j, i):
        return remote(sp1.at[j, i], rp1.at[j, i], s_a.at[0], r_a.at[j], device(others(x)[i], y, z, core))

    def to_column(j, n):
        return remote(sz.at[j], rz.at[j, n - 1], s_z.at[0], r_z.at[j], device(x, y, 0, core))

    def to_root(j, t, n):
        return remote(sy.at[j], ry.at[j, 4 * t + n - 1], s_y.at[0], r_y.at[j], device(x, 0, 0, 0))

    def reduce0(j):
        for b in range(QUARTERS):
            sc[j, b] = g[j, b, 1 - core].astype(BF16)
        pair(j).start()

    def own_reduce1(j):
        pa, pb = partners(x, j)
        so1[j, 0] = g[j, 4 + pa].astype(BF16)
        so1[j, 1] = g[j, 4 + opp].astype(BF16)
        own1(j).start()

    def reduce1(j):
        pair(j).wait_recv()
        for b in range(QUARTERS):
            gs[j, b] = g[j, b, core] + rc[j, b].astype(F32)
        for i in (2, 0, 1):
            sp1[j, i] = gs[j, others(x)[i]].astype(BF16)
            across(j, i).start()

    def own_reduce2(j):
        pa, pb = partners(x, j)
        own1(j).wait_recv()
        so2[j] = (g[j, 4 + pb] + ro1[j, 1].astype(F32)).astype(BF16)
        own2(j).start()

    def reduce3(j):
        total = gs[j, x]
        drain(rp1.at[j], r_a.at[j])
        for i in range(3):
            total = total + rp1[j, i].astype(F32)
        part[j] = total
        sz[j] = total.astype(BF16)

        @pl.when(z != 0)
        def _():
            to_column(j, z).start()

    def reduce4(j):
        @pl.when(z == 0)
        def _():
            total = part[j]
            drain(rz.at[j], r_z.at[j])
            for n in range(1, NZ):
                total = total + rz[j, n - 1].astype(F32)
            part[j] = total
            sy[j] = total.astype(BF16)

            @pl.when((y != 0) | (core == 1))
            def _():
                to_root(j, core, y).start()

    def own_result(j):
        own2(j).wait_recv()
        cols = pl.ds(j * D, D)
        total = g[j, 4 + x] + ro1[j, 0].astype(F32) + ro2[j].astype(F32)
        g[j, 4 + x] = total
        dk_ref[:, cols] = total[0].astype(BF16)
        dv_ref[:, cols] = total[1].astype(BF16)

    def root_result(j):
        @pl.when(is_root)
        def _():
            cols = pl.ds(j * D, D)
            drain(ry.at[j], r_y.at[j])
            total = g[j, 4 + x, 0] + part[j]
            for n in range(1, NY):
                total = total + ry[j, n - 1].astype(F32)
            dk_ref[:, cols] = total.astype(BF16)
            total = g[j, 4 + x, 1]
            for n in range(NY):
                total = total + ry[j, 3 + n].astype(F32)
            dv_ref[:, cols] = total.astype(BF16)

    relay(0)
    relay(1)
    forward(0)
    relay(2)
    forward(1)
    relay(3)
    forward(2)
    own_part(0)
    prompt1(0)
    forward(3)
    own_part(1)
    prompt1(1)
    own_part(2)
    prompt1(2)
    prompt3(0)
    own_part(3)
    prompt1(3)
    between = {
        (0, 0): lambda: prompt3(1),
        (0, 2): lambda: prompt3(2),
        (1, 0): lambda: prompt3(3),
        (1, 2): lambda: reduce1(0),
        (2, 1): lambda: reduce1(1),
        (2, 3): lambda: reduce3(0),
        (3, 1): lambda: reduce1(2),
        (3, 3): lambda: reduce3(1),
    }
    for j in range(HEADS):
        prompt_here(j)
        flip_values(j)
        for i, (at, width) in enumerate(TILES):
            prompt_part(j, at, width)
            between.get((j, i), lambda: None)()
        key_terms(j, 0)
        reduce0(j)
        take_out(att_s, att_hbm, 0, j)
    own_terms(0)
    reduce1(3)
    own_reduce1(0)
    own_terms(1)
    own_reduce1(1)
    reduce3(2)
    own_terms(2)
    own_reduce1(2)
    reduce4(0)
    own_terms(3)
    reduce3(3)
    own_reduce1(3)
    own_reduce2(0)
    reduce4(1)
    query_part(0)
    own_reduce2(1)
    reduce4(2)
    query_part(1)
    own_reduce2(2)
    query_part(2)
    query_part(3)
    reduce4(3)
    own_reduce2(3)
    own_result(0)
    own_result(1)
    own_result(2)
    own_result(3)

    twelve = kv.at[pl.ds(0, 2), pl.ds(0, 6)]
    sixteen = kv.at[pl.ds(0, 2)]
    drain(twelve, s_own.at[0])

    @pl.when(core == 0)
    def _():
        drain(sixteen, s_c.at[0])

    @pl.when(mesh_c0)
    def _():
        drain(twelve, s_pr.at[0])

    @pl.when(column)
    def _():
        drain(sixteen, s_bz.at[0])

    @pl.when(leaf & (z == 2))
    def _():
        drain(kv.at[0], s_bz.at[0])

    @pl.when(leaf & (z == 6))
    def _():
        drain(kv.at[0, pl.ds(0, 4)], s_bz.at[0])

    @pl.when(is_root)
    def _():
        drain(twelve, s_by.at[0])

    drain(so1, ss.at[0])
    drain(so2, ss.at[1])
    drain(sc, ss.at[2])
    drain(sp1, s_a.at[0])

    @pl.when(z != 0)
    def _():
        drain(sz, s_z.at[0])

    @pl.when((z == 0) & ((y != 0) | (core == 1)))
    def _():
        drain(sy, s_y.at[0])

    drain(att_s, osem.at[0])
    drain(dq_s, osem.at[1])

    for j in range(HEADS):
        root_result(j)


def main(mask, k, v, q, c):
    dma, vmem = pltpu.SemaphoreType.DMA, pltpu.VMEM
    block = (D, D)
    wide = jax.ShapeDtypeStruct(q.shape, BF16)
    narrow = jax.ShapeDtypeStruct(k.shape, BF16)
    here = pl.BlockSpec(memory_space=pltpu.VMEM)
    there = pl.BlockSpec(memory_space=pl.ANY)
    return pl.pallas_call(
        main_kernel,
        out_shape=(wide, wide, narrow, narrow),
        in_specs=[pl.BlockSpec(memory_space=pltpu.SMEM), there, there, there, there],
        out_specs=(there, there, here, here),
        scratch_shapes=[
            vmem((HEADS, 8, 2) + block, BF16),
            vmem((HEADS, WIDE, D), BF16),
            vmem((HEADS, WIDE, D), BF16),
            vmem((HEADS, WIDE, D), BF16),
            vmem((HEADS, WIDE, D), BF16),
            vmem((4 * D, 2 * D), F32),
            vmem((HEADS, 4 * D, WIDE), F32),
            vmem((HEADS, 4 * D, WIDE), F32),
            vmem((HEADS, 1, WIDE), F32),
            vmem((HEADS, 1, WIDE), F32),
            vmem((HEADS, 1, WIDE), F32),
            vmem((HEADS, 1, WIDE), F32),
            vmem((4 * D, 2 * D), F32),
            vmem((4 * D, 2 * D), F32),
            vmem((4 * D, 2 * D), BF16),
            vmem((HEADS, D, WIDE), F32),
            vmem((HEADS, 8 * D, WIDE), BF16),
            vmem((HEADS, 8 * D, WIDE), BF16),
            vmem((D, 8 * D), BF16),
            vmem((HEADS, 8, 2) + block, F32),
            vmem((HEADS, 2, 2) + block, BF16),
            vmem((HEADS, 2, 2) + block, BF16),
            vmem((HEADS, 2) + block, BF16),
            vmem((HEADS, 2) + block, BF16),
            vmem((HEADS, 4) + block, BF16),
            vmem((HEADS, 4) + block, BF16),
            vmem((HEADS, 4) + block, F32),
            vmem((HEADS, 3) + block, BF16),
            vmem((HEADS, 3) + block, BF16),
            vmem((HEADS,) + block, F32),
            vmem((HEADS,) + block, BF16),
            vmem((HEADS, NZ - 1) + block, BF16),
            vmem((HEADS,) + block, BF16),
            vmem((HEADS, 2 * NY - 1) + block, BF16),
            dma((2,)),
            dma((2,)),
            dma((2,)),
            dma((1,)),
            dma((HEADS, 2)),
            dma((1,)),
            dma((HEADS,)),
            dma((1,)),
            dma((1,)),
            dma((HEADS,)),
            dma((1,)),
            dma((HEADS,)),
            dma((3,)),
            dma((3, HEADS)),
            dma((1,)),
            dma((HEADS,)),
            dma((1,)),
            dma((HEADS,)),
            dma((1,)),
            dma((HEADS,)),
        ],
        compiler_params=pltpu.CompilerParams(
            collective_id=0, has_side_effects=True, vmem_limit_bytes=60 * 2**20
        ),
        name="tree_attention",
    )(mask, k, v, q, c)


PIECES = 2


def hand_on_kernel(*refs):
    arrays, outs, held, (came, went) = refs[:4], refs[4:8], refs[8:12], refs[12:]

    def copies(i, p):
        rows = pl.ds(p * (D // PIECES), D // PIECES)
        inner = held[i].at[rows]
        return (
            pltpu.make_async_copy(arrays[i].at[rows], inner, came.at[i, p]),
            pltpu.make_async_copy(inner, outs[i].at[rows], went.at[i, p]),
        )

    order = [(i, p) for i in (2, 3, 0, 1) for p in range(PIECES)]
    for at in order:
        copies(*at)[0].start()
    for at in order:
        copies(*at)[0].wait()
        copies(*at)[1].start()
    for at in order:
        copies(*at)[1].wait()


def hand_on(arrays):
    there = pl.BlockSpec(memory_space=pl.ANY)
    return pl.pallas_call(
        hand_on_kernel,
        out_shape=[jax.ShapeDtypeStruct(a.shape, a.dtype) for a in arrays],
        in_specs=[there] * 4,
        out_specs=[there] * 4,
        scratch_shapes=[pltpu.VMEM(a.shape, a.dtype) for a in arrays]
        + [pltpu.SemaphoreType.DMA((4, PIECES))] * 2,
        name="hand_on",
    )(*arrays)


def on_device(queries, rotated_key_rows, value_matrix, cotangent, tree_mask):
    return tuple(hand_on(main(tree_mask, rotated_key_rows, value_matrix, queries, cotangent)))


def solution(mesh):
    rows = P(("seq", "head"), None)
    return jax.shard_map(
        on_device,
        mesh=mesh,
        in_specs=(rows, rows, rows, rows, P("seq", None)),
        out_specs=(rows, rows, rows, rows),
        check_vma=False,
    )
```

```python
import jax
import jax.numpy as jnp
from jax import lax
from jax.experimental import pallas as pl
from jax.experimental.pallas import tpu as pltpu
from jax.sharding import PartitionSpec as P

HEADS = 4
GROUP = 7
D = 128
QUARTERS = 4
NY, NZ = 4, 8
SCALE = D ** (-0.5)
LOG2E = 1.4426950408889634
MESH = pl.DeviceIdType.MESH
BF16 = jnp.bfloat16
F32 = jnp.float32


def place():
    seq = lax.axis_index("seq")
    x = lax.axis_index("head")
    return x, seq // (2 * NZ), (seq // 2) % NZ, seq % 2


def device(x, y, z, core):
    return ((y * NZ + z) * 2 + core, x)


def remote(src, dst, send_sem, recv_sem, target):
    return pltpu.make_async_remote_copy(
        src_ref=src,
        dst_ref=dst,
        send_sem=send_sem,
        recv_sem=recv_sem,
        device_id=target,
        device_id_type=MESH,
    )


def partners(x, j):
    flip, mirror = x + 1 - 2 * (x % 2), 3 - x
    return (flip, mirror) if j % 2 == 0 else (mirror, flip)


def drain(view, sem):
    pltpu.make_async_copy(view, view, sem).wait()


def others(x):
    return (x + 1 - 2 * (x % 2), 3 - x, (x + 2) % 4)


def say_hello(x, y, z, core):
    sem = pltpu.get_barrier_semaphore()

    def signal(condition, targets):
        @pl.when(condition)
        def _():
            for target in targets:
                pl.semaphore_signal(sem, inc=1, device_id=target, device_id_type=MESH)

    first = core == 0
    signal((z == 0) & (y == 0) & first, [device(x, n, 0, c) for n in (2, 1, 3) for c in (0, 1)])
    signal(z == 0, [device(x, y, n, core) for n in (4, 3, 5, 2, 6, 1, 7)])
    signal((z == 0) & (y != 0), [device(x, 0, 0, 0)])
    signal(z != 0, [device(x, y, 0, core)])
    signal((z == 2) & first, [device(x, y, 3, 0), device(x, y, 4, 0)])
    signal((z == 6) & first, [device(x, y, 5, 0)])
    signal(((z == 3) | (z == 4)) & first, [device(x, y, 2, 0)])
    signal((z == 5) & first, [device(x, y, 6, 0)])
    signal(z >= 0, [device(n, y, z, core) for n in others(x)] + [device(x, y, z, 1 - core)])


def hear_all(x, y, z, core):
    sem = pltpu.get_barrier_semaphore()
    first = core == 0
    end = (z == 1) | (z == 7)
    for role, peers in (
        ((z == 0) & (y == 0) & first, 17),
        ((z == 0) & (y == 0) & ~first, 11),
        ((z == 0) & (y != 0), 12),
        ((z != 0) & (~first | end), 5),
        ((z == 2) & first, 7),
        ((z != 0) & (z != 2) & ~end & first, 6),
    ):
        @pl.when(role)
        def _():
            pl.semaphore_wait(sem, peers)


TILES = ((0, 256), (256, 256), (512, 256), (768, 128))
WIDE = GROUP * D
EXP_SCALE = SCALE * LOG2E


def nt(a, b):
    return lax.dot_general(a, b, (((1,), (1,)), ((), ())), preferred_element_type=F32)


def nn(a, b):
    return lax.dot_general(a, b, (((1,), (0,)), ((), ())), preferred_element_type=F32)


def fold_max(a):
    return jnp.max(a.reshape(D // 8, 8, a.shape[1]), axis=0)


def fold_sum(a):
    return jnp.sum(a.reshape(D // 8, 8, a.shape[1]), axis=0)


def main_kernel(
    mask_ref, k_ref, v_ref, q_hbm, c_hbm,
    att_hbm, dq_hbm, dk_ref, dv_ref,
    kv, q_s, c_s, att_s, dq_s, bias, po, dpo, mo, lo, fo, de, sp, dpp, pb, oo, ps, dss, vt,
    g, so1, ro1, so2, ro2, sc, rc, gs, sp1, rp1, part, sz, rz, sy, ry,
    lsem, qsem, osem, s_own, r_own, s_pr, r_pr, s_by, s_bz, r_t, s_c, r_c,
    ss, rs, s_a, r_a, s_y, r_y, s_z, r_z,
):
    x, y, z, core = place()
    opp = (x + 2) % 4
    seq = lax.axis_index("seq")
    top_row = (z == 0) & (y == 0)
    is_root = top_row & (core == 0)
    column = (core == 0) & (z == 0)
    leaf = (core == 0) & (z != 0)
    mesh_c0 = (core == 0) & ~top_row

    say_hello(x, y, z, core)

    def local(j, block, base):
        return [
            pltpu.make_async_copy(ref.at[:, pl.ds(j * D, D)], kv.at[j, block, t], lsem.at[base])
            for t, ref in enumerate((k_ref, v_ref))
        ]

    @pl.when(is_root)
    def _():
        for j in range(HEADS):
            for b in range(QUARTERS):
                for copy in local(j, b, 1):
                    copy.start()

    for j in range(HEADS):
        for copy in local(j, 4 + x, 0):
            copy.start()

    def take_out(buf, hbm, i, j):
        for h in range(GROUP):
            cols, rows = pl.ds((j * GROUP + h) * D, D), pl.ds(h * D, D)
            pltpu.make_async_copy(buf.at[j, rows], hbm.at[:, cols], osem.at[i]).start()

    hear_all(x, y, z, core)

    def y_send(j, n):
        blk = kv.at[j, x]
        return remote(blk, blk, s_by.at[0], r_t.at[j], device(x, n, 0, 0))

    def z_send(j, n):
        blk = kv.at[j, x]
        return remote(blk, blk, s_bz.at[1 if j == 0 else 0], r_t.at[j], device(x, y, n, 0))

    def pass_on(j):
        for n in (4, 5, 3, 6, 2, 7, 1) if j == 0 else (2, 6, 1, 7):
            z_send(j, n).start()

    def x_send(j, base, ss, rs, i):
        pa, pb = partners(x, j)
        blk = kv.at[j, base + (x, x, pa)[i]]
        return remote(blk, blk, ss.at[0], rs.at[j, (0, 1, 1)[i]], device((pa, pb, pb)[i], y, z, core))

    def p_send(j, i):
        blk = kv.at[j, x]
        return remote(blk, blk, s_pr.at[0], r_pr.at[j, i], device(others(x)[i], y, z, core))

    def core_send(j, i, base=0):
        n = x if i == 3 else others(x)[i]
        src, dst = kv.at[j, base + n], kv.at[j, n]
        return remote(src, dst, s_c.at[0], r_c.at[j], device(x, y, z, 1 - core))

    def spread(j):
        for i in (2, 0, 1):
            p_send(j, i).start()
        core_send(j, 3).start()

    @pl.when(is_root)
    def _():
        drain(kv.at[:, pl.ds(0, 4)], lsem.at[1])
        for j in range(HEADS):
            for n in (2, 1, 3):
                y_send(j, n).start()
            pass_on(j)
            core_send(j, 3).start()

    drain(kv.at[:, pl.ds(4, 1)], lsem.at[0])
    for j in range(HEADS):
        x_send(j, 4, s_own, r_own, 0).start()
        x_send(j, 4, s_own, r_own, 1).start()

    for j in range(HEADS):
        for h in range(GROUP):
            cols, rows = pl.ds((j * GROUP + h) * D, D), pl.ds(h * D, D)
            pltpu.make_async_copy(q_hbm.at[:, cols], q_s.at[j, rows], qsem.at[0]).start()
            pltpu.make_async_copy(c_hbm.at[:, cols], c_s.at[j, rows], qsem.at[1]).start()

    key = lax.broadcasted_iota(jnp.int32, (D, D), 0)
    query = lax.broadcasted_iota(jnp.int32, (D, D), 1)
    for b in range(QUARTERS):
        seen = key + b * D <= query + x * D
        tile = jnp.where(seen, 0.0, -1e30).astype(F32)
        bias[pl.ds(b * D, D), pl.ds(0, D)] = tile
        bias[pl.ds(b * D, D), pl.ds(D, D)] = tile
    levels = []
    for b in range(QUARTERS):
        reads = jnp.where(seq > 0, mask_ref[x, b], 0)
        levels.append(jnp.where(reads > 0, 0.0, -1e30).astype(F32))

    def relay(j):
        @pl.when(column & (y != 0))
        def _():
            y_send(j, y).wait_recv()
            pass_on(j)

        drain(kv.at[j, pl.ds(4, 1)], r_own.at[j, 0])
        x_send(j, 4, s_own, r_own, 2).start()

    relaying = leaf & ((z == 2) | (z == 6))
    quiet = leaf & (z != 2) & (z != 6)

    def forward(j):
        @pl.when(relaying)
        def _():
            z_send(j, z).wait_recv()

            @pl.when(z == 2)
            def _():
                z_send(j, 4).start()
                z_send(j, 3).start()

            @pl.when(z == 6)
            def _():
                z_send(j, 5).start()

    far = (z > 2) & (z < 6)

    def prompt1(j, here=None):
        here = mesh_c0 if here is None else mesh_c0 & here

        @pl.when(here & (leaf if j == 0 else quiet))
        def _():
            z_send(j, z).wait_recv()

        @pl.when(here)
        def _():
            spread(j)

    def prompt3(j):
        @pl.when(is_root)
        def _():
            for i in (0, 1, 2):
                core_send(j, i, 4).start()

        @pl.when(mesh_c0)
        def _():
            for i in (0, 1, 2):
                drain(kv.at[j, pl.ds(0, 1)], r_pr.at[j, i])
                core_send(j, i).start()

    def prompt_here(j):
        @pl.when(core == 1)
        def _():
            drain(kv.at[j, pl.ds(0, 4)], r_c.at[j])

    def own_part(j):
        drain(kv.at[j, pl.ds(4, 2)], r_own.at[j, 1])
        if j == 0:
            drain(q_s, qsem.at[0])
            drain(c_s, qsem.at[1])
        for b in range(QUARTERS):
            vt[:, pl.ds(b * D, D)] = kv[j, 4 + b, 1].T
        for at, width in TILES:
            cols, wide = pl.ds(at, width), pl.ds(0, width)
            keys = kv[j, 4:8, 0].reshape(4 * D, D)
            values = kv[j, 4:8, 1].reshape(4 * D, D)
            po[j, :, cols] = nt(keys, q_s[j, cols, :]) + bias[:, pl.ds(0, width)]
            top = None
            for b in range(QUARTERS):
                part_top = fold_max(po[j, pl.ds(b * D, D), cols])
                top = part_top if top is None else jnp.maximum(top, part_top)
            top = jnp.max(top, axis=0, keepdims=True)
            total = None
            for b in range(QUARTERS):
                p = jnp.exp2((po[j, pl.ds(b * D, D), cols] - top) * EXP_SCALE)
                po[j, pl.ds(b * D, D), cols] = p
                pb[pl.ds(b * D, D), wide] = p.astype(BF16)
                part_sum = fold_sum(p)
                total = part_sum if total is None else total + part_sum
            mo[j, :, cols] = top
            lo[j, :, cols] = jnp.sum(total, axis=0, keepdims=True)
            oo[j, :, cols] = nn(vt[:, pl.ds(0, 4 * D)], pb[:, wide])
            dpo[j, :, cols] = nt(values, c_s[j, cols, :])

    def flip_values(j):
        for b in range(QUARTERS):
            vt[:, pl.ds(b * D, D)] = kv[j, b, 1].T

    def prompt_part(j, at, width):
        cols, wide = pl.ds(at, width), pl.ds(0, width)
        c = c_s[j, cols, :]
        sp[:, wide] = nt(kv[j, 0:4, 0].reshape(4 * D, D), q_s[j, cols, :])
        dpp[:, wide] = nt(kv[j, 0:4, 1].reshape(4 * D, D), c)
        own_top = mo[j, :, cols]
        top = None
        for b in range(QUARTERS):
            part_top = fold_max(sp[pl.ds(b * D, D), wide]) + levels[b]
            top = part_top if top is None else jnp.maximum(top, part_top)
        top = jnp.maximum(own_top, jnp.max(top, axis=0, keepdims=True))
        shrink = jnp.exp2((own_top - top) * EXP_SCALE)
        total = None
        for b in range(QUARTERS):
            rows = pl.ds(b * D, D)
            p = jnp.exp2((sp[rows, wide] - (top - levels[b])) * EXP_SCALE)
            sp[rows, wide] = p
            part_sum = fold_sum(p)
            total = part_sum if total is None else total + part_sum
        total = jnp.sum(total, axis=0, keepdims=True) + lo[j, :, cols] * shrink
        inverse = 1.0 / total
        shrink = shrink * inverse
        fo[j, :, cols] = shrink
        for b in range(QUARTERS):
            rows = pl.ds(b * D, D)
            ps[j, rows, cols] = (sp[rows, wide] * inverse).astype(BF16)
        out_t = nn(vt[:, pl.ds(0, 4 * D)], ps[j, pl.ds(0, 4 * D), cols])
        out_t = (out_t + oo[j, :, cols] * shrink).astype(BF16)
        deltas = []
        for i in range(width // D):
            lanes, rows = slice(i * D, i * D + D), pl.ds(at + i * D, D)
            att_s[j, rows, :] = out_t[:, lanes].T
            prod = c_s[j, rows, :].T.astype(F32) * out_t[:, lanes].astype(F32)
            deltas.append(jnp.sum(prod, axis=0, keepdims=True))
        delta = jnp.concatenate(deltas, axis=1)
        de[j, :, cols] = delta
        for b in range(QUARTERS):
            rows = pl.ds(b * D, D)
            dss[j, rows, cols] = ((sp[rows, wide] * inverse) * (dpp[rows, wide] - delta)).astype(BF16)

    def own_terms(j):
        for at, width in TILES:
            cols = pl.ds(at, width)
            for b in range(QUARTERS):
                rows = pl.ds(b * D, D)
                p = po[j, rows, cols] * fo[j, :, cols]
                ps[j, pl.ds((4 + b) * D, D), cols] = p.astype(BF16)
                dss[j, pl.ds((4 + b) * D, D), cols] = (
                    p * (dpo[j, rows, cols] - de[j, :, cols])
                ).astype(BF16)
        key_terms(j, 4)

    def key_terms(j, first):
        rows = pl.ds(first * D, 4 * D)
        g[j, first : first + 4, 0] = (nn(dss[j, rows, :], q_s[j]) * SCALE).reshape(4, D, D)
        g[j, first : first + 4, 1] = nn(ps[j, rows, :], c_s[j]).reshape(4, D, D)

    def query_part(j):
        for b in range(2 * QUARTERS):
            vt[:, pl.ds(b * D, D)] = kv[j, b, 0].T
        for at, width in TILES:
            grad_t = (nn(vt[...], dss[j, :, pl.ds(at, width)]) * SCALE).astype(BF16)
            for i in range(width // D):
                dq_s[j, pl.ds(at + i * D, D), :] = grad_t[:, i * D : i * D + D].T
        take_out(dq_s, dq_hbm, 1, j)

    def hop(send, arrive, i, j, target):
        return remote(send.at[j], arrive.at[j], ss.at[i], rs.at[i, j], target)

    def own1(j):
        return hop(so1, ro1, 0, j, device(partners(x, j)[0], y, z, core))

    def own2(j):
        return hop(so2, ro2, 1, j, device(partners(x, j)[1], y, z, core))

    def pair(j):
        return hop(sc, rc, 2, j, device(x, y, z, 1 - core))

    def across(j, i):
        return remote(sp1.at[j, i], rp1.at[j, i], s_a.at[0], r_a.at[j], device(others(x)[i], y, z, core))

    def to_column(j, n):
        return remote(sz.at[j], rz.at[j, n - 1], s_z.at[0], r_z.at[j], device(x, y, 0, core))

    def to_root(j, t, n):
        return remote(sy.at[j], ry.at[j, 4 * t + n - 1], s_y.at[0], r_y.at[j], device(x, 0, 0, 0))

    def reduce0(j):
        for b in range(QUARTERS):
            sc[j, b] = g[j, b, 1 - core].astype(BF16)
        pair(j).start()

    def own_reduce1(j):
        pa, pb = partners(x, j)
        so1[j, 0] = g[j, 4 + pa].astype(BF16)
        so1[j, 1] = g[j, 4 + opp].astype(BF16)
        own1(j).start()

    def reduce1(j):
        pair(j).wait_recv()
        for b in range(QUARTERS):
            gs[j, b] = g[j, b, core] + rc[j, b].astype(F32)
        for i in (2, 0, 1):
            sp1[j, i] = gs[j, others(x)[i]].astype(BF16)
            across(j, i).start()

    def own_reduce2(j):
        pa, pb = partners(x, j)
        own1(j).wait_recv()
        so2[j] = (g[j, 4 + pb] + ro1[j, 1].astype(F32)).astype(BF16)
        own2(j).start()

    def reduce3(j):
        total = gs[j, x]
        drain(rp1.at[j], r_a.at[j])
        for i in range(3):
            total = total + rp1[j, i].astype(F32)
        part[j] = total
        sz[j] = total.astype(BF16)

        @pl.when(z != 0)
        def _():
            to_column(j, z).start()

    def reduce4(j):
        @pl.when(z == 0)
        def _():
            total = part[j]
            drain(rz.at[j], r_z.at[j])
            for n in range(1, NZ):
                total = total + rz[j, n - 1].astype(F32)
            part[j] = total
            sy[j] = total.astype(BF16)

            @pl.when((y != 0) | (core == 1))
            def _():
                to_root(j, core, y).start()

    def own_result(j):
        own2(j).wait_recv()
        cols = pl.ds(j * D, D)
        total = g[j, 4 + x] + ro1[j, 0].astype(F32) + ro2[j].astype(F32)
        g[j, 4 + x] = total
        dk_ref[:, cols] = total[0].astype(BF16)
        dv_ref[:, cols] = total[1].astype(BF16)

    def root_result(j):
        @pl.when(is_root)
        def _():
            cols = pl.ds(j * D, D)
            drain(ry.at[j], r_y.at[j])
            total = g[j, 4 + x, 0] + part[j]
            for n in range(1, NY):
                total = total + ry[j, n - 1].astype(F32)
            dk_ref[:, cols] = total.astype(BF16)
            total = g[j, 4 + x, 1]
            for n in range(NY):
                total = total + ry[j, 3 + n].astype(F32)
            dv_ref[:, cols] = total.astype(BF16)

    relay(0)
    relay(1)
    relay(2)
    relay(3)
    prompt1(0, ~far)
    forward(1)
    own_part(0)
    prompt1(0, far)
    forward(2)
    own_part(1)
    forward(3)
    prompt1(1)
    own_part(2)
    prompt3(0)
    prompt1(2)
    own_part(3)
    prompt1(3)
    between = {
        (0, 0): lambda: prompt3(1),
        (0, 2): lambda: prompt3(2),
        (1, 0): lambda: prompt3(3),
        (1, 2): lambda: reduce1(0),
        (2, 1): lambda: reduce1(1),
        (2, 3): lambda: reduce3(0),
        (3, 1): lambda: reduce1(2),
        (3, 3): lambda: reduce3(1),
    }
    for j in range(HEADS):
        prompt_here(j)
        flip_values(j)
        for i, (at, width) in enumerate(TILES):
            prompt_part(j, at, width)
            between.get((j, i), lambda: None)()
        key_terms(j, 0)
        reduce0(j)
        take_out(att_s, att_hbm, 0, j)
    own_terms(0)
    reduce1(3)
    own_reduce1(0)
    own_terms(1)
    own_reduce1(1)
    reduce3(2)
    own_terms(2)
    own_reduce1(2)
    reduce4(0)
    own_terms(3)
    reduce3(3)
    own_reduce1(3)
    own_reduce2(0)
    reduce4(1)
    query_part(0)
    own_reduce2(1)
    reduce4(2)
    query_part(1)
    own_reduce2(2)
    reduce4(3)
    own_reduce2(3)
    query_part(2)
    query_part(3)
    own_result(0)
    own_result(1)
    own_result(2)
    own_result(3)

    twelve = kv.at[pl.ds(0, 2), pl.ds(0, 6)]
    sixteen = kv.at[pl.ds(0, 2)]
    drain(twelve, s_own.at[0])

    @pl.when(core == 0)
    def _():
        drain(sixteen, s_c.at[0])

    @pl.when(mesh_c0)
    def _():
        drain(twelve, s_pr.at[0])

    @pl.when(column)
    def _():
        drain(twelve, s_bz.at[0])
        drain(kv.at[0, pl.ds(0, 7)], s_bz.at[1])

    @pl.when(leaf & (z == 2))
    def _():
        drain(kv.at[0, pl.ds(0, 6)], s_bz.at[0])

    @pl.when(leaf & (z == 6))
    def _():
        drain(kv.at[0, pl.ds(0, 3)], s_bz.at[0])

    @pl.when(is_root)
    def _():
        drain(twelve, s_by.at[0])

    drain(so1, ss.at[0])
    drain(so2, ss.at[1])
    drain(sc, ss.at[2])
    drain(sp1, s_a.at[0])

    @pl.when(z != 0)
    def _():
        drain(sz, s_z.at[0])

    @pl.when((z == 0) & ((y != 0) | (core == 1)))
    def _():
        drain(sy, s_y.at[0])

    drain(att_s, osem.at[0])
    drain(dq_s, osem.at[1])

    for j in range(HEADS):
        root_result(j)


def main(mask, k, v, q, c):
    dma, vmem = pltpu.SemaphoreType.DMA, pltpu.VMEM
    block = (D, D)
    wide = jax.ShapeDtypeStruct(q.shape, BF16)
    narrow = jax.ShapeDtypeStruct(k.shape, BF16)
    here = pl.BlockSpec(memory_space=pltpu.VMEM)
    there = pl.BlockSpec(memory_space=pl.ANY)
    return pl.pallas_call(
        main_kernel,
        out_shape=(wide, wide, narrow, narrow),
        in_specs=[pl.BlockSpec(memory_space=pltpu.SMEM), there, there, there, there],
        out_specs=(there, there, here, here),
        scratch_shapes=[
            vmem((HEADS, 8, 2) + block, BF16),
            vmem((HEADS, WIDE, D), BF16),
            vmem((HEADS, WIDE, D), BF16),
            vmem((HEADS, WIDE, D), BF16),
            vmem((HEADS, WIDE, D), BF16),
            vmem((4 * D, 2 * D), F32),
            vmem((HEADS, 4 * D, WIDE), F32),
            vmem((HEADS, 4 * D, WIDE), F32),
            vmem((HEADS, 1, WIDE), F32),
            vmem((HEADS, 1, WIDE), F32),
            vmem((HEADS, 1, WIDE), F32),
            vmem((HEADS, 1, WIDE), F32),
            vmem((4 * D, 2 * D), F32),
            vmem((4 * D, 2 * D), F32),
            vmem((4 * D, 2 * D), BF16),
            vmem((HEADS, D, WIDE), F32),
            vmem((HEADS, 8 * D, WIDE), BF16),
            vmem((HEADS, 8 * D, WIDE), BF16),
            vmem((D, 8 * D), BF16),
            vmem((HEADS, 8, 2) + block, F32),
            vmem((HEADS, 2, 2) + block, BF16),
            vmem((HEADS, 2, 2) + block, BF16),
            vmem((HEADS, 2) + block, BF16),
            vmem((HEADS, 2) + block, BF16),
            vmem((HEADS, 4) + block, BF16),
            vmem((HEADS, 4) + block, BF16),
            vmem((HEADS, 4) + block, F32),
            vmem((HEADS, 3) + block, BF16),
            vmem((HEADS, 3) + block, BF16),
            vmem((HEADS,) + block, F32),
            vmem((HEADS,) + block, BF16),
            vmem((HEADS, NZ - 1) + block, BF16),
            vmem((HEADS,) + block, BF16),
            vmem((HEADS, 2 * NY - 1) + block, BF16),
            dma((2,)),
            dma((2,)),
            dma((2,)),
            dma((1,)),
            dma((HEADS, 2)),
            dma((1,)),
            dma((HEADS, 3)),
            dma((1,)),
            dma((2,)),
            dma((HEADS,)),
            dma((1,)),
            dma((HEADS,)),
            dma((3,)),
            dma((3, HEADS)),
            dma((1,)),
            dma((HEADS,)),
            dma((1,)),
            dma((HEADS,)),
            dma((1,)),
            dma((HEADS,)),
        ],
        compiler_params=pltpu.CompilerParams(
            collective_id=0, has_side_effects=True, vmem_limit_bytes=60 * 2**20
        ),
        name="tree_attention",
    )(mask, k, v, q, c)


PIECES = 2


def hand_on_kernel(*refs):
    arrays, outs, held, (came, went) = refs[:4], refs[4:8], refs[8:12], refs[12:]

    def copies(i, p):
        rows = pl.ds(p * (D // PIECES), D // PIECES)
        inner = held[i].at[rows]
        return (
            pltpu.make_async_copy(arrays[i].at[rows], inner, came.at[i, p]),
            pltpu.make_async_copy(inner, outs[i].at[rows], went.at[i, p]),
        )

    order = [(i, p) for i in (2, 3, 0, 1) for p in range(PIECES)]
    for at in order:
        copies(*at)[0].start()
    for at in order:
        copies(*at)[0].wait()
        copies(*at)[1].start()
    for at in order:
        copies(*at)[1].wait()


def hand_on(arrays):
    there = pl.BlockSpec(memory_space=pl.ANY)
    return pl.pallas_call(
        hand_on_kernel,
        out_shape=[jax.ShapeDtypeStruct(a.shape, a.dtype) for a in arrays],
        in_specs=[there] * 4,
        out_specs=[there] * 4,
        scratch_shapes=[pltpu.VMEM(a.shape, a.dtype) for a in arrays]
        + [pltpu.SemaphoreType.DMA((4, PIECES))] * 2,
        name="hand_on",
    )(*arrays)


def on_device(queries, rotated_key_rows, value_matrix, cotangent, tree_mask):
    return tuple(hand_on(main(tree_mask, rotated_key_rows, value_matrix, queries, cotangent)))


def solution(mesh):
    rows = P(("seq", "head"), None)
    return jax.shard_map(
        on_device,
        mesh=mesh,
        in_specs=(rows, rows, rows, rows, P("seq", None)),
        out_specs=(rows, rows, rows, rows),
        check_vma=False,
    )
```

```python
import jax
import jax.numpy as jnp
from jax import lax
from jax.experimental import pallas as pl
from jax.experimental.pallas import tpu as pltpu
from jax.sharding import PartitionSpec as P

HEADS = 4
GROUP = 7
D = 128
QUARTERS = 4
NY, NZ = 4, 8
SCALE = D ** (-0.5)
LOG2E = 1.4426950408889634
MESH = pl.DeviceIdType.MESH
BF16 = jnp.bfloat16
F32 = jnp.float32


def place():
    seq = lax.axis_index("seq")
    x = lax.axis_index("head")
    return x, seq // (2 * NZ), (seq // 2) % NZ, seq % 2


def device(x, y, z, core):
    return ((y * NZ + z) * 2 + core, x)


def remote(src, dst, send_sem, recv_sem, target):
    return pltpu.make_async_remote_copy(
        src_ref=src,
        dst_ref=dst,
        send_sem=send_sem,
        recv_sem=recv_sem,
        device_id=target,
        device_id_type=MESH,
    )


def partners(x, j):
    flip, mirror = x + 1 - 2 * (x % 2), 3 - x
    return (flip, mirror) if j % 2 == 0 else (mirror, flip)


def drain(view, sem):
    pltpu.make_async_copy(view, view, sem).wait()


def others(x):
    return (x + 1 - 2 * (x % 2), 3 - x, (x + 2) % 4)


def say_hello(x, y, z, core):
    sem = pltpu.get_barrier_semaphore()

    def signal(condition, targets):
        @pl.when(condition)
        def _():
            for target in targets:
                pl.semaphore_signal(sem, inc=1, device_id=target, device_id_type=MESH)

    first = core == 0
    signal((z == 0) & (y == 0) & first, [device(x, n, 0, c) for n in (2, 1, 3) for c in (0, 1)])
    signal(z == 0, [device(x, y, n, core) for n in (4, 3, 5, 2, 6, 1, 7)])
    signal((z == 0) & (y != 0), [device(x, 0, 0, 0)])
    signal(z != 0, [device(x, y, 0, core)])
    signal((z == 2) & first, [device(x, y, 3, 0), device(x, y, 4, 0)])
    signal((z == 6) & first, [device(x, y, 5, 0)])
    signal(((z == 3) | (z == 4)) & first, [device(x, y, 2, 0)])
    signal((z == 5) & first, [device(x, y, 6, 0)])
    signal(z >= 0, [device(n, y, z, core) for n in others(x)] + [device(x, y, z, 1 - core)])


def hear_all(x, y, z, core):
    sem = pltpu.get_barrier_semaphore()
    first = core == 0
    end = (z == 1) | (z == 7)
    for role, peers in (
        ((z == 0) & (y == 0) & first, 17),
        ((z == 0) & (y == 0) & ~first, 11),
        ((z == 0) & (y != 0), 12),
        ((z != 0) & (~first | end), 5),
        ((z == 2) & first, 7),
        ((z != 0) & (z != 2) & ~end & first, 6),
    ):
        @pl.when(role)
        def _():
            pl.semaphore_wait(sem, peers)


TILES = ((0, 256), (256, 256), (512, 256), (768, 128))
WIDE = GROUP * D
EXP_SCALE = SCALE * LOG2E


def nt(a, b):
    return lax.dot_general(a, b, (((1,), (1,)), ((), ())), preferred_element_type=F32)


def nn(a, b):
    return lax.dot_general(a, b, (((1,), (0,)), ((), ())), preferred_element_type=F32)


def fold_max(a):
    return jnp.max(a.reshape(D // 8, 8, a.shape[1]), axis=0)


def fold_sum(a):
    return jnp.sum(a.reshape(D // 8, 8, a.shape[1]), axis=0)


def main_kernel(
    mask_ref, k_ref, v_ref, q_hbm, c_hbm,
    att_hbm, dq_hbm, dk_ref, dv_ref,
    kv, q_s, c_s, att_s, dq_s, bias, po, mo, lo, fo, de, sp, dpp, pb, oo, ps, dss, vt,
    g, so1, ro1, so2, ro2, sc, rc, gs, sp1, rp1, part, sz, rz, sy, ry,
    lsem, qsem, osem, s_own, r_own, s_pr, r_pr, s_by, s_bz, r_t, s_c, r_c,
    ss, rs, s_a, r_a, s_y, r_y, s_z, r_z,
):
    x, y, z, core = place()
    opp = (x + 2) % 4
    seq = lax.axis_index("seq")
    top_row = (z == 0) & (y == 0)
    is_root = top_row & (core == 0)
    column = (core == 0) & (z == 0)
    leaf = (core == 0) & (z != 0)
    mesh_c0 = (core == 0) & ~top_row

    say_hello(x, y, z, core)

    def local(j, block, base):
        return [
            pltpu.make_async_copy(ref.at[:, pl.ds(j * D, D)], kv.at[j, block, t], lsem.at[base])
            for t, ref in enumerate((k_ref, v_ref))
        ]

    @pl.when(is_root)
    def _():
        for j in range(HEADS):
            for b in range(QUARTERS):
                for copy in local(j, b, 1):
                    copy.start()

    for j in range(HEADS):
        for copy in local(j, 4 + x, 0):
            copy.start()

    def take_out(buf, hbm, i, j):
        for h in range(GROUP):
            cols, rows = pl.ds((j * GROUP + h) * D, D), pl.ds(h * D, D)
            pltpu.make_async_copy(buf.at[j, rows], hbm.at[:, cols], osem.at[i]).start()

    hear_all(x, y, z, core)

    def y_send(j, n):
        blk = kv.at[j, x]
        return remote(blk, blk, s_by.at[0], r_t.at[j], device(x, n, 0, 0))

    def z_send(j, n):
        blk = kv.at[j, x]
        return remote(blk, blk, s_bz.at[1 if j == 0 else 0], r_t.at[j], device(x, y, n, 0))

    def pass_on(j):
        for n in (4, 5, 3, 6, 2, 7, 1) if j == 0 else (2, 6, 1, 7):
            z_send(j, n).start()

    def x_send(j, base, ss, rs, i):
        pa, pb = partners(x, j)
        blk = kv.at[j, base + (x, x, pa)[i]]
        return remote(blk, blk, ss.at[0], rs.at[j, (0, 1, 1)[i]], device((pa, pb, pb)[i], y, z, core))

    def p_send(j, i):
        blk = kv.at[j, x]
        return remote(blk, blk, s_pr.at[0], r_pr.at[j, i], device(others(x)[i], y, z, core))

    def core_send(j, i, base=0):
        n = x if i == 3 else others(x)[i]
        src, dst = kv.at[j, base + n], kv.at[j, n]
        return remote(src, dst, s_c.at[0], r_c.at[j], device(x, y, z, 1 - core))

    def spread(j):
        for i in (2, 0, 1):
            p_send(j, i).start()
        core_send(j, 3).start()

    @pl.when(is_root)
    def _():
        drain(kv.at[:, pl.ds(0, 4)], lsem.at[1])
        for j in range(HEADS):
            for n in (2, 1, 3):
                y_send(j, n).start()
            pass_on(j)
            core_send(j, 3).start()

    drain(kv.at[:, pl.ds(4, 1)], lsem.at[0])
    for j in range(HEADS):
        x_send(j, 4, s_own, r_own, 0).start()
        x_send(j, 4, s_own, r_own, 1).start()

    for j in range(HEADS):
        for h in range(GROUP):
            cols, rows = pl.ds((j * GROUP + h) * D, D), pl.ds(h * D, D)
            pltpu.make_async_copy(q_hbm.at[:, cols], q_s.at[j, rows], qsem.at[0]).start()
            pltpu.make_async_copy(c_hbm.at[:, cols], c_s.at[j, rows], qsem.at[1]).start()

    key = lax.broadcasted_iota(jnp.int32, (D, D), 0)
    query = lax.broadcasted_iota(jnp.int32, (D, D), 1)
    for b in range(QUARTERS):
        seen = key + b * D <= query + x * D
        tile = jnp.where(seen, 0.0, -1e30).astype(F32)
        bias[pl.ds(b * D, D), pl.ds(0, D)] = tile
        bias[pl.ds(b * D, D), pl.ds(D, D)] = tile
    levels = []
    for b in range(QUARTERS):
        reads = jnp.where(seq > 0, mask_ref[x, b], 0)
        levels.append(jnp.where(reads > 0, 0.0, -1e30).astype(F32))

    def relay(j):
        @pl.when(column & (y != 0))
        def _():
            y_send(j, y).wait_recv()
            pass_on(j)

        drain(kv.at[j, pl.ds(4, 1)], r_own.at[j, 0])
        x_send(j, 4, s_own, r_own, 2).start()

    relaying = leaf & ((z == 2) | (z == 6))
    quiet = leaf & (z != 2) & (z != 6)

    def forward(j):
        @pl.when(relaying)
        def _():
            z_send(j, z).wait_recv()

            @pl.when(z == 2)
            def _():
                z_send(j, 4).start()
                z_send(j, 3).start()

            @pl.when(z == 6)
            def _():
                z_send(j, 5).start()

    far = (z > 2) & (z < 6)

    def prompt1(j, here=None):
        here = mesh_c0 if here is None else mesh_c0 & here

        @pl.when(here & (leaf if j == 0 else quiet))
        def _():
            z_send(j, z).wait_recv()

        @pl.when(here)
        def _():
            spread(j)

    def prompt3(j):
        @pl.when(is_root)
        def _():
            for i in (0, 1, 2):
                core_send(j, i, 4).start()

        @pl.when(mesh_c0)
        def _():
            for i in (0, 1, 2):
                drain(kv.at[j, pl.ds(0, 1)], r_pr.at[j, i])
                core_send(j, i).start()

    def prompt_here(j):
        @pl.when(core == 1)
        def _():
            drain(kv.at[j, pl.ds(0, 4)], r_c.at[j])

    def own_part(j):
        drain(kv.at[j, pl.ds(4, 2)], r_own.at[j, 1])
        if j == 0:
            drain(q_s, qsem.at[0])
            drain(c_s, qsem.at[1])
        for b in range(QUARTERS):
            vt[:, pl.ds(b * D, D)] = kv[j, 4 + b, 1].T
        for at, width in TILES:
            cols, wide = pl.ds(at, width), pl.ds(0, width)
            keys = kv[j, 4:8, 0].reshape(4 * D, D)
            po[j, :, cols] = nt(keys, q_s[j, cols, :]) + bias[:, pl.ds(0, width)]
            top = None
            for b in range(QUARTERS):
                part_top = fold_max(po[j, pl.ds(b * D, D), cols])
                top = part_top if top is None else jnp.maximum(top, part_top)
            top = jnp.max(top, axis=0, keepdims=True)
            total = None
            for b in range(QUARTERS):
                p = jnp.exp2((po[j, pl.ds(b * D, D), cols] - top) * EXP_SCALE)
                po[j, pl.ds(b * D, D), cols] = p
                pb[pl.ds(b * D, D), wide] = p.astype(BF16)
                part_sum = fold_sum(p)
                total = part_sum if total is None else total + part_sum
            mo[j, :, cols] = top
            lo[j, :, cols] = jnp.sum(total, axis=0, keepdims=True)
            oo[j, :, cols] = nn(vt[:, pl.ds(0, 4 * D)], pb[:, wide])

    def flip_values(j):
        for b in range(QUARTERS):
            vt[:, pl.ds(b * D, D)] = kv[j, b, 1].T

    def prompt_part(j, at, width):
        cols, wide = pl.ds(at, width), pl.ds(0, width)
        c = c_s[j, cols, :]
        sp[:, wide] = nt(kv[j, 0:4, 0].reshape(4 * D, D), q_s[j, cols, :])
        dpp[:, wide] = nt(kv[j, 0:4, 1].reshape(4 * D, D), c)
        own_top = mo[j, :, cols]
        top = None
        for b in range(QUARTERS):
            part_top = fold_max(sp[pl.ds(b * D, D), wide]) + levels[b]
            top = part_top if top is None else jnp.maximum(top, part_top)
        top = jnp.maximum(own_top, jnp.max(top, axis=0, keepdims=True))
        shrink = jnp.exp2((own_top - top) * EXP_SCALE)
        total = None
        for b in range(QUARTERS):
            rows = pl.ds(b * D, D)
            p = jnp.exp2((sp[rows, wide] - (top - levels[b])) * EXP_SCALE)
            sp[rows, wide] = p
            part_sum = fold_sum(p)
            total = part_sum if total is None else total + part_sum
        total = jnp.sum(total, axis=0, keepdims=True) + lo[j, :, cols] * shrink
        inverse = 1.0 / total
        shrink = shrink * inverse
        fo[j, :, cols] = shrink
        for b in range(QUARTERS):
            rows = pl.ds(b * D, D)
            ps[j, rows, cols] = (sp[rows, wide] * inverse).astype(BF16)
        out_t = nn(vt[:, pl.ds(0, 4 * D)], ps[j, pl.ds(0, 4 * D), cols])
        out_t = (out_t + oo[j, :, cols] * shrink).astype(BF16)
        deltas = []
        for i in range(width // D):
            lanes, rows = slice(i * D, i * D + D), pl.ds(at + i * D, D)
            att_s[j, rows, :] = out_t[:, lanes].T
            prod = c_s[j, rows, :].T.astype(F32) * out_t[:, lanes].astype(F32)
            deltas.append(jnp.sum(prod, axis=0, keepdims=True))
        delta = jnp.concatenate(deltas, axis=1)
        de[j, :, cols] = delta
        for b in range(QUARTERS):
            rows = pl.ds(b * D, D)
            dss[j, rows, cols] = ((sp[rows, wide] * inverse) * (dpp[rows, wide] - delta)).astype(BF16)

    def own_terms(j):
        for at, width in TILES:
            cols, wide = pl.ds(at, width), pl.ds(0, width)
            dpp[:, wide] = nt(kv[j, 4:8, 1].reshape(4 * D, D), c_s[j, cols, :])
            for b in range(QUARTERS):
                rows = pl.ds(b * D, D)
                p = po[j, rows, cols] * fo[j, :, cols]
                ps[j, pl.ds((4 + b) * D, D), cols] = p.astype(BF16)
                dss[j, pl.ds((4 + b) * D, D), cols] = (
                    p * (dpp[rows, wide] - de[j, :, cols])
                ).astype(BF16)
        key_terms(j, 4)

    def key_terms(j, first):
        rows = pl.ds(first * D, 4 * D)
        g[j, first : first + 4, 0] = (nn(dss[j, rows, :], q_s[j]) * SCALE).reshape(4, D, D)
        g[j, first : first + 4, 1] = nn(ps[j, rows, :], c_s[j]).reshape(4, D, D)

    def query_part(j):
        for b in range(2 * QUARTERS):
            vt[:, pl.ds(b * D, D)] = kv[j, b, 0].T
        for at, width in TILES:
            grad_t = (nn(vt[...], dss[j, :, pl.ds(at, width)]) * SCALE).astype(BF16)
            for i in range(width // D):
                dq_s[j, pl.ds(at + i * D, D), :] = grad_t[:, i * D : i * D + D].T
        take_out(dq_s, dq_hbm, 1, j)

    def hop(send, arrive, i, j, target):
        return remote(send.at[j], arrive.at[j], ss.at[i], rs.at[i, j], target)

    def own1(j):
        return hop(so1, ro1, 0, j, device(partners(x, j)[0], y, z, core))

    def own2(j):
        return hop(so2, ro2, 1, j, device(partners(x, j)[1], y, z, core))

    def pair(j):
        return hop(sc, rc, 2, j, device(x, y, z, 1 - core))

    def across(j, i):
        return remote(sp1.at[j, i], rp1.at[j, i], s_a.at[0], r_a.at[j], device(others(x)[i], y, z, core))

    def to_column(j, n):
        return remote(sz.at[j], rz.at[j, n - 1], s_z.at[0], r_z.at[j], device(x, y, 0, core))

    def to_root(j, t, n):
        return remote(sy.at[j], ry.at[j, 4 * t + n - 1], s_y.at[0], r_y.at[j], device(x, 0, 0, 0))

    def reduce0(j):
        for b in range(QUARTERS):
            sc[j, b] = g[j, b, 1 - core].astype(BF16)
        pair(j).start()

    def own_reduce1(j):
        pa, pb = partners(x, j)
        so1[j, 0] = g[j, 4 + pa].astype(BF16)
        so1[j, 1] = g[j, 4 + opp].astype(BF16)
        own1(j).start()

    def reduce1(j):
        pair(j).wait_recv()
        for b in range(QUARTERS):
            gs[j, b] = g[j, b, core] + rc[j, b].astype(F32)
        for i in (2, 0, 1):
            sp1[j, i] = gs[j, others(x)[i]].astype(BF16)
            across(j, i).start()

    def own_reduce2(j):
        pa, pb = partners(x, j)
        own1(j).wait_recv()
        so2[j] = (g[j, 4 + pb] + ro1[j, 1].astype(F32)).astype(BF16)
        own2(j).start()

    def reduce3(j):
        total = gs[j, x]
        drain(rp1.at[j], r_a.at[j])
        for i in range(3):
            total = total + rp1[j, i].astype(F32)
        part[j] = total
        sz[j] = total.astype(BF16)

        @pl.when(z != 0)
        def _():
            to_column(j, z).start()

    def reduce4(j):
        @pl.when(z == 0)
        def _():
            total = part[j]
            drain(rz.at[j], r_z.at[j])
            for n in range(1, NZ):
                total = total + rz[j, n - 1].astype(F32)
            part[j] = total
            sy[j] = total.astype(BF16)

            @pl.when((y != 0) | (core == 1))
            def _():
                to_root(j, core, y).start()

    def own_result(j):
        own2(j).wait_recv()
        cols = pl.ds(j * D, D)
        total = g[j, 4 + x] + ro1[j, 0].astype(F32) + ro2[j].astype(F32)
        g[j, 4 + x] = total
        dk_ref[:, cols] = total[0].astype(BF16)
        dv_ref[:, cols] = total[1].astype(BF16)

    def root_result(j):
        @pl.when(is_root)
        def _():
            cols = pl.ds(j * D, D)
            drain(ry.at[j], r_y.at[j])
            total = g[j, 4 + x, 0] + part[j]
            for n in range(1, NY):
                total = total + ry[j, n - 1].astype(F32)
            dk_ref[:, cols] = total.astype(BF16)
            total = g[j, 4 + x, 1]
            for n in range(NY):
                total = total + ry[j, 3 + n].astype(F32)
            dv_ref[:, cols] = total.astype(BF16)

    relay(0)
    relay(1)
    relay(2)
    relay(3)
    prompt1(0, ~far)
    forward(1)
    own_part(0)
    prompt1(0, far)
    forward(2)
    own_part(1)
    forward(3)
    prompt1(1)
    own_part(2)
    prompt3(0)
    prompt1(2)
    own_part(3)
    prompt1(3)
    between = {
        (0, 0): lambda: prompt3(1),
        (0, 2): lambda: prompt3(2),
        (1, 0): lambda: prompt3(3),
        (1, 2): lambda: reduce1(0),
        (2, 1): lambda: reduce1(1),
        (2, 3): lambda: reduce3(0),
        (3, 1): lambda: reduce1(2),
        (3, 3): lambda: reduce3(1),
    }
    for j in range(HEADS):
        prompt_here(j)
        flip_values(j)
        for i, (at, width) in enumerate(TILES):
            prompt_part(j, at, width)
            between.get((j, i), lambda: None)()
        key_terms(j, 0)
        reduce0(j)
        take_out(att_s, att_hbm, 0, j)
    own_terms(0)
    reduce1(3)
    own_reduce1(0)
    own_terms(1)
    own_reduce1(1)
    reduce3(2)
    own_terms(2)
    own_reduce1(2)
    reduce4(0)
    own_terms(3)
    reduce3(3)
    own_reduce1(3)
    own_reduce2(0)
    reduce4(1)
    query_part(0)
    own_reduce2(1)
    reduce4(2)
    query_part(1)
    own_reduce2(2)
    reduce4(3)
    own_reduce2(3)
    query_part(2)
    query_part(3)
    own_result(0)
    own_result(1)
    own_result(2)
    own_result(3)

    twelve = kv.at[pl.ds(0, 2), pl.ds(0, 6)]
    sixteen = kv.at[pl.ds(0, 2)]
    drain(twelve, s_own.at[0])

    @pl.when(core == 0)
    def _():
        drain(sixteen, s_c.at[0])

    @pl.when(mesh_c0)
    def _():
        drain(twelve, s_pr.at[0])

    @pl.when(column)
    def _():
        drain(twelve, s_bz.at[0])
        drain(kv.at[0, pl.ds(0, 7)], s_bz.at[1])

    @pl.when(leaf & (z == 2))
    def _():
        drain(kv.at[0, pl.ds(0, 6)], s_bz.at[0])

    @pl.when(leaf & (z == 6))
    def _():
        drain(kv.at[0, pl.ds(0, 3)], s_bz.at[0])

    @pl.when(is_root)
    def _():
        drain(twelve, s_by.at[0])

    drain(so1, ss.at[0])
    drain(so2, ss.at[1])
    drain(sc, ss.at[2])
    drain(sp1, s_a.at[0])

    @pl.when(z != 0)
    def _():
        drain(sz, s_z.at[0])

    @pl.when((z == 0) & ((y != 0) | (core == 1)))
    def _():
        drain(sy, s_y.at[0])

    drain(att_s, osem.at[0])
    drain(dq_s, osem.at[1])

    for j in range(HEADS):
        root_result(j)


def main(mask, k, v, q, c):
    dma, vmem = pltpu.SemaphoreType.DMA, pltpu.VMEM
    block = (D, D)
    wide = jax.ShapeDtypeStruct(q.shape, BF16)
    narrow = jax.ShapeDtypeStruct(k.shape, BF16)
    here = pl.BlockSpec(memory_space=pltpu.VMEM)
    there = pl.BlockSpec(memory_space=pl.ANY)
    return pl.pallas_call(
        main_kernel,
        out_shape=(wide, wide, narrow, narrow),
        in_specs=[pl.BlockSpec(memory_space=pltpu.SMEM), there, there, there, there],
        out_specs=(there, there, here, here),
        scratch_shapes=[
            vmem((HEADS, 8, 2) + block, BF16),
            vmem((HEADS, WIDE, D), BF16),
            vmem((HEADS, WIDE, D), BF16),
            vmem((HEADS, WIDE, D), BF16),
            vmem((HEADS, WIDE, D), BF16),
            vmem((4 * D, 2 * D), F32),
            vmem((HEADS, 4 * D, WIDE), F32),
            vmem((HEADS, 1, WIDE), F32),
            vmem((HEADS, 1, WIDE), F32),
            vmem((HEADS, 1, WIDE), F32),
            vmem((HEADS, 1, WIDE), F32),
            vmem((4 * D, 2 * D), F32),
            vmem((4 * D, 2 * D), F32),
            vmem((4 * D, 2 * D), BF16),
            vmem((HEADS, D, WIDE), F32),
            vmem((HEADS, 8 * D, WIDE), BF16),
            vmem((HEADS, 8 * D, WIDE), BF16),
            vmem((D, 8 * D), BF16),
            vmem((HEADS, 8, 2) + block, F32),
            vmem((HEADS, 2, 2) + block, BF16),
            vmem((HEADS, 2, 2) + block, BF16),
            vmem((HEADS, 2) + block, BF16),
            vmem((HEADS, 2) + block, BF16),
            vmem((HEADS, 4) + block, BF16),
            vmem((HEADS, 4) + block, BF16),
            vmem((HEADS, 4) + block, F32),
            vmem((HEADS, 3) + block, BF16),
            vmem((HEADS, 3) + block, BF16),
            vmem((HEADS,) + block, F32),
            vmem((HEADS,) + block, BF16),
            vmem((HEADS, NZ - 1) + block, BF16),
            vmem((HEADS,) + block, BF16),
            vmem((HEADS, 2 * NY - 1) + block, BF16),
            dma((2,)),
            dma((2,)),
            dma((2,)),
            dma((1,)),
            dma((HEADS, 2)),
            dma((1,)),
            dma((HEADS, 3)),
            dma((1,)),
            dma((2,)),
            dma((HEADS,)),
            dma((1,)),
            dma((HEADS,)),
            dma((3,)),
            dma((3, HEADS)),
            dma((1,)),
            dma((HEADS,)),
            dma((1,)),
            dma((HEADS,)),
            dma((1,)),
            dma((HEADS,)),
        ],
        compiler_params=pltpu.CompilerParams(
            collective_id=0, has_side_effects=True, vmem_limit_bytes=60 * 2**20
        ),
        name="tree_attention",
    )(mask, k, v, q, c)


PIECES = 2


def hand_on_kernel(*refs):
    arrays, outs, held, (came, went) = refs[:4], refs[4:8], refs[8:12], refs[12:]

    def copies(i, p):
        rows = pl.ds(p * (D // PIECES), D // PIECES)
        inner = held[i].at[rows]
        return (
            pltpu.make_async_copy(arrays[i].at[rows], inner, came.at[i, p]),
            pltpu.make_async_copy(inner, outs[i].at[rows], went.at[i, p]),
        )

    order = [(i, p) for i in (2, 3, 0, 1) for p in range(PIECES)]
    for at in order:
        copies(*at)[0].start()
    for at in order:
        copies(*at)[0].wait()
        copies(*at)[1].start()
    for at in order:
        copies(*at)[1].wait()


def hand_on(arrays):
    there = pl.BlockSpec(memory_space=pl.ANY)
    return pl.pallas_call(
        hand_on_kernel,
        out_shape=[jax.ShapeDtypeStruct(a.shape, a.dtype) for a in arrays],
        in_specs=[there] * 4,
        out_specs=[there] * 4,
        scratch_shapes=[pltpu.VMEM(a.shape, a.dtype) for a in arrays]
        + [pltpu.SemaphoreType.DMA((4, PIECES))] * 2,
        name="hand_on",
    )(*arrays)


def on_device(queries, rotated_key_rows, value_matrix, cotangent, tree_mask):
    return tuple(hand_on(main(tree_mask, rotated_key_rows, value_matrix, queries, cotangent)))


def solution(mesh):
    rows = P(("seq", "head"), None)
    return jax.shard_map(
        on_device,
        mesh=mesh,
        in_specs=(rows, rows, rows, rows, P("seq", None)),
        out_specs=(rows, rows, rows, rows),
        check_vma=False,
    )
```

```python
import jax
import jax.numpy as jnp
from jax import lax
from jax.experimental import pallas as pl
from jax.experimental.pallas import tpu as pltpu
from jax.sharding import PartitionSpec as P

HEADS = 4
GROUP = 7
D = 128
QUARTERS = 4
NY, NZ = 4, 8
SCALE = D ** (-0.5)
LOG2E = 1.4426950408889634
MESH = pl.DeviceIdType.MESH
BF16 = jnp.bfloat16
F32 = jnp.float32


def place():
    seq = lax.axis_index("seq")
    x = lax.axis_index("head")
    return x, seq // (2 * NZ), (seq // 2) % NZ, seq % 2


def device(x, y, z, core):
    return ((y * NZ + z) * 2 + core, x)


def remote(src, dst, send_sem, recv_sem, target):
    return pltpu.make_async_remote_copy(
        src_ref=src,
        dst_ref=dst,
        send_sem=send_sem,
        recv_sem=recv_sem,
        device_id=target,
        device_id_type=MESH,
    )


def partners(x, j):
    flip, mirror = x + 1 - 2 * (x % 2), 3 - x
    return (flip, mirror) if j % 2 == 0 else (mirror, flip)


def drain(view, sem):
    pltpu.make_async_copy(view, view, sem).wait()


def others(x):
    return (x + 1 - 2 * (x % 2), 3 - x, (x + 2) % 4)


def say_hello(x, y, z, core):
    sem = pltpu.get_barrier_semaphore()

    def signal(condition, targets):
        @pl.when(condition)
        def _():
            for target in targets:
                pl.semaphore_signal(sem, inc=1, device_id=target, device_id_type=MESH)

    first = core == 0
    signal((z == 0) & (y == 0) & first, [device(x, n, 0, c) for n in (2, 1, 3) for c in (0, 1)])
    signal(z == 0, [device(x, y, n, core) for n in (4, 3, 5, 2, 6, 1, 7)])
    signal((z == 0) & (y != 0), [device(x, 0, 0, 0)])
    signal(z != 0, [device(x, y, 0, core)])
    signal((z == 2) & first, [device(x, y, 3, 0), device(x, y, 4, 0)])
    signal((z == 6) & first, [device(x, y, 5, 0)])
    signal(((z == 3) | (z == 4)) & first, [device(x, y, 2, 0)])
    signal((z == 5) & first, [device(x, y, 6, 0)])
    signal(z >= 0, [device(n, y, z, core) for n in others(x)] + [device(x, y, z, 1 - core)])


def hear_all(x, y, z, core):
    sem = pltpu.get_barrier_semaphore()
    first = core == 0
    end = (z == 1) | (z == 7)
    for role, peers in (
        ((z == 0) & (y == 0) & first, 17),
        ((z == 0) & (y == 0) & ~first, 11),
        ((z == 0) & (y != 0), 12),
        ((z != 0) & (~first | end), 5),
        ((z == 2) & first, 7),
        ((z != 0) & (z != 2) & ~end & first, 6),
    ):
        @pl.when(role)
        def _():
            pl.semaphore_wait(sem, peers)


TILES = ((0, 256), (256, 256), (512, 256), (768, 128))
WIDE = GROUP * D
EXP_SCALE = SCALE * LOG2E


def nt(a, b):
    return lax.dot_general(a, b, (((1,), (1,)), ((), ())), preferred_element_type=F32)


def nn(a, b):
    return lax.dot_general(a, b, (((1,), (0,)), ((), ())), preferred_element_type=F32)


def fold_max(a):
    return jnp.max(a.reshape(D // 8, 8, a.shape[1]), axis=0)


def fold_sum(a):
    return jnp.sum(a.reshape(D // 8, 8, a.shape[1]), axis=0)


def main_kernel(
    mask_ref, k_ref, v_ref, q_hbm, c_hbm,
    att_hbm, dq_hbm, dk_ref, dv_ref,
    kv, q_s, c_s, att_s, dq_s, bias, po, dpo, mo, lo, fo, de, sp, dpp, pb, oo, ps, dss, vt,
    g, so1, ro1, so2, ro2, sc, rc, gs, sp1, rp1, part, sz, rz, sy, ry,
    lsem, qsem, osem, s_own, r_own, s_pr, r_pr, s_by, s_bz, r_t, s_c, r_c,
    ss, rs, s_a, r_a, s_y, r_y, s_z, r_z,
):
    x, y, z, core = place()
    opp = (x + 2) % 4
    seq = lax.axis_index("seq")
    top_row = (z == 0) & (y == 0)
    is_root = top_row & (core == 0)
    column = (core == 0) & (z == 0)
    leaf = (core == 0) & (z != 0)
    mesh_c0 = (core == 0) & ~top_row

    say_hello(x, y, z, core)

    def local(j, block, base):
        return [
            pltpu.make_async_copy(ref.at[:, pl.ds(j * D, D)], kv.at[j, block, t], lsem.at[base])
            for t, ref in enumerate((k_ref, v_ref))
        ]

    @pl.when(is_root)
    def _():
        for j in range(HEADS):
            for b in range(QUARTERS):
                for copy in local(j, b, 1):
                    copy.start()

    for j in range(HEADS):
        for copy in local(j, 4 + x, 0):
            copy.start()

    def take_out(buf, hbm, i, j):
        for h in range(GROUP):
            cols, rows = pl.ds((j * GROUP + h) * D, D), pl.ds(h * D, D)
            pltpu.make_async_copy(buf.at[j, rows], hbm.at[:, cols], osem.at[i]).start()

    hear_all(x, y, z, core)

    def y_send(j, n):
        blk = kv.at[j, x]
        return remote(blk, blk, s_by.at[0], r_t.at[j], device(x, n, 0, 0))

    def z_send(j, n):
        blk = kv.at[j, x]
        return remote(blk, blk, s_bz.at[1 if j == 0 else 0], r_t.at[j], device(x, y, n, 0))

    def pass_on(j):
        for n in (4, 5, 3, 6, 2, 7, 1) if j == 0 else (2, 6, 1, 7):
            z_send(j, n).start()

    def x_send(j, base, ss, rs, i):
        pa, pb = partners(x, j)
        blk = kv.at[j, base + (x, x, pa)[i]]
        return remote(blk, blk, ss.at[0], rs.at[j, (0, 1, 1)[i]], device((pa, pb, pb)[i], y, z, core))

    def p_send(j, i):
        blk = kv.at[j, x]
        return remote(blk, blk, s_pr.at[0], r_pr.at[j, i], device(others(x)[i], y, z, core))

    def core_send(j, i, base=0):
        n = x if i == 3 else others(x)[i]
        src, dst = kv.at[j, base + n], kv.at[j, n]
        return remote(src, dst, s_c.at[0], r_c.at[j], device(x, y, z, 1 - core))

    def spread(j):
        for i in (2, 0, 1):
            p_send(j, i).start()
        core_send(j, 3).start()

    @pl.when(is_root)
    def _():
        drain(kv.at[:, pl.ds(0, 4)], lsem.at[1])
        for j in range(HEADS):
            for n in (2, 1, 3):
                y_send(j, n).start()
            pass_on(j)
            core_send(j, 3).start()

    drain(kv.at[:, pl.ds(4, 1)], lsem.at[0])
    for j in range(HEADS):
        x_send(j, 4, s_own, r_own, 0).start()
        x_send(j, 4, s_own, r_own, 1).start()

    for j in range(HEADS):
        for h in range(GROUP):
            cols, rows = pl.ds((j * GROUP + h) * D, D), pl.ds(h * D, D)
            pltpu.make_async_copy(q_hbm.at[:, cols], q_s.at[j, rows], qsem.at[0]).start()
            pltpu.make_async_copy(c_hbm.at[:, cols], c_s.at[j, rows], qsem.at[1]).start()

    key = lax.broadcasted_iota(jnp.int32, (D, D), 0)
    query = lax.broadcasted_iota(jnp.int32, (D, D), 1)
    for b in range(QUARTERS):
        seen = key + b * D <= query + x * D
        tile = jnp.where(seen, 0.0, -1e30).astype(F32)
        bias[pl.ds(b * D, D), pl.ds(0, D)] = tile
        bias[pl.ds(b * D, D), pl.ds(D, D)] = tile
    levels = []
    for b in range(QUARTERS):
        reads = jnp.where(seq > 0, mask_ref[x, b], 0)
        levels.append(jnp.where(reads > 0, 0.0, -1e30).astype(F32))

    def relay(j):
        @pl.when(column & (y != 0))
        def _():
            y_send(j, y).wait_recv()
            pass_on(j)

        drain(kv.at[j, pl.ds(4, 1)], r_own.at[j, 0])
        x_send(j, 4, s_own, r_own, 2).start()

    relaying = leaf & ((z == 2) | (z == 6))
    quiet = leaf & (z != 2) & (z != 6)

    def forward(j):
        @pl.when(relaying)
        def _():
            z_send(j, z).wait_recv()

            @pl.when(z == 2)
            def _():
                z_send(j, 4).start()
                z_send(j, 3).start()

            @pl.when(z == 6)
            def _():
                z_send(j, 5).start()

    far = (z > 2) & (z < 6)

    def prompt1(j, here=None):
        here = mesh_c0 if here is None else mesh_c0 & here

        @pl.when(here & (leaf if j == 0 else quiet))
        def _():
            z_send(j, z).wait_recv()

        @pl.when(here)
        def _():
            spread(j)

    def prompt3(j):
        @pl.when(is_root)
        def _():
            for i in (0, 1, 2):
                core_send(j, i, 4).start()

        @pl.when(mesh_c0)
        def _():
            for i in (0, 1, 2):
                drain(kv.at[j, pl.ds(0, 1)], r_pr.at[j, i])
                core_send(j, i).start()

    def prompt_here(j):
        @pl.when(core == 1)
        def _():
            drain(kv.at[j, pl.ds(0, 4)], r_c.at[j])

    def own_part(j):
        drain(kv.at[j, pl.ds(4, 2)], r_own.at[j, 1])
        if j == 0:
            drain(q_s, qsem.at[0])
            drain(c_s, qsem.at[1])
        for b in range(QUARTERS):
            vt[:, pl.ds(b * D, D)] = kv[j, 4 + b, 1].T
        for at, width in TILES:
            cols, wide = pl.ds(at, width), pl.ds(0, width)
            keys = kv[j, 4:8, 0].reshape(4 * D, D)
            values = kv[j, 4:8, 1].reshape(4 * D, D)
            po[j, :, cols] = nt(keys, q_s[j, cols, :]) + bias[:, pl.ds(0, width)]
            top = None
            for b in range(QUARTERS):
                part_top = fold_max(po[j, pl.ds(b * D, D), cols])
                top = part_top if top is None else jnp.maximum(top, part_top)
            top = jnp.max(top, axis=0, keepdims=True)
            total = None
            for b in range(QUARTERS):
                p = jnp.exp2((po[j, pl.ds(b * D, D), cols] - top) * EXP_SCALE)
                po[j, pl.ds(b * D, D), cols] = p
                pb[pl.ds(b * D, D), wide] = p.astype(BF16)
                part_sum = fold_sum(p)
                total = part_sum if total is None else total + part_sum
            mo[j, :, cols] = top
            lo[j, :, cols] = jnp.sum(total, axis=0, keepdims=True)
            oo[j, :, cols] = nn(vt[:, pl.ds(0, 4 * D)], pb[:, wide])
            dpo[j, :, cols] = nt(values, c_s[j, cols, :])

    def flip_values(j):
        for b in range(QUARTERS):
            vt[:, pl.ds(b * D, D)] = kv[j, b, 1].T

    def prompt_part(j, at, width):
        cols, wide = pl.ds(at, width), pl.ds(0, width)
        c = c_s[j, cols, :]
        sp[:, wide] = nt(kv[j, 0:4, 0].reshape(4 * D, D), q_s[j, cols, :])
        dpp[:, wide] = nt(kv[j, 0:4, 1].reshape(4 * D, D), c)
        own_top = mo[j, :, cols]
        top = None
        for b in range(QUARTERS):
            part_top = fold_max(sp[pl.ds(b * D, D), wide]) + levels[b]
            top = part_top if top is None else jnp.maximum(top, part_top)
        top = jnp.maximum(own_top, jnp.max(top, axis=0, keepdims=True))
        shrink = jnp.exp2((own_top - top) * EXP_SCALE)
        total = None
        for b in range(QUARTERS):
            rows = pl.ds(b * D, D)
            p = jnp.exp2((sp[rows, wide] - (top - levels[b])) * EXP_SCALE)
            sp[rows, wide] = p
            part_sum = fold_sum(p)
            total = part_sum if total is None else total + part_sum
        total = jnp.sum(total, axis=0, keepdims=True) + lo[j, :, cols] * shrink
        inverse = 1.0 / total
        shrink = shrink * inverse
        fo[j, :, cols] = shrink
        for b in range(QUARTERS):
            rows = pl.ds(b * D, D)
            ps[j, rows, cols] = (sp[rows, wide] * inverse).astype(BF16)
        out_t = nn(vt[:, pl.ds(0, 4 * D)], ps[j, pl.ds(0, 4 * D), cols])
        out_t = (out_t + oo[j, :, cols] * shrink).astype(BF16)
        deltas = []
        for i in range(width // D):
            lanes, rows = slice(i * D, i * D + D), pl.ds(at + i * D, D)
            att_s[j, rows, :] = out_t[:, lanes].T
            prod = c_s[j, rows, :].T.astype(F32) * out_t[:, lanes].astype(F32)
            deltas.append(jnp.sum(prod, axis=0, keepdims=True))
        delta = jnp.concatenate(deltas, axis=1)
        de[j, :, cols] = delta
        for b in range(QUARTERS):
            rows = pl.ds(b * D, D)
            dss[j, rows, cols] = ((sp[rows, wide] * inverse) * (dpp[rows, wide] - delta)).astype(BF16)

    def own_terms(j):
        for at, width in TILES:
            cols = pl.ds(at, width)
            for b in range(QUARTERS):
                rows = pl.ds(b * D, D)
                p = po[j, rows, cols] * fo[j, :, cols]
                ps[j, pl.ds((4 + b) * D, D), cols] = p.astype(BF16)
                dss[j, pl.ds((4 + b) * D, D), cols] = (
                    p * (dpo[j, rows, cols] - de[j, :, cols])
                ).astype(BF16)
        key_terms(j, 4)

    def key_terms(j, first):
        rows = pl.ds(first * D, 4 * D)
        g[j, first : first + 4, 0] = (nn(dss[j, rows, :], q_s[j]) * SCALE).reshape(4, D, D)
        g[j, first : first + 4, 1] = nn(ps[j, rows, :], c_s[j]).reshape(4, D, D)

    def query_part(j):
        for b in range(2 * QUARTERS):
            vt[:, pl.ds(b * D, D)] = kv[j, b, 0].T
        for at, width in TILES:
            grad_t = (nn(vt[...], dss[j, :, pl.ds(at, width)]) * SCALE).astype(BF16)
            for i in range(width // D):
                dq_s[j, pl.ds(at + i * D, D), :] = grad_t[:, i * D : i * D + D].T
        take_out(dq_s, dq_hbm, 1, j)

    def hop(send, arrive, i, j, target):
        return remote(send.at[j], arrive.at[j], ss.at[i], rs.at[i, j], target)

    def own1(j):
        return hop(so1, ro1, 0, j, device(partners(x, j)[0], y, z, core))

    def own2(j):
        return hop(so2, ro2, 1, j, device(partners(x, j)[1], y, z, core))

    def pair(j):
        return hop(sc, rc, 2, j, device(x, y, z, 1 - core))

    def across(j, i):
        return remote(sp1.at[j, i], rp1.at[j, i], s_a.at[0], r_a.at[j], device(others(x)[i], y, z, core))

    def to_column(j, n):
        return remote(sz.at[j], rz.at[j, n - 1], s_z.at[0], r_z.at[j], device(x, y, 0, core))

    def to_root(j, t, n):
        return remote(sy.at[j], ry.at[j, 4 * t + n - 1], s_y.at[0], r_y.at[j], device(x, 0, 0, 0))

    def reduce0(j):
        for b in range(QUARTERS):
            sc[j, b] = g[j, b, 1 - core].astype(BF16)
        pair(j).start()

    def own_reduce1(j):
        pa, pb = partners(x, j)
        so1[j, 0] = g[j, 4 + pa].astype(BF16)
        so1[j, 1] = g[j, 4 + opp].astype(BF16)
        own1(j).start()

    def reduce1(j):
        pair(j).wait_recv()
        for b in range(QUARTERS):
            gs[j, b] = g[j, b, core] + rc[j, b].astype(F32)
        for i in (2, 0, 1):
            sp1[j, i] = gs[j, others(x)[i]].astype(BF16)
            across(j, i).start()

    def own_reduce2(j):
        pa, pb = partners(x, j)
        own1(j).wait_recv()
        so2[j] = (g[j, 4 + pb] + ro1[j, 1].astype(F32)).astype(BF16)
        own2(j).start()

    def reduce3(j):
        total = gs[j, x]
        drain(rp1.at[j], r_a.at[j])
        for i in range(3):
            total = total + rp1[j, i].astype(F32)
        part[j] = total
        sz[j] = total.astype(BF16)

        @pl.when(z != 0)
        def _():
            to_column(j, z).start()

    def reduce4(j):
        @pl.when(z == 0)
        def _():
            total = part[j]
            drain(rz.at[j], r_z.at[j])
            for n in range(1, NZ):
                total = total + rz[j, n - 1].astype(F32)
            part[j] = total
            sy[j] = total.astype(BF16)

            @pl.when((y != 0) | (core == 1))
            def _():
                to_root(j, core, y).start()

    def own_result(j):
        own2(j).wait_recv()
        cols = pl.ds(j * D, D)
        total = g[j, 4 + x] + ro1[j, 0].astype(F32) + ro2[j].astype(F32)
        g[j, 4 + x] = total
        dk_ref[:, cols] = total[0].astype(BF16)
        dv_ref[:, cols] = total[1].astype(BF16)

    def root_result(j):
        @pl.when(is_root)
        def _():
            cols = pl.ds(j * D, D)
            drain(ry.at[j], r_y.at[j])
            total = g[j, 4 + x, 0] + part[j]
            for n in range(1, NY):
                total = total + ry[j, n - 1].astype(F32)
            dk_ref[:, cols] = total.astype(BF16)
            total = g[j, 4 + x, 1]
            for n in range(NY):
                total = total + ry[j, 3 + n].astype(F32)
            dv_ref[:, cols] = total.astype(BF16)

    relay(0)
    relay(1)
    relay(2)
    relay(3)
    prompt1(0, ~far)
    forward(1)
    own_part(0)
    prompt1(0, far)
    forward(2)
    own_part(1)
    forward(3)
    prompt1(1)
    own_part(2)
    prompt3(0)
    prompt1(2)
    own_part(3)
    prompt1(3)
    between = {
        (0, 0): lambda: prompt3(1),
        (0, 2): lambda: prompt3(2),
        (1, 0): lambda: prompt3(3),
        (1, 2): lambda: reduce1(0),
        (2, 1): lambda: reduce1(1),
        (2, 3): lambda: reduce3(0),
        (3, 1): lambda: reduce1(2),
        (3, 3): lambda: reduce3(1),
    }
    for j in range(HEADS):
        prompt_here(j)
        flip_values(j)
        for i, (at, width) in enumerate(TILES):
            prompt_part(j, at, width)
            between.get((j, i), lambda: None)()
        key_terms(j, 0)
        reduce0(j)
        take_out(att_s, att_hbm, 0, j)
    own_terms(0)
    reduce1(3)
    own_reduce1(0)
    own_terms(1)
    own_reduce1(1)
    reduce3(2)
    own_terms(2)
    own_reduce1(2)
    reduce4(0)
    own_terms(3)
    reduce3(3)
    own_reduce1(3)
    query_part(0)
    query_part(1)
    query_part(2)
    query_part(3)
    own_reduce2(0)
    reduce4(1)
    own_reduce2(1)
    reduce4(2)
    own_reduce2(2)
    reduce4(3)
    own_reduce2(3)
    own_result(0)
    own_result(1)
    own_result(2)
    own_result(3)

    twelve = kv.at[pl.ds(0, 2), pl.ds(0, 6)]
    sixteen = kv.at[pl.ds(0, 2)]
    drain(twelve, s_own.at[0])

    @pl.when(core == 0)
    def _():
        drain(sixteen, s_c.at[0])

    @pl.when(mesh_c0)
    def _():
        drain(twelve, s_pr.at[0])

    @pl.when(column)
    def _():
        drain(twelve, s_bz.at[0])
        drain(kv.at[0, pl.ds(0, 7)], s_bz.at[1])

    @pl.when(leaf & (z == 2))
    def _():
        drain(kv.at[0, pl.ds(0, 6)], s_bz.at[0])

    @pl.when(leaf & (z == 6))
    def _():
        drain(kv.at[0, pl.ds(0, 3)], s_bz.at[0])

    @pl.when(is_root)
    def _():
        drain(twelve, s_by.at[0])

    drain(so1, ss.at[0])
    drain(so2, ss.at[1])
    drain(sc, ss.at[2])
    drain(sp1, s_a.at[0])

    @pl.when(z != 0)
    def _():
        drain(sz, s_z.at[0])

    @pl.when((z == 0) & ((y != 0) | (core == 1)))
    def _():
        drain(sy, s_y.at[0])

    drain(att_s, osem.at[0])
    drain(dq_s, osem.at[1])

    for j in range(HEADS):
        root_result(j)


def main(mask, k, v, q, c):
    dma, vmem = pltpu.SemaphoreType.DMA, pltpu.VMEM
    block = (D, D)
    wide = jax.ShapeDtypeStruct(q.shape, BF16)
    narrow = jax.ShapeDtypeStruct(k.shape, BF16)
    here = pl.BlockSpec(memory_space=pltpu.VMEM)
    there = pl.BlockSpec(memory_space=pl.ANY)
    return pl.pallas_call(
        main_kernel,
        out_shape=(wide, wide, narrow, narrow),
        in_specs=[pl.BlockSpec(memory_space=pltpu.SMEM), there, there, there, there],
        out_specs=(there, there, here, here),
        scratch_shapes=[
            vmem((HEADS, 8, 2) + block, BF16),
            vmem((HEADS, WIDE, D), BF16),
            vmem((HEADS, WIDE, D), BF16),
            vmem((HEADS, WIDE, D), BF16),
            vmem((HEADS, WIDE, D), BF16),
            vmem((4 * D, 2 * D), F32),
            vmem((HEADS, 4 * D, WIDE), F32),
            vmem((HEADS, 4 * D, WIDE), F32),
            vmem((HEADS, 1, WIDE), F32),
            vmem((HEADS, 1, WIDE), F32),
            vmem((HEADS, 1, WIDE), F32),
            vmem((HEADS, 1, WIDE), F32),
            vmem((4 * D, 2 * D), F32),
            vmem((4 * D, 2 * D), F32),
            vmem((4 * D, 2 * D), BF16),
            vmem((HEADS, D, WIDE), F32),
            vmem((HEADS, 8 * D, WIDE), BF16),
            vmem((HEADS, 8 * D, WIDE), BF16),
            vmem((D, 8 * D), BF16),
            vmem((HEADS, 8, 2) + block, F32),
            vmem((HEADS, 2, 2) + block, BF16),
            vmem((HEADS, 2, 2) + block, BF16),
            vmem((HEADS, 2) + block, BF16),
            vmem((HEADS, 2) + block, BF16),
            vmem((HEADS, 4) + block, BF16),
            vmem((HEADS, 4) + block, BF16),
            vmem((HEADS, 4) + block, F32),
            vmem((HEADS, 3) + block, BF16),
            vmem((HEADS, 3) + block, BF16),
            vmem((HEADS,) + block, F32),
            vmem((HEADS,) + block, BF16),
            vmem((HEADS, NZ - 1) + block, BF16),
            vmem((HEADS,) + block, BF16),
            vmem((HEADS, 2 * NY - 1) + block, BF16),
            dma((2,)),
            dma((2,)),
            dma((2,)),
            dma((1,)),
            dma((HEADS, 2)),
            dma((1,)),
            dma((HEADS, 3)),
            dma((1,)),
            dma((2,)),
            dma((HEADS,)),
            dma((1,)),
            dma((HEADS,)),
            dma((3,)),
            dma((3, HEADS)),
            dma((1,)),
            dma((HEADS,)),
            dma((1,)),
            dma((HEADS,)),
            dma((1,)),
            dma((HEADS,)),
        ],
        compiler_params=pltpu.CompilerParams(
            collective_id=0, has_side_effects=True, vmem_limit_bytes=60 * 2**20
        ),
        name="tree_attention",
    )(mask, k, v, q, c)


PIECES = 2


def hand_on_kernel(*refs):
    arrays, outs, held, (came, went) = refs[:4], refs[4:8], refs[8:12], refs[12:]

    def copies(i, p):
        rows = pl.ds(p * (D // PIECES), D // PIECES)
        inner = held[i].at[rows]
        return (
            pltpu.make_async_copy(arrays[i].at[rows], inner, came.at[i, p]),
            pltpu.make_async_copy(inner, outs[i].at[rows], went.at[i, p]),
        )

    order = [(i, p) for i in (2, 3, 0, 1) for p in range(PIECES)]
    for at in order:
        copies(*at)[0].start()
    for at in order:
        copies(*at)[0].wait()
        copies(*at)[1].start()
    for at in order:
        copies(*at)[1].wait()


def hand_on(arrays):
    there = pl.BlockSpec(memory_space=pl.ANY)
    return pl.pallas_call(
        hand_on_kernel,
        out_shape=[jax.ShapeDtypeStruct(a.shape, a.dtype) for a in arrays],
        in_specs=[there] * 4,
        out_specs=[there] * 4,
        scratch_shapes=[pltpu.VMEM(a.shape, a.dtype) for a in arrays]
        + [pltpu.SemaphoreType.DMA((4, PIECES))] * 2,
        name="hand_on",
    )(*arrays)


def on_device(queries, rotated_key_rows, value_matrix, cotangent, tree_mask):
    return tuple(hand_on(main(tree_mask, rotated_key_rows, value_matrix, queries, cotangent)))


def solution(mesh):
    rows = P(("seq", "head"), None)
    return jax.shard_map(
        on_device,
        mesh=mesh,
        in_specs=(rows, rows, rows, rows, P("seq", None)),
        out_specs=(rows, rows, rows, rows),
        check_vma=False,
    )
```
